32 devices in a mesh: rays: 8 (over z, x), views: 4 (over y, core).
Axes of the slice: x: 2, y: 2, z: 4, core: 2. Of those that a mesh axis runs over, the one named last changes fastest.
Arguments:
- master: float32 [11384], P('rays')
- first_moment: float32 [11384], P('rays'), may hold values from -0.75 to 0.75
- second_moment: float32 [11384], P('rays'), may hold values from 0.001 to 0.01
- step_count: int32 [1], replicated, may hold values from 2 to 20
- feature_maps: bfloat16 [12, 35, 12032], P('views'), may hold values from -6 to 6
- pixel_index: int32 [24576, 12], P('rays', 'views'), may hold values from 0 to 12031
- visible: int32 [24576, 12], P('rays', 'views'), may hold values from 0 to 1, as said below
- deltas: float32 [128, 192], P('rays'), may hold values from 0.002 to 0.02
- targets: float32 [128, 3], P('rays'), may hold values from -3 to 3
- scene_id: int32 [128], P('rays'), may hold values from 0 to 7
- scene_weight: int32 [8], replicated, may hold values from 1 to 4
Outputs:
- loss: float32 [], replicated
- master_new: float32 [11384], P('rays')
- first_new: float32 [11384], P('rays')
- second_new: float32 [11384], P('rays')
The draws below stay inside these ranges and needn't reach their ends.
Inputs may be any that keep to these rules, and one draw needn't show every extreme that they name: Every sample is visible in at least one of the first 10 view slots; the last two slots are never visible.
All inputs are finite; a program needn't handle non-finite values.
Results may differ from the reference program's by a relative error of at most 0.00077.
Values may be sent and summed in bfloat16 or wider, within the bound.
No kernel may reach another device: no remote copies, remote signals or barrier semaphores. Data moves between devices by JAX's collectives and lax.ppermute only.
A program may use at most 128 MiB of HBM per device.

```python
import math
import jax
import jax.numpy as jnp
import numpy as np
from jax import lax

SAMPLES = 192
PIX = 12032
SCENES = 8
RAYS = 128
POINTS = 24576
VIEWS = 12
PARAMS_PAD = 11384


SECTION_SCALES = ((2240, 35 ** (-0.5)), (64, 0.2), (2048, 64 ** (-0.5)), (32, 0.2), (2048, 64 ** (-0.5)), (32, 0.2), (512, 3.0 * 32 ** (-0.5)), (16, 0.3), (1024, 0.5), (1024, 0.5), (1024, 0.25), (1024, 0.25), (256, 0.25), (16, 0.2), (16, 0.25), (1, 0.2))


def draw_master(key, part):
    pieces = [np.full((amount,), scale_value, np.float32) for amount, scale_value in SECTION_SCALES]
    table = np.concatenate(pieces)
    padded = np.concatenate([table, np.full((PARAMS_PAD - table.shape[0],), 0.1, np.float32)])
    return jax.random.normal(key, (PARAMS_PAD,), jnp.float32) * jnp.asarray(padded)


def draw_visible(key, part):
    first_key, second_key = jax.random.split(jax.random.fold_in(key, 11))
    dice_roll = jax.random.randint(first_key, (POINTS, VIEWS), 0, 10)
    forced = jax.random.randint(second_key, (POINTS, 1), 0, VIEWS - 2)
    view_slot = jnp.arange(VIEWS)[None, :]
    drawn_mask = ((dice_roll < 7) | (view_slot == forced)) & (view_slot < VIEWS - 2)
    return drawn_mask.astype(jnp.int32)


def touch_ends(values, stream_key, low, largest):
    spot = [jax.random.randint(jax.random.fold_in(stream_key, axis), (), 0, length) for axis, length in enumerate(values.shape)]
    widest = values.shape.index(max(values.shape))
    next_to = spot[:widest] + [(spot[widest] + 1) % values.shape[widest]] + spot[widest + 1:]
    return values.at[tuple(spot)].set(low).at[tuple(next_to)].set(largest)


def block_scale(stream_key, shape, cuts, least, high):
    factor_of, own = 1.0, jax.random.fold_in(stream_key, 6)
    for position, shards_of in cuts:
        steps = jnp.exp(jax.random.uniform(jax.random.fold_in(own, position), (shards_of,), jnp.float32, least / len(cuts), high / len(cuts)))
        factor_of = factor_of * jnp.repeat(steps, shape[position] // shards_of).reshape([-1 if axis == position else 1 for axis in range(len(shape))])
    return factor_of


def normal_values(own_key, extent, deviation, limit, cuts=(), held_as=jnp.bfloat16):
    array = jax.random.normal(own_key, extent, jnp.float32) * deviation
    if len(cuts) > 0:
        array = block_scale(own_key, extent, cuts, -0.22, 0.18) * array
    return jnp.clip(array, min=-limit, max=limit).astype(held_as)


def setup_inputs(seed: int = 0) -> dict:
    key_list = jax.random.split(jax.random.key(seed), 12)
    master = draw_master(jax.random.fold_in(key_list[11], 71), 0)
    first_moment = normal_values(key_list[1], (PARAMS_PAD,), 0.05, 0.75, ((0, 8),), jnp.float32)
    second_moment = jnp.clip(jnp.exp(math.log(0.01) - 2.30258502 * jax.random.uniform(key_list[2], (PARAMS_PAD,), jnp.float32) ** block_scale(key_list[2], (PARAMS_PAD,), ((0, 8),), -0.2, 0.2)), 0.001, 0.01)
    step_count = jax.random.randint(key_list[3], (1,), 2, 21).astype(jnp.int32)
    feature_maps = normal_values(key_list[4], (VIEWS, 35, PIX), 1.0, 6.0, ((0, 4),))
    pixel_index = touch_ends(jax.random.randint(key_list[5], (POINTS, VIEWS), 0, PIX), jax.random.fold_in(key_list[5], 1), 0, PIX - 1).astype(jnp.int32)
    visible = draw_visible(jax.random.fold_in(key_list[11], 71), 0)
    deltas = jnp.clip(jnp.exp(math.log(0.02) - 2.30258502 * jax.random.uniform(key_list[7], (RAYS, SAMPLES), jnp.float32) ** block_scale(key_list[7], (RAYS, SAMPLES), ((0, 8),), -0.2, 0.2)), 0.002, 0.02)
    targets = normal_values(key_list[8], (RAYS, 3), 0.5, 3.0, ((0, 8),), jnp.float32)
    scene_id = touch_ends(jax.random.randint(key_list[9], (RAYS,), 0, SCENES), jax.random.fold_in(key_list[9], 1), 0, SCENES - 1).astype(jnp.int32)
    scene_weight = touch_ends(jax.random.randint(key_list[10], (SCENES,), 1, 5), jax.random.fold_in(key_list[10], 1), 1, 4).astype(jnp.int32)
    return {"master": master, "first_moment": first_moment, "second_moment": second_moment, "step_count": step_count, "feature_maps": feature_maps, "pixel_index": pixel_index, "visible": visible, "deltas": deltas, "targets": targets, "scene_id": scene_id, "scene_weight": scene_weight}


@jax.custom_vjp
def low(v):
    return lax.optimization_barrier(v.astype(jnp.bfloat16)).astype(jnp.float32)

@jax.custom_vjp
def low_back(v):
    return v

def low_keep(v):
    return (low(v), None)

def low_pass(kept, grad):
    return (grad,)

def back_keep(v):
    return (v, None)

def back_low(kept, grad):
    return (low(grad),)
low.defvjp(low_keep, low_pass)
low_back.defvjp(back_keep, back_low)
LAYOUT = (('w1', (35, 64)), ('b1', (64,)), ('w2', (64, 32)), ('b2', (32,)), ('u1', (64, 32)), ('c1', (32,)), ('u2', (32, 16)), ('c2', (16,)), ('wq', (16, 64)), ('wk', (16, 64)), ('wv', (16, 64)), ('wo', (64, 16)), ('s1', (16, 16)), ('d1', (16,)), ('s2', (16, 1)), ('d2', (1,)))
MOMENT_DECAY = 0.5
SQUARE_DECAY = 0.5
LEARNING_RATE = 0.05
WEIGHT_DECAY = 0.01
EPSILON = 1e-08

def matmul_high(left_op, right_op):
    return jnp.matmul(left_op, right_op, precision=lax.Precision.HIGHEST)

def unpack(flat_params):
    params = {}
    offset = 0
    for section, section_dims in LAYOUT:
        amount = math.prod(section_dims)
        params[section] = flat_params[offset:offset + amount].reshape(section_dims)
        offset = offset + amount
    return params

def views_part(params, features_in, visible_f):
    hidden = low(jax.nn.elu(matmul_high(features_in, params['w1']) + params['b1']))
    feature = jax.nn.elu(matmul_high(hidden, params['w2']) + params['b2'])
    weighted = visible_f[..., None] * feature
    return (feature, lax.optimization_barrier(jnp.sum(weighted, axis=1)), lax.optimization_barrier(jnp.sum(weighted * feature, axis=1)))

def moments(total_sum, total_square, seen_count):
    average = total_sum / seen_count[:, None]
    return (average, total_square / seen_count[:, None] - average * average)

def blend_part(params, feature, average, variance, features_in, visible_f):
    spread_cols = jnp.broadcast_to(variance[:, None, :], feature.shape)
    joined = low(jnp.concatenate([feature - average[:, None, :], spread_cols], axis=-1))
    inner_act = low(jax.nn.elu(matmul_high(joined, params['u1']) + params['c1']))
    logits = matmul_high(inner_act, params['u2']) + params['c2']
    exponent = visible_f[..., None] * jnp.exp(logits)
    numerator = lax.optimization_barrier(jnp.sum(exponent * feature[..., :16], axis=1))
    denominator = lax.optimization_barrier(jnp.sum(exponent, axis=1))
    colour_sum = lax.optimization_barrier(jnp.sum(exponent[..., :1] * features_in[..., 32:], axis=1))
    return (numerator, denominator, colour_sum)

def ray_part(params, numerator, denominator, colour_sum, deltas, targets, ray_weight):
    ray_count, samples = deltas.shape
    tokens = numerator / denominator
    colour = (colour_sum / denominator[:, :1]).reshape(ray_count, samples, 3)
    token_low = low(tokens)
    queries = low(matmul_high(token_low, params['wq'])).reshape(ray_count, samples, 4, 16)
    key_rows = low(matmul_high(token_low, params['wk'])).reshape(ray_count, samples, 4, 16)
    val_rows = low(matmul_high(token_low, params['wv'])).reshape(ray_count, samples, 4, 16)
    scores = jnp.einsum('rqhd,rkhd->rhqk', queries, key_rows, precision=lax.Precision.HIGHEST) * 0.25
    attention = low(jax.nn.softmax(scores, axis=-1))
    attended = jnp.einsum('rhqk,rkhd->rqhd', attention, val_rows, precision=lax.Precision.HIGHEST)
    attended = low(attended.reshape(ray_count * samples, 64))
    mixed_rows = tokens + matmul_high(attended, params['wo'])
    inner_act = low(jax.nn.elu(matmul_high(low(mixed_rows), params['s1']) + params['d1']))
    density = jax.nn.softplus(matmul_high(inner_act, params['s2'])[:, 0] + params['d2'][0])
    optical = density.reshape(ray_count, samples) * deltas
    before = jnp.cumsum(optical, axis=1) - optical
    render_weight = jnp.exp(-before) * (1.0 - jnp.exp(-optical))
    pixel_colour = lax.optimization_barrier(jnp.sum(render_weight[..., None] * colour, axis=1))
    return jnp.sum(ray_weight * lax.optimization_barrier(jnp.sum((pixel_colour - targets) ** 2, axis=-1)))

def adamw(master, first_moment, second_moment, gradient, step_count):
    step_float = step_count[0].astype(jnp.float32)
    first_new = MOMENT_DECAY * first_moment + (1.0 - MOMENT_DECAY) * gradient
    second_new = SQUARE_DECAY * second_moment + (1.0 - SQUARE_DECAY) * gradient * gradient
    first_fix = 1.0 - jnp.power(MOMENT_DECAY, step_float)
    second_fix = 1.0 - jnp.power(SQUARE_DECAY, step_float)
    update = first_new / first_fix / (jnp.sqrt(second_new / second_fix) + EPSILON)
    master_new = master - LEARNING_RATE * (update + WEIGHT_DECAY * master)
    return (master_new, first_new, second_new)

def reference(master, first_moment, second_moment, step_count, feature_maps, pixel_index, visible, deltas, targets, scene_id, scene_weight):
    weights_f = lax.optimization_barrier(master.astype(jnp.bfloat16)).astype(jnp.float32)
    view_slot = jnp.arange(feature_maps.shape[0])[None, :]
    features_in = feature_maps[view_slot, :, pixel_index].astype(jnp.float32)
    visible_f = visible.astype(jnp.float32)
    seen_count = lax.optimization_barrier(jnp.sum(visible_f, axis=1))
    scene_hits = (scene_id[:, None] == jnp.arange(scene_weight.shape[0])[None, :]).astype(jnp.float32)
    ray_weight = lax.optimization_barrier(jnp.sum(scene_hits * scene_weight.astype(jnp.float32)[None, :], axis=1))
    weight_sum = jnp.sum(ray_weight)
    block_rays = 16
    blocks = RAYS // block_rays

    def loss_of(flat_params):
        params = unpack(flat_params)
        feature, total_sum, total_square = views_part(params, features_in, visible_f)
        average, variance = moments(total_sum, total_square, seen_count)
        numerator, denominator, colour_sum = blend_part(params, feature, average, variance, features_in, visible_f)

        def one_block(pieces):
            return ray_part(params, *pieces)
        pieces = (numerator.reshape(blocks, -1, 16), denominator.reshape(blocks, -1, 16), colour_sum.reshape(blocks, -1, 3), deltas.reshape(blocks, block_rays, -1), targets.reshape(blocks, block_rays, 3), ray_weight.reshape(blocks, block_rays))
        partial_losses = lax.map(jax.checkpoint(one_block), pieces)
        return jnp.sum(partial_losses) / weight_sum
    loss, back_fn = jax.vjp(loss_of, weights_f)
    gradient, = back_fn(jnp.ones((), jnp.float32))
    master_new, first_new, second_new = adamw(master, first_moment, second_moment, gradient, step_count)
    return (loss, master_new, first_new, second_new)
```

```python
import jax
import jax.numpy as jnp
from jax import lax
from jax.experimental import pallas as pl
from jax.experimental.pallas import tpu as pltpu
from jax.sharding import PartitionSpec as P

F32 = jnp.float32
BF16 = jnp.bfloat16
SEEN_VIEWS = 10
CHANNELS = 35
STRIP = 40
RAY = 192
CHUNK = 2 * RAY
PASSES = 2
MOMENT_DECAY = 0.5
SQUARE_DECAY = 0.5
LEARNING_RATE = 0.05
WEIGHT_DECAY = 0.01
EPSILON = 1e-08
NN = (((1,), (0,)), ((), ()))
NT = (((1,), (1,)), ((), ()))
TN = (((0,), (0,)), ((), ()))


def dot(left, right, dims=NN):
    return lax.dot_general(left, right, dims, preferred_element_type=F32)


def parts(value, count):
    out = []
    for step in range(count):
        piece = value.astype(BF16)
        out.append(piece)
        if step + 1 < count:
            value = value - piece.astype(F32)
    return out


def dot_left(value, right, dims, count=PASSES):
    return sum(dot(piece, right, dims) for piece in parts(value, count))


def dot_right(left, value, dims, count=PASSES):
    return sum(dot(left, piece, dims) for piece in parts(value, count))


def elu_pair(value):
    slope = jnp.exp(jnp.minimum(value, 0.0))
    return jnp.maximum(value, 0.0) + (slope - 1.0), slope


def iota(shape, axis):
    return lax.broadcasted_iota(jnp.int32, shape, axis)


def gather_kernel(views, tile, pix_ref, vis_ref, map_ref, out_ref):
    pixels = map_ref.shape[2]
    strips = []
    row = iota((STRIP, tile), 0)
    for view in range(views):
        index = pix_ref[view : view + 1, :]
        high = jnp.broadcast_to(index >> 8, (STRIP, tile))
        low = jnp.broadcast_to(index & 255, (256, tile))
        picked = (iota((256, tile), 0) == low).astype(F32).astype(BF16)
        total = jnp.zeros((CHANNELS, tile), F32)
        for block in range(pixels // 256):
            found = dot(map_ref[view, :, 256 * block : 256 * (block + 1)], picked)
            total = jnp.where(high[:CHANNELS] == block, found, total)
        total = jnp.concatenate([total, jnp.zeros((STRIP - CHANNELS, tile), F32)], axis=0)
        seen = jnp.broadcast_to(vis_ref[view : view + 1, :].astype(F32), (STRIP, tile))
        total = jnp.where(row == CHANNELS, 1.0, total)
        total = jnp.where(row == CHANNELS + 1, seen, total)
        strips.append(total)
    out_ref[0] = jnp.concatenate(strips, axis=0).astype(BF16)


def gather_rows(pix, vis, maps, me, group):
    views, points = pix.shape
    tile = 256
    own = points // group
    return pl.pallas_call(
        lambda me_ref, *refs: gather_kernel(views, tile, *refs),
        out_shape=jax.ShapeDtypeStruct((group, views * STRIP, own), BF16),
        grid_spec=pltpu.PrefetchScalarGridSpec(
            num_scalar_prefetch=1,
            grid=(group, own // tile),
            in_specs=[
                pl.BlockSpec((views, tile), lambda k, t, me: (0, (me[0] ^ k) * (own // tile) + t)),
                pl.BlockSpec((views, tile), lambda k, t, me: (0, (me[0] ^ k) * (own // tile) + t)),
                pl.BlockSpec(maps.shape, lambda k, t, me: (0, 0, 0)),
            ],
            out_specs=pl.BlockSpec((1, views * STRIP, tile), lambda k, t, me: (k, 0, t)),
        ),
    )(me, pix, vis, maps)


def roll(value, shift):
    return pltpu.roll(value, shift % 128, 1)


def unpack(a_ref, r64, r32, r16):
    for b in range(2):
        r64[pl.ds(b, 18, stride=2), :] = roll(a_ref[0:18, :], -64 * b)
    for b in range(4):
        r32[pl.ds(b, 33, stride=4), :] = roll(a_ref[18:51, :], -32 * b)
    for b in range(8):
        r16[pl.ds(b, 39, stride=8), :] = roll(a_ref[50:89, :], -16 * b)


def column(rows):
    return rows.T[:, 0:1]


def main_kernel(
    views,
    ray_base,
    me_ref,
    x0,
    x1,
    x2,
    x3,
    a_ref,
    delta_ref,
    target_ref,
    weight_ref,
    out_ref,
    r64,
    r32,
    r16,
    xs,
    hb,
    he,
    ff,
    fe,
    jb,
    ib,
    ie,
    ee,
    blk,
    w2s,
    u1s,
    tri_s,
    g64,
    g32,
    g16,
    gw1,
    gb2,
    gc1,
    gc2,
    gd1,
    gs2,
    gdd,
    loss_s,
):
    step = pl.program_id(0)
    n = CHUNK
    lane = iota((1, n), 1)
    first_ray = lane < RAY
    me = me_ref[0]

    @pl.when(step == 0)
    def _():
        unpack(a_ref, r64, r32, r16)
        for ref in (g64, g32, g16, gw1, gb2, gc1, gc2, gd1, gs2, gdd, loss_s):
            ref[...] = jnp.zeros_like(ref)
        before = (iota((n, n), 0) < iota((n, n), 1)) & (
            (iota((n, n), 0) < RAY) == (iota((n, n), 1) < RAY)
        )
        tri_s[...] = before.astype(F32).astype(BF16)
        w1t = jnp.where(iota((64, 128), 1) < 36, 1.0, 0.0) * jnp.concatenate(
            [r64[0:36, :], jnp.zeros((92, 128), F32)], axis=0
        ).T[:64]
        for view in range(views):
            blk[64 * view : 64 * (view + 1), :] = roll(w1t, STRIP * view).astype(BF16)

    for k, ref in enumerate((x0, x1, x2, x3)):
        xs[me ^ k] = ref[0]

    w2 = r32[0:64, :][:, :32]
    w2b = w2.astype(BF16)
    w2t = w2.T.astype(BF16)
    b2 = column(r32[64:72, :])[:32]
    u1 = r32[65:129, :][:, :32]
    u1b = u1.astype(BF16)
    u1at = u1[:32].T.astype(BF16)
    u1bt = u1[32:].T.astype(BF16)
    c1 = column(r32[129:137, :])[:32]
    u2 = r16[4:36, :][:, :16]
    u2b = u2.astype(BF16)
    u2t = u2.T.astype(BF16)
    c2 = column(r16[36:44, :])[:16]
    keep16 = iota((48, 128), 1) < 16
    qkv = sum(
        roll(jnp.where(keep16, r16[pl.ds(37 + a, 48, stride=4), :], 0.0), 16 * a) for a in range(4)
    )
    wq, wk, wv = qkv[0:16], qkv[16:32], qkv[32:48]
    wqb = wq[:, :64].astype(BF16)
    wqt = wq[:, :64].T.astype(BF16)
    wk_of = [roll(wk, 64 * r).astype(BF16) for r in range(2)]
    wv_of = [roll(wv, 64 * r).astype(BF16) for r in range(2)]
    wo = r16[229:293, :][:, :16]
    wob = wo.astype(BF16)
    wot = wo.T.astype(BF16)
    s1 = r16[293:309, :][:, :16]
    s1b = s1.astype(BF16)
    s1t = s1.T.astype(BF16)
    d1 = column(r16[309:317, :])[:16]
    s2 = column(r16[310:318, :])[:16]
    d2 = r16[311:312, 0:1]

    def seen_of(view):
        at = STRIP * (view % views)
        return xs[view // views, at : at + STRIP, :].astype(F32)

    sum1 = jnp.zeros((32, n), F32)
    sum2 = jnp.zeros((32, n), F32)
    seen = jnp.zeros((1, n), F32)
    for group in range(-(-SEEN_VIEWS // views)):
        count = min(views, SEEN_VIEWS - group * views)
        pre = dot(blk[0 : 64 * count, 0 : views * STRIP], xs[group])
        for local in range(count):
            view = group * views + local
            value, slope = elu_pair(pre[64 * local : 64 * (local + 1)])
            hidden = value.astype(BF16)
            hb[view] = hidden
            he[view] = slope
            value, slope = elu_pair(dot(w2t, hidden) + b2)
            ff[view] = value
            fe[view] = slope
            vis = seen_of(view)[CHANNELS + 1 : CHANNELS + 2]
            part = vis * value
            sum1 = sum1 + part
            sum2 = sum2 + part * value
            seen = seen + vis
    average = sum1 / seen
    variance = sum2 / seen - average * average
    variance_low = variance.astype(BF16)
    shared = dot(u1bt, variance_low) + c1
    num = jnp.zeros((16, n), F32)
    den = jnp.zeros((16, n), F32)
    col = jnp.zeros((3, n), F32)
    for view in range(SEEN_VIEWS):
        strip = seen_of(view)
        feature = ff[view]
        joined = (feature - average).astype(BF16)
        jb[view] = joined
        value, slope = elu_pair(dot(u1at, joined) + shared)
        inner = value.astype(BF16)
        ib[view] = inner
        ie[view] = slope
        e = strip[CHANNELS + 1 : CHANNELS + 2] * jnp.exp(dot(u2t, inner) + c2)
        ee[view] = e
        num = num + e * feature[:16]
        den = den + e
        col = col + e[0:1] * strip[32:35]

    inv = 1.0 / den
    tokens = num / den
    colour = col / den[0:1]
    token_low = tokens.astype(BF16)
    token_t = tokens.T.astype(BF16)
    halves = [token_t[RAY * r : RAY * (r + 1)] for r in range(2)]
    query = dot(wqt, token_low).astype(BF16)
    kk_f = dot(halves[0], wk_of[0]) + dot(halves[1], wk_of[1])
    vv_f = dot(halves[0], wv_of[0]) + dot(halves[1], wv_of[1])
    kk = kk_f.astype(BF16)
    vv = vv_f.astype(BF16)
    kkt = kk.astype(F32).T.astype(BF16)
    vvt = vv.astype(F32).T.astype(BF16)
    row64 = iota((64, n), 0)

    def spread(value, head):
        mine = jnp.where((row64 >> 4) == head, value.astype(F32), 0.0)
        one = jnp.where(first_ray, mine, 0.0)
        return jnp.concatenate([one, mine - one], axis=0)

    def fold(value):
        return jnp.where(first_ray, value[:16], value[16:])

    def head_rows(value, head):
        at = 16 * head
        return jnp.concatenate([value[at : at + 16], value[64 + at : 80 + at]], axis=0)

    probs = []
    attended = []
    query_of = []
    for head in range(4):
        q_head = spread(query, head).astype(BF16)
        query_of.append(q_head)
        score = dot(kk, q_head) * 0.25
        score = jnp.exp(score - jnp.max(score, axis=0, keepdims=True))
        prob = score / jnp.sum(score, axis=0, keepdims=True)
        probs.append(prob)
        attended.append(fold(dot(head_rows(vvt, head), prob.astype(BF16))))
    attended = jnp.concatenate(attended, axis=0).astype(BF16)
    mixed = tokens + dot(wot, attended)
    mixed_low = mixed.astype(BF16)
    value, s_slope = elu_pair(dot(s1t, mixed_low) + d1)
    act = value.astype(BF16).astype(F32)
    z = jnp.sum(act * s2, axis=0, keepdims=True) + d2
    delta = delta_ref[0]
    ez = jnp.exp(-jnp.abs(z))
    density = jnp.maximum(z, 0.0) + jnp.log1p(ez)
    sigmoid = jnp.where(z >= 0.0, 1.0, ez) / (1.0 + ez)
    optical = density * delta
    tri = tri_s[...]

    def exact_rows(value):
        pad = jnp.zeros((13, n), F32)
        return jnp.concatenate([p.astype(F32) for p in parts(value, 3)] + [pad], axis=0).astype(BF16)

    before = jnp.sum(dot(exact_rows(optical), tri), axis=0, keepdims=True)
    through = jnp.exp(-before)
    gone = jnp.exp(-optical)
    render = through * (1.0 - gone)
    drawn = render * colour
    targets = target_ref[0]
    rweight = weight_ref[0]
    d_pixel = jnp.zeros((3, n), F32)
    loss = jnp.zeros((1, 1), F32)
    for r in range(2):
        mask = first_ray if r == 0 else jnp.logical_not(first_ray)
        pixel = jnp.sum(jnp.where(mask, drawn, 0.0), axis=1, keepdims=True)
        miss = pixel - targets[0:3, r : r + 1]
        scale = rweight[0:1, r : r + 1]
        loss = loss + scale * jnp.sum(miss * miss, axis=0, keepdims=True)
        d_pixel = d_pixel + jnp.where(mask, 2.0 * scale * miss, 0.0)
    place = iota((8, 128), 1) + 128 * iota((8, 128), 0)
    loss_s[...] += jnp.where(place == 0, loss, 0.0) + jnp.where(
        place == 1, rweight[0:1, 0:1] + rweight[0:1, 1:2], 0.0
    )

    d_render = jnp.sum(d_pixel * colour, axis=0, keepdims=True)
    d_colour = d_pixel * render
    d_before = -render * d_render
    d_optical = through * gone * d_render + jnp.sum(
        dot(exact_rows(d_before), tri, NT), axis=0, keepdims=True
    )
    dz = d_optical * delta * sigmoid
    gs2[...] += act * dz
    gdd[...] += jnp.where(iota((8, n), 0) == 0, dz, 0.0)
    d_pre = s2 * dz * s_slope
    gd1[...] += d_pre
    g16[293:309, :] += widen(dot_right(mixed_low, d_pre, NT))
    d_mixed = dot_right(s1b, d_pre, NN)
    g16[229:293, :] += widen(dot_right(attended, d_mixed, NT))
    d_att = dot_right(wob, d_mixed, NN)
    d_query = []
    d_kk = jnp.zeros((RAY, 128), F32)
    d_vv = jnp.zeros((RAY, 128), F32)
    for head in range(4):
        prob = probs[head]
        d_head = parts(spread(d_att, head), PASSES)
        d_prob = sum(dot(vv, piece) for piece in d_head)
        low = prob.astype(BF16)
        d_vv = d_vv + sum(dot(low, piece, NT) for piece in d_head)
        d_score = prob * (d_prob - jnp.sum(prob * d_prob, axis=0, keepdims=True)) * 0.25
        pieces = parts(d_score, PASSES)
        d_query.append(fold(sum(dot(head_rows(kkt, head), piece) for piece in pieces)))
        d_kk = d_kk + sum(dot(piece, query_of[head], NT) for piece in pieces)
    d_query = jnp.concatenate(d_query, axis=0)
    gq = dot_right(token_low, d_query, NT)
    gk = [dot_right(halves[r], d_kk, TN) for r in range(2)]
    gv = [dot_right(halves[r], d_vv, TN) for r in range(2)]
    wide = jnp.concatenate([widen(gq), gk[0] + roll(gk[1], 64), gv[0] + roll(gv[1], 64)], axis=0)
    for a in range(4):
        at = pl.ds(37 + a, 48, stride=4)
        g16[at, :] += jnp.where(keep16, roll(wide, -16 * a), 0.0)
    d_halves = [
        dot_left(d_kk, wk_of[r], NT) + dot_left(d_vv, wv_of[r], NT) for r in range(2)
    ]
    d_tokens = d_mixed + dot_right(wqb, d_query, NN) + jnp.concatenate(d_halves, axis=0).T
    d_num = d_tokens * inv
    d_den = -d_num * tokens
    d_col = d_colour * inv[0:1]
    d_den0 = -jnp.sum(d_col * colour, axis=0, keepdims=True)
    row16 = iota((16, n), 0)
    d_den = d_den + jnp.where(row16 == 0, d_den0, 0.0)

    d_average = jnp.zeros((32, n), F32)
    d_shared = jnp.zeros((32, n), F32)
    sum_c2 = jnp.zeros((16, n), F32)
    grad_u2 = jnp.zeros((32, 16), F32)
    grad_u1 = jnp.zeros((32, 32), F32)
    for view in range(SEEN_VIEWS):
        strip = seen_of(view)
        e = ee[view]
        feature = ff[view]
        d_e = d_num * feature[:16] + d_den
        d_e = d_e + jnp.where(
            row16 == 0, jnp.sum(d_col * strip[32:35], axis=0, keepdims=True), 0.0
        )
        d_logit = d_e * e
        sum_c2 = sum_c2 + d_logit
        pieces = parts(d_logit, PASSES)
        grad_u2 = grad_u2 + sum(dot(ib[view], piece, NT) for piece in pieces)
        d_inner = sum(dot(u2b, piece) for piece in pieces) * ie[view]
        d_shared = d_shared + d_inner
        pieces = parts(d_inner, PASSES)
        grad_u1 = grad_u1 + sum(dot(jb[view], piece, NT) for piece in pieces)
        d_joined = sum(dot(u1b[:32], piece) for piece in pieces)
        d_average = d_average - d_joined
        ee[view] = d_num * e
        ie[view] = d_joined
    pieces = parts(d_shared, PASSES)
    d_variance = sum(dot(u1b[32:], piece) for piece in pieces)
    g16[4:36, :] += widen(grad_u2)
    g32[65:97, :] += widen(grad_u1)
    g32[97:129, :] += widen(sum(dot(variance_low, piece, NT) for piece in pieces))
    gc1[...] += d_shared
    gc2[...] += sum_c2
    inv_seen = 1.0 / seen
    d_square = d_variance * inv_seen
    d_sum = (d_average - 2.0 * average * d_variance) * inv_seen

    grad_w2 = jnp.zeros((64, 32), F32)
    sum_b2 = jnp.zeros((32, n), F32)
    for group in range(-(-SEEN_VIEWS // views)):
        count = min(views, SEEN_VIEWS - group * views)
        d_hidden = []
        for local in range(count):
            view = group * views + local
            vis = seen_of(view)[CHANNELS + 1 : CHANNELS + 2]
            d_feature = ie[view] + vis * (d_sum + 2.0 * ff[view] * d_square)
            d_feature = d_feature + jnp.concatenate([ee[view], jnp.zeros((16, n), F32)], axis=0)
            d_feature = d_feature * fe[view]
            sum_b2 = sum_b2 + d_feature
            pieces = parts(d_feature, PASSES)
            grad_w2 = grad_w2 + sum(dot(hb[view], piece, NT) for piece in pieces)
            d_hidden.append(sum(dot(w2b, piece) for piece in pieces) * he[view])
        d_hidden = jnp.concatenate(d_hidden, axis=0)
        gw1[:, 0 : 64 * count] += dot_right(xs[group], d_hidden, NT)
    g32[0:64, :] += widen(grad_w2)
    gb2[...] += sum_b2

    @pl.when(step == pl.num_programs(0) - 1)
    def _():
        ones = jnp.ones((8, n), BF16)
        row_of = lambda ref: widen(dot_right(ones, ref[...], NT, 3)[0:1])
        g32[64:65, :] = row_of(gb2)
        g32[129:130, :] = row_of(gc1)
        g16[36:37, :] = row_of(gc2)
        g16[309:310, :] = row_of(gd1)
        g16[310:311, :] = row_of(gs2)
        g16[311:312, :] = jnp.where(iota((1, 128), 1) == 0, row_of(gdd), 0.0)
        total = gw1[0:36, 0:128]
        total = total + roll(gw1[STRIP : STRIP + 36, 0:128], 64)
        total = total + gw1[2 * STRIP : 2 * STRIP + 36, 128:256]
        g64[0:36, :] = jnp.where(iota((36, 128), 1) < 64, total, 0.0)
        out_ref[...] = jnp.zeros_like(out_ref)
        out_ref[0:18, :] = sum(roll(g64[pl.ds(b, 18, stride=2), :], 64 * b) for b in range(2))
        out_ref[18:51, :] += sum(roll(g32[pl.ds(b, 33, stride=4), :], 32 * b) for b in range(4))
        out_ref[50:89, :] += sum(roll(g16[pl.ds(b, 39, stride=8), :], 16 * b) for b in range(8))
        out_ref[96:104, :] = loss_s[...]


def widen(value):
    rows, width = value.shape
    return jnp.concatenate([value, jnp.zeros((rows, 128 - width), F32)], axis=1)


def run_main(me, blocks, weights, deltas, targets, ray_weight, ray_base=None):
    rows, points = blocks[0].shape[1:]
    views = rows // STRIP
    n = CHUNK
    steps = points // n
    v = SEEN_VIEWS
    pairs = deltas.reshape(steps, 1, n)
    target_pairs = jnp.pad(
        targets.reshape(steps, 2, 3).transpose(0, 2, 1), ((0, 0), (0, 5), (0, 126))
    )
    weight_pairs = jnp.pad(ray_weight.reshape(steps, 1, 2), ((0, 0), (0, 7), (0, 126)))
    vm = pltpu.VMEM
    order = [k if blocks[k].shape[0] > 1 else 0 for k in range(len(blocks))]
    block = lambda k: pl.BlockSpec((1, rows, n), lambda t, me: (order[k], 0, t))
    return pl.pallas_call(
        lambda *refs: main_kernel(views, 0, *refs),
        out_shape=jax.ShapeDtypeStruct((104, 128), F32),
        grid_spec=pltpu.PrefetchScalarGridSpec(
            num_scalar_prefetch=1,
            grid=(steps,),
            in_specs=[block(k) for k in range(4)]
            + [
                pl.BlockSpec(weights.shape, lambda t, me: (0, 0)),
                pl.BlockSpec((1, 1, n), lambda t, me: (t, 0, 0)),
                pl.BlockSpec((1, 8, 128), lambda t, me: (t, 0, 0)),
                pl.BlockSpec((1, 8, 128), lambda t, me: (t, 0, 0)),
            ],
            out_specs=pl.BlockSpec((104, 128), lambda t, me: (0, 0)),
            scratch_shapes=[
                vm((40, 128), F32),
                vm((144, 128), F32),
                vm((320, 128), F32),
                vm((4, rows, n), BF16),
                vm((v, 64, n), BF16),
                vm((v, 64, n), F32),
                vm((v, 32, n), F32),
                vm((v, 32, n), F32),
                vm((v, 32, n), BF16),
                vm((v, 32, n), BF16),
                vm((v, 32, n), F32),
                vm((v, 16, n), F32),
                vm((64 * views, 128), BF16),
                vm((8, 128), BF16),
                vm((8, 128), BF16),
                vm((n, n), BF16),
                vm((40, 128), F32),
                vm((136, 128), F32),
                vm((312, 128), F32),
                vm((rows, 256), F32),
                vm((32, n), F32),
                vm((32, n), F32),
                vm((16, n), F32),
                vm((16, n), F32),
                vm((16, n), F32),
                vm((8, n), F32),
                vm((8, 128), F32),
            ],
        ),
        compiler_params=pltpu.CompilerParams(vmem_limit_bytes=48 * 1024 * 1024),
    )(me, *blocks, weights, pairs, target_pairs, weight_pairs)


def adamw(master, first_moment, second_moment, gradient, step_count):
    step_float = step_count[0].astype(F32)
    first_new = MOMENT_DECAY * first_moment + (1.0 - MOMENT_DECAY) * gradient
    second_new = SQUARE_DECAY * second_moment + (1.0 - SQUARE_DECAY) * gradient * gradient
    first_fix = 1.0 - jnp.power(MOMENT_DECAY, step_float)
    second_fix = 1.0 - jnp.power(SQUARE_DECAY, step_float)
    update = first_new / first_fix / (jnp.sqrt(second_new / second_fix) + EPSILON)
    master_new = master - LEARNING_RATE * (update + WEIGHT_DECAY * master)
    return (master_new, first_new, second_new)


def body(
    master,
    first_moment,
    second_moment,
    step_count,
    feature_maps,
    pixel_index,
    visible,
    deltas,
    targets,
    scene_id,
    scene_weight,
):
    group = lax.axis_size("views")
    shards = lax.axis_size("rays")
    rays = deltas.shape[0]
    own = rays // group
    shard = master.shape[0]
    spot = lax.axis_index("views")
    me = spot.astype(jnp.int32).reshape(1)
    hits = (scene_id[:, None] == jnp.arange(scene_weight.shape[0])[None, :]).astype(F32)
    ray_weight = jnp.sum(hits * scene_weight.astype(F32)[None, :], axis=1)
    narrow = lax.all_gather(master.astype(BF16), "rays", axis=0, tiled=True)
    flat = narrow.astype(F32)[:11384]
    weights = jnp.pad(flat, (0, 96 * 128 - flat.shape[0])).reshape(96, 128)
    rows = gather_rows(pixel_index.T, visible.T, feature_maps, me, group)
    blocks = [rows]
    for k in range(1, group):
        pairs = [(i, i ^ k) for i in range(group)]
        blocks.append(lax.ppermute(rows[k : k + 1], "views", pairs))
    mine = lambda array: lax.dynamic_slice_in_dim(array, spot * own, own, 0)
    packed = run_main(me, blocks, weights, mine(deltas), mine(targets), mine(ray_weight))
    summed = packed[:89].reshape(-1)
    size = shards * shard
    if summed.shape[0] < size:
        summed = jnp.pad(summed, (0, size - summed.shape[0]))
    extra = jnp.broadcast_to(packed[96, :2][None], (shards, 2))
    send = jnp.concatenate([summed[:size].reshape(shards, shard), extra], axis=1)
    got = lax.all_to_all(send, "rays", 0, 0, tiled=True)
    partial = jnp.sum(got, axis=0)
    whole = partial
    for k in range(1, group):
        whole = whole + lax.ppermute(partial, "views", [(i, i ^ k) for i in range(group)])
    seed = 1.0 / whole[shard + 1]
    loss = whole[shard] * seed
    gradient = whole[:shard] * seed
    return (loss, *adamw(master, first_moment, second_moment, gradient, step_count))


def solution(mesh):
    placed = (
        P("rays"),
        P("rays"),
        P("rays"),
        P(),
        P("views", None, None),
        P("rays", "views"),
        P("rays", "views"),
        P("rays", None),
        P("rays", None),
        P("rays"),
        P(),
    )
    return jax.shard_map(
        body,
        mesh=mesh,
        in_specs=placed,
        out_specs=(P(), P("rays"), P("rays"), P("rays")),
        check_vma=False,
    )
```

```python
import jax
import jax.numpy as jnp
from jax import lax
from jax.experimental import pallas as pl
from jax.experimental.pallas import tpu as pltpu
from jax.sharding import PartitionSpec as P


F32 = jnp.float32
BF16 = jnp.bfloat16
SEEN_VIEWS = 10
CHANNELS = 35
STRIP = 40
BAND = 48
GATHER_TILE = 256
RAY = 192
CHUNK = 2 * RAY
PASSES = 2
MOMENT_DECAY = 0.5
SQUARE_DECAY = 0.5
LEARNING_RATE = 0.05
WEIGHT_DECAY = 0.01
EPSILON = 1e-08
NN = (((1,), (0,)), ((), ()))
NT = (((1,), (1,)), ((), ()))
TN = (((0,), (0,)), ((), ()))


def dot(left, right, dims=NN):
    return lax.dot_general(left, right, dims, preferred_element_type=F32)


def parts(value, count):
    out = []
    for step in range(count):
        piece = value.astype(BF16)
        out.append(piece)
        if step + 1 < count:
            value = value - piece.astype(F32)
    return out


def dot_left(value, right, dims, count=PASSES):
    return sum(dot(piece, right, dims) for piece in parts(value, count))


def dot_right(left, value, dims, count=PASSES):
    return sum(dot(left, piece, dims) for piece in parts(value, count))


def elu_pair(value):
    slope = jnp.exp(jnp.minimum(value, 0.0))
    return jnp.maximum(value, 0.0) + (slope - 1.0), slope


def iota(shape, axis):
    return lax.broadcasted_iota(jnp.int32, shape, axis)


def gather_kernel(views, tile, count, *refs):
    pix_refs, vis_refs = refs[1 : 1 + count], refs[1 + count : 1 + 2 * count]
    map_ref = refs[1 + 2 * count]
    outs, stacked = refs[2 + 2 * count : -1], refs[-1]
    blocks = map_ref.shape[2] // 256

    @pl.when(pl.program_id(0) == 0)
    def _():
        for view in range(views):
            for block in range(blocks):
                stacked[view, BAND * block : BAND * block + CHANNELS, :] = map_ref[
                    view, :, 256 * block : 256 * (block + 1)
                ]

    row = iota((STRIP, tile), 0)
    for pix_ref, vis_ref, out_ref in zip(pix_refs, vis_refs, outs):
        strips = []
        for view in range(views):
            index = pix_ref[view : view + 1, :]
            high = jnp.broadcast_to(index >> 8, (STRIP, tile))
            low = jnp.broadcast_to(index & 255, (256, tile))
            picked = (iota((256, tile), 0) == low).astype(F32).astype(BF16)
            found = dot(stacked[view], picked)
            total = jnp.zeros((STRIP, tile), F32)
            for block in range(blocks):
                total = jnp.where(
                    high == block, found[BAND * block : BAND * block + STRIP], total
                )
            seen = jnp.broadcast_to(vis_ref[view : view + 1, :].astype(F32), (STRIP, tile))
            total = jnp.where(row == CHANNELS, 1.0, total)
            total = jnp.where(row == CHANNELS + 1, seen, total)
            total = jnp.where(row > CHANNELS + 1, 0.0, total)
            strips.append(total)
        out_ref[0] = jnp.concatenate(strips, axis=0).astype(BF16)


def gather_rows(pix, vis, maps, me, group, ways):
    views, points = pix.shape
    tile = GATHER_TILE
    own = points // group
    tiles = own // tile
    count = len(ways)
    part = lambda k: pl.BlockSpec((views, tile), lambda t, me: (0, (me[0] ^ k) * tiles + t))
    out = jax.ShapeDtypeStruct((1, views * STRIP, own), BF16)
    flops = 2 * views * own * count * BAND * maps.shape[2]
    return pl.pallas_call(
        lambda *refs: gather_kernel(views, tile, count, *refs),
        out_shape=[out] * count,
        grid_spec=pltpu.PrefetchScalarGridSpec(
            num_scalar_prefetch=1,
            grid=(tiles,),
            in_specs=[part(k) for k in ways] * 2
            + [pl.BlockSpec(maps.shape, lambda t, me: (0, 0, 0))],
            out_specs=[pl.BlockSpec((1, views * STRIP, tile), lambda t, me: (0, 0, t))] * count,
            scratch_shapes=[pltpu.VMEM((views, BAND * (maps.shape[2] // 256), 256), BF16)],
        ),
        compiler_params=pltpu.CompilerParams(vmem_limit_bytes=40 * 1024 * 1024),
        cost_estimate=pl.CostEstimate(flops=flops, bytes_accessed=maps.size * 2, transcendentals=0),
    )(me, *([pix] * count), *([vis] * count), maps)


def roll(value, shift):
    return pltpu.roll(value, shift % 128, 1)


def unpack(a_ref, r64, r32, r16):
    for b in range(2):
        r64[pl.ds(b, 18, stride=2), :] = roll(a_ref[0:18, :], -64 * b)
    for b in range(4):
        r32[pl.ds(b, 33, stride=4), :] = roll(a_ref[18:51, :], -32 * b)
    for b in range(8):
        r16[pl.ds(b, 39, stride=8), :] = roll(a_ref[50:89, :], -16 * b)


def assemble(place, shard, shard_refs, a_ref):
    a_ref[...] = jnp.zeros_like(a_ref)
    shards, rows, _ = shard_refs.shape
    for k in range(shards):
        start = (place ^ k) * shard
        shift = start & 127
        value = pltpu.roll(shard_refs[k].astype(F32), shift, 1)
        keep = iota((rows, 128), 1) >= shift
        first = start >> 7
        a_ref[pl.ds(first, rows), :] += jnp.where(keep, value, 0.0)
        a_ref[pl.ds(first + 1, rows), :] += jnp.where(keep, 0.0, value)


def column(rows):
    return rows.T[:, 0:1]


def main_kernel(views, shard, me_ref, *refs):
    shard_refs, refs = refs[0], refs[1:]
    (
    x0,
    x1,
    x2,
    x3,
    delta_ref,
    target_ref,
    weight_ref,
    out_ref,
    a_ref,
    r64,
    r32,
    r16,
    xs,
    hb,
    he,
    ff,
    fe,
    jb,
    ib,
    ie,
    ee,
    blk,
    _,
    _,
    tri_s,
    g64,
    g32,
    g16,
    gw1,
    gb2,
    gc1,
    gc2,
    gd1,
    gs2,
    gdd,
    loss_s,
    ) = refs
    step = pl.program_id(0)
    n = CHUNK
    lane = iota((1, n), 1)
    first_ray = lane < RAY
    me = me_ref[0]

    @pl.when(step == 0)
    def _():
        assemble(me_ref[1], shard, shard_refs, a_ref)
        unpack(a_ref, r64, r32, r16)
        for ref in (g64, g32, g16, gw1, gb2, gc1, gc2, gd1, gs2, gdd, loss_s):
            ref[...] = jnp.zeros_like(ref)
        before = (iota((n, n), 0) < iota((n, n), 1)) & (
            (iota((n, n), 0) < RAY) == (iota((n, n), 1) < RAY)
        )
        tri_s[...] = before.astype(F32).astype(BF16)
        w1t = jnp.where(iota((64, 128), 1) < 36, 1.0, 0.0) * jnp.concatenate(
            [r64[0:36, :], jnp.zeros((92, 128), F32)], axis=0
        ).T[:64]
        for view in range(views):
            blk[64 * view : 64 * (view + 1), :] = roll(w1t, STRIP * view).astype(BF16)

    for k, ref in enumerate((x0, x1, x2, x3)):
        xs[me ^ k] = ref[0]

    w2 = r32[0:64, :][:, :32]
    w2b = w2.astype(BF16)
    w2t = w2.T.astype(BF16)
    b2 = column(r32[64:72, :])[:32]
    u1 = r32[65:129, :][:, :32]
    u1b = u1.astype(BF16)
    u1at = u1[:32].T.astype(BF16)
    u1bt = u1[32:].T.astype(BF16)
    c1 = column(r32[129:137, :])[:32]
    u2 = r16[4:36, :][:, :16]
    u2b = u2.astype(BF16)
    u2t = u2.T.astype(BF16)
    c2 = column(r16[36:44, :])[:16]
    keep16 = iota((48, 128), 1) < 16
    qkv = sum(
        roll(jnp.where(keep16, r16[pl.ds(37 + a, 48, stride=4), :], 0.0), 16 * a) for a in range(4)
    )
    wq, wk, wv = qkv[0:16], qkv[16:32], qkv[32:48]
    wqb = wq[:, :64].astype(BF16)
    wqt = wq[:, :64].T.astype(BF16)
    wk_of = [roll(wk, 64 * r).astype(BF16) for r in range(2)]
    wv_of = [roll(wv, 64 * r).astype(BF16) for r in range(2)]
    wo = r16[229:293, :][:, :16]
    wob = wo.astype(BF16)
    wot = wo.T.astype(BF16)
    s1 = r16[293:309, :][:, :16]
    s1b = s1.astype(BF16)
    s1t = s1.T.astype(BF16)
    d1 = column(r16[309:317, :])[:16]
    s2 = column(r16[310:318, :])[:16]
    d2 = r16[311:312, 0:1]

    def seen_of(view):
        at = STRIP * (view % views)
        return xs[view // views, at : at + STRIP, :].astype(F32)

    sum1 = jnp.zeros((32, n), F32)
    sum2 = jnp.zeros((32, n), F32)
    seen = jnp.zeros((1, n), F32)
    for group in range(-(-SEEN_VIEWS // views)):
        count = min(views, SEEN_VIEWS - group * views)
        pre = dot(blk[0 : 64 * count, 0 : views * STRIP], xs[group])
        for local in range(count):
            view = group * views + local
            value, slope = elu_pair(pre[64 * local : 64 * (local + 1)])
            hidden = value.astype(BF16)
            hb[view] = hidden
            he[view] = slope
            value, slope = elu_pair(dot(w2t, hidden) + b2)
            ff[view] = value
            fe[view] = slope
            vis = seen_of(view)[CHANNELS + 1 : CHANNELS + 2]
            part = vis * value
            sum1 = sum1 + part
            sum2 = sum2 + part * value
            seen = seen + vis
    average = sum1 / seen
    variance = sum2 / seen - average * average
    variance_low = variance.astype(BF16)
    shared = dot(u1bt, variance_low) + c1
    num = jnp.zeros((16, n), F32)
    den = jnp.zeros((16, n), F32)
    col = jnp.zeros((3, n), F32)
    for view in range(SEEN_VIEWS):
        strip = seen_of(view)
        feature = ff[view]
        joined = (feature - average).astype(BF16)
        jb[view] = joined
        value, slope = elu_pair(dot(u1at, joined) + shared)
        inner = value.astype(BF16)
        ib[view] = inner
        ie[view] = slope
        e = strip[CHANNELS + 1 : CHANNELS + 2] * jnp.exp(dot(u2t, inner) + c2)
        ee[view] = e
        num = num + e * feature[:16]
        den = den + e
        col = col + e[0:1] * strip[32:35]

    inv = 1.0 / den
    tokens = num / den
    colour = col / den[0:1]
    token_low = tokens.astype(BF16)
    token_t = tokens.T.astype(BF16)
    halves = [token_t[RAY * r : RAY * (r + 1)] for r in range(2)]
    query = dot(wqt, token_low).astype(BF16)
    kk_f = dot(halves[0], wk_of[0]) + dot(halves[1], wk_of[1])
    vv_f = dot(halves[0], wv_of[0]) + dot(halves[1], wv_of[1])
    kk = kk_f.astype(BF16)
    vv = vv_f.astype(BF16)
    kkt = kk.astype(F32).T.astype(BF16)
    vvt = vv.astype(F32).T.astype(BF16)
    row64 = iota((64, n), 0)

    def spread(value, head):
        mine = jnp.where((row64 >> 4) == head, value.astype(F32), 0.0)
        one = jnp.where(first_ray, mine, 0.0)
        return jnp.concatenate([one, mine - one], axis=0)

    def fold(value):
        return jnp.where(first_ray, value[:16], value[16:])

    def head_rows(value, head):
        at = 16 * head
        return jnp.concatenate([value[at : at + 16], value[64 + at : 80 + at]], axis=0)

    probs = []
    attended = []
    query_of = []
    for head in range(4):
        q_head = spread(query, head).astype(BF16)
        query_of.append(q_head)
        score = dot(kk, q_head) * 0.25
        score = jnp.exp(score - jnp.max(score, axis=0, keepdims=True))
        prob = score / jnp.sum(score, axis=0, keepdims=True)
        probs.append(prob)
        attended.append(fold(dot(head_rows(vvt, head), prob.astype(BF16))))
    attended = jnp.concatenate(attended, axis=0).astype(BF16)
    mixed = tokens + dot(wot, attended)
    mixed_low = mixed.astype(BF16)
    value, s_slope = elu_pair(dot(s1t, mixed_low) + d1)
    act = value.astype(BF16).astype(F32)
    z = jnp.sum(act * s2, axis=0, keepdims=True) + d2
    delta = delta_ref[0]
    ez = jnp.exp(-jnp.abs(z))
    density = jnp.maximum(z, 0.0) + jnp.log1p(ez)
    sigmoid = jnp.where(z >= 0.0, 1.0, ez) / (1.0 + ez)
    optical = density * delta
    tri = tri_s[...]

    def exact_rows(value):
        pad = jnp.zeros((13, n), F32)
        return jnp.concatenate([p.astype(F32) for p in parts(value, 3)] + [pad], axis=0).astype(BF16)

    before = jnp.sum(dot(exact_rows(optical), tri), axis=0, keepdims=True)
    through = jnp.exp(-before)
    gone = jnp.exp(-optical)
    render = through * (1.0 - gone)
    drawn = render * colour
    targets = target_ref[0]
    rweight = weight_ref[0]
    d_pixel = jnp.zeros((3, n), F32)
    loss = jnp.zeros((1, 1), F32)
    for r in range(2):
        mask = first_ray if r == 0 else jnp.logical_not(first_ray)
        pixel = jnp.sum(jnp.where(mask, drawn, 0.0), axis=1, keepdims=True)
        miss = pixel - targets[0:3, r : r + 1]
        scale = rweight[0:1, r : r + 1]
        loss = loss + scale * jnp.sum(miss * miss, axis=0, keepdims=True)
        d_pixel = d_pixel + jnp.where(mask, 2.0 * scale * miss, 0.0)
    place = iota((8, 128), 1) + 128 * iota((8, 128), 0)
    loss_s[...] += jnp.where(place == 0, loss, 0.0) + jnp.where(
        place == 1, rweight[0:1, 0:1] + rweight[0:1, 1:2], 0.0
    )

    d_render = jnp.sum(d_pixel * colour, axis=0, keepdims=True)
    d_colour = d_pixel * render
    d_before = -render * d_render
    d_optical = through * gone * d_render + jnp.sum(
        dot(exact_rows(d_before), tri, NT), axis=0, keepdims=True
    )
    dz = d_optical * delta * sigmoid
    gs2[...] += act * dz
    gdd[...] += jnp.where(iota((8, n), 0) == 0, dz, 0.0)
    d_pre = s2 * dz * s_slope
    gd1[...] += d_pre
    g16[293:309, :] += widen(dot_right(mixed_low, d_pre, NT))
    d_mixed = dot_right(s1b, d_pre, NN)
    g16[229:293, :] += widen(dot_right(attended, d_mixed, NT))
    d_att = dot_right(wob, d_mixed, NN)
    d_query = []
    d_kk = jnp.zeros((RAY, 128), F32)
    d_vv = jnp.zeros((RAY, 128), F32)
    for head in range(4):
        prob = probs[head]
        d_head = parts(spread(d_att, head), PASSES)
        d_prob = sum(dot(vv, piece) for piece in d_head)
        low = prob.astype(BF16)
        d_vv = d_vv + sum(dot(low, piece, NT) for piece in d_head)
        d_score = prob * (d_prob - jnp.sum(prob * d_prob, axis=0, keepdims=True)) * 0.25
        pieces = parts(d_score, PASSES)
        d_query.append(fold(sum(dot(head_rows(kkt, head), piece) for piece in pieces)))
        d_kk = d_kk + sum(dot(piece, query_of[head], NT) for piece in pieces)
    d_query = jnp.concatenate(d_query, axis=0)
    gq = dot_right(token_low, d_query, NT)
    gk = [dot_right(halves[r], d_kk, TN) for r in range(2)]
    gv = [dot_right(halves[r], d_vv, TN) for r in range(2)]
    wide = jnp.concatenate([widen(gq), gk[0] + roll(gk[1], 64), gv[0] + roll(gv[1], 64)], axis=0)
    for a in range(4):
        at = pl.ds(37 + a, 48, stride=4)
        g16[at, :] += jnp.where(keep16, roll(wide, -16 * a), 0.0)
    d_halves = [
        dot_left(d_kk, wk_of[r], NT) + dot_left(d_vv, wv_of[r], NT) for r in range(2)
    ]
    d_tokens = d_mixed + dot_right(wqb, d_query, NN) + jnp.concatenate(d_halves, axis=0).T
    d_num = d_tokens * inv
    d_den = -d_num * tokens
    d_col = d_colour * inv[0:1]
    d_den0 = -jnp.sum(d_col * colour, axis=0, keepdims=True)
    row16 = iota((16, n), 0)
    d_den = d_den + jnp.where(row16 == 0, d_den0, 0.0)

    d_average = jnp.zeros((32, n), F32)
    d_shared = jnp.zeros((32, n), F32)
    sum_c2 = jnp.zeros((16, n), F32)
    grad_u2 = jnp.zeros((32, 16), F32)
    grad_u1 = jnp.zeros((32, 32), F32)
    for view in range(SEEN_VIEWS):
        strip = seen_of(view)
        e = ee[view]
        feature = ff[view]
        d_e = d_num * feature[:16] + d_den
        d_e = d_e + jnp.where(
            row16 == 0, jnp.sum(d_col * strip[32:35], axis=0, keepdims=True), 0.0
        )
        d_logit = d_e * e
        sum_c2 = sum_c2 + d_logit
        pieces = parts(d_logit, PASSES)
        grad_u2 = grad_u2 + sum(dot(ib[view], piece, NT) for piece in pieces)
        d_inner = sum(dot(u2b, piece) for piece in pieces) * ie[view]
        d_shared = d_shared + d_inner
        pieces = parts(d_inner, PASSES)
        grad_u1 = grad_u1 + sum(dot(jb[view], piece, NT) for piece in pieces)
        d_joined = sum(dot(u1b[:32], piece) for piece in pieces)
        d_average = d_average - d_joined
        ee[view] = d_num * e
        ie[view] = d_joined
    pieces = parts(d_shared, PASSES)
    d_variance = sum(dot(u1b[32:], piece) for piece in pieces)
    g16[4:36, :] += widen(grad_u2)
    g32[65:97, :] += widen(grad_u1)
    g32[97:129, :] += widen(sum(dot(variance_low, piece, NT) for piece in pieces))
    gc1[...] += d_shared
    gc2[...] += sum_c2
    inv_seen = 1.0 / seen
    d_square = d_variance * inv_seen
    d_sum = (d_average - 2.0 * average * d_variance) * inv_seen

    grad_w2 = jnp.zeros((64, 32), F32)
    sum_b2 = jnp.zeros((32, n), F32)
    for group in range(-(-SEEN_VIEWS // views)):
        count = min(views, SEEN_VIEWS - group * views)
        d_hidden = []
        for local in range(count):
            view = group * views + local
            vis = seen_of(view)[CHANNELS + 1 : CHANNELS + 2]
            d_feature = ie[view] + vis * (d_sum + 2.0 * ff[view] * d_square)
            d_feature = d_feature + jnp.concatenate([ee[view], jnp.zeros((16, n), F32)], axis=0)
            d_feature = d_feature * fe[view]
            sum_b2 = sum_b2 + d_feature
            pieces = parts(d_feature, PASSES)
            grad_w2 = grad_w2 + sum(dot(hb[view], piece, NT) for piece in pieces)
            d_hidden.append(sum(dot(w2b, piece) for piece in pieces) * he[view])
        d_hidden = jnp.concatenate(d_hidden, axis=0)
        gw1[:, 0 : 64 * count] += dot_right(xs[group], d_hidden, NT)
    g32[0:64, :] += widen(grad_w2)
    gb2[...] += sum_b2

    @pl.when(step == pl.num_programs(0) - 1)
    def _():
        ones = jnp.ones((8, n), BF16)
        row_of = lambda ref: widen(dot_right(ones, ref[...], NT, 3)[0:1])
        g32[64:65, :] = row_of(gb2)
        g32[129:130, :] = row_of(gc1)
        g16[36:37, :] = row_of(gc2)
        g16[309:310, :] = row_of(gd1)
        g16[310:311, :] = row_of(gs2)
        g16[311:312, :] = jnp.where(iota((1, 128), 1) == 0, row_of(gdd), 0.0)
        total = gw1[0:36, 0:128]
        total = total + roll(gw1[STRIP : STRIP + 36, 0:128], 64)
        total = total + gw1[2 * STRIP : 2 * STRIP + 36, 128:256]
        g64[0:36, :] = jnp.where(iota((36, 128), 1) < 64, total, 0.0)
        out_ref[...] = jnp.zeros_like(out_ref)
        out_ref[0:18, :] = sum(roll(g64[pl.ds(b, 18, stride=2), :], 64 * b) for b in range(2))
        out_ref[18:51, :] += sum(roll(g32[pl.ds(b, 33, stride=4), :], 32 * b) for b in range(4))
        out_ref[50:89, :] += sum(roll(g16[pl.ds(b, 39, stride=8), :], 16 * b) for b in range(8))
        out_ref[96:104, :] = loss_s[...]


def widen(value):
    rows, width = value.shape
    return jnp.concatenate([value, jnp.zeros((rows, 128 - width), F32)], axis=1)


def run_main(me, blocks, pieces, shard, deltas, targets, ray_weight):
    rows, points = blocks[0].shape[1:]
    views = rows // STRIP
    n = CHUNK
    steps = points // n
    v = SEEN_VIEWS
    whole = deltas.shape[0] // 2
    pairs = deltas.reshape(whole, 1, n)
    target_pairs = jnp.pad(
        targets.reshape(whole, 2, 3).transpose(0, 2, 1), ((0, 0), (0, 5), (0, 126))
    )
    weight_pairs = jnp.pad(ray_weight.reshape(whole, 1, 2), ((0, 0), (0, 7), (0, 126)))
    vm = pltpu.VMEM
    own = lambda t, me: (me[0] * steps + t, 0, 0)
    block = pl.BlockSpec((1, rows, n), lambda t, me: (0, 0, t))
    piece = pl.BlockSpec(pieces.shape, lambda t, me: (0, 0, 0))
    return pl.pallas_call(
        lambda *refs: main_kernel(views, shard, *refs),
        out_shape=jax.ShapeDtypeStruct((104, 128), F32),
        grid_spec=pltpu.PrefetchScalarGridSpec(
            num_scalar_prefetch=1,
            grid=(steps,),
            in_specs=[piece]
            + [block] * 4
            + [
                pl.BlockSpec((1, 1, n), own),
                pl.BlockSpec((1, 8, 128), own),
                pl.BlockSpec((1, 8, 128), own),
            ],
            out_specs=pl.BlockSpec((104, 128), lambda t, me: (0, 0)),
            scratch_shapes=[
                vm((120, 128), F32),
                vm((40, 128), F32),
                vm((144, 128), F32),
                vm((320, 128), F32),
                vm((4, rows, n), BF16),
                vm((v, 64, n), BF16),
                vm((v, 64, n), F32),
                vm((v, 32, n), F32),
                vm((v, 32, n), F32),
                vm((v, 32, n), BF16),
                vm((v, 32, n), BF16),
                vm((v, 32, n), F32),
                vm((v, 16, n), F32),
                vm((64 * views, 128), BF16),
                vm((8, 128), BF16),
                vm((8, 128), BF16),
                vm((n, n), BF16),
                vm((40, 128), F32),
                vm((136, 128), F32),
                vm((312, 128), F32),
                vm((rows, 256), F32),
                vm((32, n), F32),
                vm((32, n), F32),
                vm((16, n), F32),
                vm((16, n), F32),
                vm((16, n), F32),
                vm((8, n), F32),
                vm((8, 128), F32),
            ],
        ),
        compiler_params=pltpu.CompilerParams(vmem_limit_bytes=48 * 1024 * 1024),
    )(me, pieces, *blocks, pairs, target_pairs, weight_pairs)


def adamw(master, first_moment, second_moment, gradient, step_count):
    step_float = step_count[0].astype(F32)
    first_new = MOMENT_DECAY * first_moment + (1.0 - MOMENT_DECAY) * gradient
    second_new = SQUARE_DECAY * second_moment + (1.0 - SQUARE_DECAY) * gradient * gradient
    first_fix = 1.0 - jnp.power(MOMENT_DECAY, step_float)
    second_fix = 1.0 - jnp.power(SQUARE_DECAY, step_float)
    update = first_new / first_fix / (jnp.sqrt(second_new / second_fix) + EPSILON)
    master_new = master - LEARNING_RATE * (update + WEIGHT_DECAY * master)
    return (master_new, first_new, second_new)


def body(
    master,
    first_moment,
    second_moment,
    step_count,
    feature_maps,
    pixel_index,
    visible,
    deltas,
    targets,
    scene_id,
    scene_weight,
):
    group = lax.axis_size("views")
    shards = lax.axis_size("rays")
    shard = master.shape[0]
    spots = [lax.axis_index("views"), lax.axis_index("rays")]
    me = jnp.stack(spots).astype(jnp.int32)
    swap = lambda size, k: [(i, i ^ k) for i in range(size)]
    rows = -(-shard // 2048) * 16
    piece = jnp.pad(master.astype(BF16), (0, rows * 128 - shard)).reshape(rows, 128)
    pix, vis = pixel_index.T, visible.T
    held = piece[None]
    links = shards.bit_length() - 1
    for link in range(links):
        held = jnp.concatenate([held, lax.ppermute(held, "rays", swap(shards, 1 << link))])
    far = gather_rows(pix, vis, feature_maps, me, group, (3, 2))
    three = lax.ppermute(far[0], "views", swap(group, 3))
    two = lax.ppermute(far[1], "views", swap(group, 2))
    near = gather_rows(pix, vis, feature_maps, me, group, (1, 0))
    one = lax.ppermute(near[0], "views", swap(group, 1))
    hits = (scene_id[:, None] == jnp.arange(scene_weight.shape[0])[None, :]).astype(F32)
    ray_weight = jnp.sum(hits * scene_weight.astype(F32)[None, :], axis=1)
    packed = run_main(me, [near[1], one, two, three], held, shard, deltas, targets, ray_weight)
    summed = packed[:89].reshape(-1)
    size = shards * shard
    if summed.shape[0] < size:
        summed = jnp.pad(summed, (0, size - summed.shape[0]))
    extra = jnp.broadcast_to(packed[96, :2][None], (shards, 2))
    send = jnp.concatenate([summed[:size].reshape(shards, shard), extra], axis=1)
    got = lax.all_to_all(send, "rays", 0, 0, tiled=True)
    partial = jnp.sum(got, axis=0)
    whole = partial
    for k in range(1, group):
        whole = whole + lax.ppermute(partial, "views", [(i, i ^ k) for i in range(group)])
    seed = 1.0 / whole[shard + 1]
    loss = whole[shard] * seed
    gradient = whole[:shard] * seed
    return (loss, *adamw(master, first_moment, second_moment, gradient, step_count))


def solution(mesh):
    placed = (
        P("rays"),
        P("rays"),
        P("rays"),
        P(),
        P("views", None, None),
        P("rays", "views"),
        P("rays", "views"),
        P("rays", None),
        P("rays", None),
        P("rays"),
        P(),
    )
    return jax.shard_map(
        body,
        mesh=mesh,
        in_specs=placed,
        out_specs=(P(), P("rays"), P("rays"), P("rays")),
        check_vma=False,
    )
```

```python
import jax
import jax.numpy as jnp
from jax import lax
from jax.experimental import pallas as pl
from jax.experimental.pallas import tpu as pltpu
from jax.sharding import PartitionSpec as P


F32 = jnp.float32
BF16 = jnp.bfloat16
SEEN_VIEWS = 10
CHANNELS = 35
STRIP = 40
BAND = 40
SEEN_SHIFT = 14
SEEN_BIT = 1 << SEEN_SHIFT
GATHER_TILE = 256
RAY = 192
CHUNK = 2 * RAY
PASSES = 1
MOMENT_DECAY = 0.5
SQUARE_DECAY = 0.5
LEARNING_RATE = 0.05
WEIGHT_DECAY = 0.01
EPSILON = 1e-08
NN = (((1,), (0,)), ((), ()))
NT = (((1,), (1,)), ((), ()))
TN = (((0,), (0,)), ((), ()))


def dot(left, right, dims=NN):
    return lax.dot_general(left, right, dims, preferred_element_type=F32)


def parts(value, count):
    out = []
    for step in range(count):
        piece = value.astype(BF16)
        out.append(piece)
        if step + 1 < count:
            value = value - piece.astype(F32)
    return out


def dot_left(value, right, dims, count=PASSES):
    return sum(dot(piece, right, dims) for piece in parts(value, count))


def dot_right(left, value, dims, count=PASSES):
    return sum(dot(left, piece, dims) for piece in parts(value, count))


def elu_pair(value):
    slope = jnp.exp(jnp.minimum(value, 0.0))
    return jnp.maximum(value, 0.0) + (slope - 1.0), slope


def iota(shape, axis):
    return lax.broadcasted_iota(jnp.int32, shape, axis)


def stack_maps(map_ref, stacked):
    views, channels, pixels = map_ref.shape
    blocks = pixels // 256
    for view in range(views):
        for block in range(0, blocks, 2):
            strips = []
            for part in range(block, min(block + 2, blocks)):
                strips.append(map_ref[view, :, 256 * part : 256 * (part + 1)].astype(F32))
                strips.append(jnp.zeros((BAND - channels, 256), F32))
            strips = jnp.concatenate(strips, axis=0)
            stacked[view, BAND * block : BAND * block + strips.shape[0], :] = strips.astype(BF16)


def gather_kernel(views, tile, count, *refs):
    packed_refs, source = refs[1 : 1 + count], refs[1 + count]
    outs, stacked = refs[2 + count : -1], refs[-1]
    blocks = stacked.shape[1] // BAND

    @pl.when(pl.program_id(0) == 0)
    def _():
        stack_maps(source, stacked)

    row = iota((8, tile), 0) + 8 * (CHANNELS // 8)
    for packed_ref, out_ref in zip(packed_refs, outs):
        strips = []
        for view in range(views):
            packed = packed_ref[view : view + 1, :]
            index = packed & (SEEN_BIT - 1)
            high = jnp.broadcast_to(index >> 8, (8, tile))
            low = jnp.broadcast_to(index & 255, (256, tile))
            picked = (iota((256, tile), 0) == low).astype(F32).astype(BF16)
            found = dot(stacked[view], picked)
            totals = [jnp.zeros((8, tile), F32)] * (STRIP // 8)
            for block in range(blocks):
                here = high == block
                for part in range(STRIP // 8):
                    at = BAND * block + 8 * part
                    totals[part] = jnp.where(here, found[at : at + 8], totals[part])
            seen = jnp.broadcast_to((packed >> SEEN_SHIFT).astype(F32), (8, tile))
            last = jnp.where(row == CHANNELS, 1.0, totals[-1])
            last = jnp.where(row == CHANNELS + 1, seen, last)
            totals[-1] = jnp.where(row > CHANNELS + 1, 0.0, last)
            strips += totals
        out_ref[0] = jnp.concatenate(strips, axis=0).astype(BF16)


def gather_rows(packed, source, me, group, ways):
    views, points = packed.shape
    tile = GATHER_TILE
    own = points // group
    tiles = own // tile
    count = len(ways)
    part = lambda k: pl.BlockSpec((views, tile), lambda t, me: (0, (me[0] ^ k) * tiles + t))
    whole = lambda shape: pl.BlockSpec(shape, lambda t, me: (0, 0, 0))
    outs = [jax.ShapeDtypeStruct((1, views * STRIP, own), BF16)] * count
    out_specs = [pl.BlockSpec((1, views * STRIP, tile), lambda t, me: (0, 0, t))] * count
    table = (views, BAND * (source.shape[2] // 256), 256)
    flops = 2 * views * own * count * table[1] * 256
    return pl.pallas_call(
        lambda *refs: gather_kernel(views, tile, count, *refs),
        out_shape=outs,
        grid_spec=pltpu.PrefetchScalarGridSpec(
            num_scalar_prefetch=1,
            grid=(tiles,),
            in_specs=[part(k) for k in ways] + [whole(source.shape)],
            out_specs=out_specs,
            scratch_shapes=[pltpu.VMEM(table, BF16)],
        ),
        compiler_params=pltpu.CompilerParams(vmem_limit_bytes=32 * 1024 * 1024),
        cost_estimate=pl.CostEstimate(
            flops=flops, bytes_accessed=source.size * 2, transcendentals=0
        ),
    )(me, *([packed] * count), source)


def roll(value, shift):
    return pltpu.roll(value, shift % 128, 1)


def unpack(a_ref, r64, r32, r16):
    for b in range(2):
        r64[pl.ds(b, 18, stride=2), :] = roll(a_ref[0:18, :], -64 * b)
    for b in range(4):
        r32[pl.ds(b, 33, stride=4), :] = roll(a_ref[18:51, :], -32 * b)
    for b in range(8):
        r16[pl.ds(b, 39, stride=8), :] = roll(a_ref[50:89, :], -16 * b)


def assemble(place, shard, shard_refs, a_ref):
    a_ref[...] = jnp.zeros_like(a_ref)
    shards, rows, _ = shard_refs.shape
    for k in range(shards):
        start = (place ^ k) * shard
        shift = start & 127
        value = pltpu.roll(shard_refs[k].astype(F32), shift, 1)
        keep = iota((rows, 128), 1) >= shift
        first = start >> 7
        a_ref[pl.ds(first, rows), :] += jnp.where(keep, value, 0.0)
        a_ref[pl.ds(first + 1, rows), :] += jnp.where(keep, 0.0, value)


def column(rows):
    return rows.T[:, 0:1]


def main_kernel(views, shard, me_ref, *refs):
    shard_refs, refs = refs[0], refs[1:]
    (
    x0,
    x1,
    x2,
    x3,
    delta_ref,
    target_ref,
    weight_ref,
    out_ref,
    a_ref,
    r64,
    r32,
    r16,
    xs,
    hb,
    he,
    ff,
    fe,
    jb,
    ib,
    ie,
    ee,
    blk,
    _,
    _,
    tri_s,
    g64,
    g32,
    g16,
    gw1,
    gb2,
    gc1,
    gc2,
    gd1,
    gs2,
    gdd,
    loss_s,
    ) = refs
    step = pl.program_id(0)
    n = CHUNK
    lane = iota((1, n), 1)
    first_ray = lane < RAY
    me = me_ref[0]

    @pl.when(step == 0)
    def _():
        assemble(me_ref[1], shard, shard_refs, a_ref)
        unpack(a_ref, r64, r32, r16)
        for ref in (g64, g32, g16, gw1, gb2, gc1, gc2, gd1, gs2, gdd, loss_s):
            ref[...] = jnp.zeros_like(ref)
        before = (iota((n, n), 0) < iota((n, n), 1)) & (
            (iota((n, n), 0) < RAY) == (iota((n, n), 1) < RAY)
        )
        tri_s[...] = before.astype(F32).astype(BF16)
        w1t = jnp.where(iota((64, 128), 1) < 36, 1.0, 0.0) * jnp.concatenate(
            [r64[0:36, :], jnp.zeros((92, 128), F32)], axis=0
        ).T[:64]
        for view in range(views):
            blk[64 * view : 64 * (view + 1), :] = roll(w1t, STRIP * view).astype(BF16)

    for k, ref in enumerate((x0, x1, x2, x3)):
        xs[me ^ k] = ref[0]

    w2 = r32[0:64, :][:, :32]
    w2b = w2.astype(BF16)
    w2t = w2.T.astype(BF16)
    b2 = column(r32[64:72, :])[:32]
    u1 = r32[65:129, :][:, :32]
    u1b = u1.astype(BF16)
    u1at = u1[:32].T.astype(BF16)
    u1bt = u1[32:].T.astype(BF16)
    c1 = column(r32[129:137, :])[:32]
    u2 = r16[4:36, :][:, :16]
    u2b = u2.astype(BF16)
    u2t = u2.T.astype(BF16)
    c2 = column(r16[36:44, :])[:16]
    keep16 = iota((48, 128), 1) < 16
    qkv = sum(
        roll(jnp.where(keep16, r16[pl.ds(37 + a, 48, stride=4), :], 0.0), 16 * a) for a in range(4)
    )
    wq, wk, wv = qkv[0:16], qkv[16:32], qkv[32:48]
    wqb = wq[:, :64].astype(BF16)
    wqt = wq[:, :64].T.astype(BF16)
    wk_of = [roll(wk, 64 * r).astype(BF16) for r in range(2)]
    wv_of = [roll(wv, 64 * r).astype(BF16) for r in range(2)]
    wo = r16[229:293, :][:, :16]
    wob = wo.astype(BF16)
    wot = wo.T.astype(BF16)
    s1 = r16[293:309, :][:, :16]
    s1b = s1.astype(BF16)
    s1t = s1.T.astype(BF16)
    d1 = column(r16[309:317, :])[:16]
    s2 = column(r16[310:318, :])[:16]
    d2 = r16[311:312, 0:1]

    def seen_of(view):
        at = STRIP * (view % views)
        return xs[view // views, at : at + STRIP, :].astype(F32)

    sum1 = jnp.zeros((32, n), F32)
    sum2 = jnp.zeros((32, n), F32)
    seen = jnp.zeros((1, n), F32)
    for group in range(-(-SEEN_VIEWS // views)):
        count = min(views, SEEN_VIEWS - group * views)
        pre = dot(blk[0 : 64 * count, 0 : views * STRIP], xs[group])
        for local in range(count):
            view = group * views + local
            value, slope = elu_pair(pre[64 * local : 64 * (local + 1)])
            hidden = value.astype(BF16)
            hb[view] = hidden
            he[view] = slope
            value, slope = elu_pair(dot(w2t, hidden) + b2)
            ff[view] = value
            fe[view] = slope
            vis = seen_of(view)[CHANNELS + 1 : CHANNELS + 2]
            part = vis * value
            sum1 = sum1 + part
            sum2 = sum2 + part * value
            seen = seen + vis
    average = sum1 / seen
    variance = sum2 / seen - average * average
    variance_low = variance.astype(BF16)
    shared = dot(u1bt, variance_low) + c1
    num = jnp.zeros((16, n), F32)
    den = jnp.zeros((16, n), F32)
    col = jnp.zeros((3, n), F32)
    for view in range(SEEN_VIEWS):
        strip = seen_of(view)
        feature = ff[view]
        joined = (feature - average).astype(BF16)
        jb[view] = joined
        value, slope = elu_pair(dot(u1at, joined) + shared)
        inner = value.astype(BF16)
        ib[view] = inner
        ie[view] = slope
        e = strip[CHANNELS + 1 : CHANNELS + 2] * jnp.exp(dot(u2t, inner) + c2)
        ee[view] = e
        num = num + e * feature[:16]
        den = den + e
        col = col + e[0:1] * strip[32:35]

    inv = 1.0 / den
    tokens = num / den
    colour = col / den[0:1]
    token_low = tokens.astype(BF16)
    token_t = tokens.T.astype(BF16)
    halves = [token_t[RAY * r : RAY * (r + 1)] for r in range(2)]
    query = dot(wqt, token_low).astype(BF16)
    kk_f = dot(halves[0], wk_of[0]) + dot(halves[1], wk_of[1])
    vv_f = dot(halves[0], wv_of[0]) + dot(halves[1], wv_of[1])
    kk = kk_f.astype(BF16)
    vv = vv_f.astype(BF16)
    kkt = kk.astype(F32).T.astype(BF16)
    vvt = vv.astype(F32).T.astype(BF16)
    row64 = iota((64, n), 0)

    def spread(value, head):
        mine = jnp.where((row64 >> 4) == head, value.astype(F32), 0.0)
        one = jnp.where(first_ray, mine, 0.0)
        return jnp.concatenate([one, mine - one], axis=0)

    def fold(value):
        return jnp.where(first_ray, value[:16], value[16:])

    def head_rows(value, head):
        at = 16 * head
        return jnp.concatenate([value[at : at + 16], value[64 + at : 80 + at]], axis=0)

    probs = []
    attended = []
    query_of = []
    for head in range(4):
        q_head = spread(query, head).astype(BF16)
        query_of.append(q_head)
        score = dot(kk, q_head) * 0.25
        score = jnp.exp(score - jnp.max(score, axis=0, keepdims=True))
        prob = score / jnp.sum(score, axis=0, keepdims=True)
        probs.append(prob)
        attended.append(fold(dot(head_rows(vvt, head), prob.astype(BF16))))
    attended = jnp.concatenate(attended, axis=0).astype(BF16)
    mixed = tokens + dot(wot, attended)
    mixed_low = mixed.astype(BF16)
    value, s_slope = elu_pair(dot(s1t, mixed_low) + d1)
    act = value.astype(BF16).astype(F32)
    z = jnp.sum(act * s2, axis=0, keepdims=True) + d2
    delta = delta_ref[0]
    ez = jnp.exp(-jnp.abs(z))
    density = jnp.maximum(z, 0.0) + jnp.log1p(ez)
    sigmoid = jnp.where(z >= 0.0, 1.0, ez) / (1.0 + ez)
    optical = density * delta
    tri = tri_s[...]

    def exact_rows(value):
        pad = jnp.zeros((13, n), F32)
        return jnp.concatenate([p.astype(F32) for p in parts(value, 3)] + [pad], axis=0).astype(BF16)

    before = jnp.sum(dot(exact_rows(optical), tri), axis=0, keepdims=True)
    through = jnp.exp(-before)
    gone = jnp.exp(-optical)
    render = through * (1.0 - gone)
    drawn = render * colour
    targets = target_ref[0]
    rweight = weight_ref[0]
    d_pixel = jnp.zeros((3, n), F32)
    loss = jnp.zeros((1, 1), F32)
    for r in range(2):
        mask = first_ray if r == 0 else jnp.logical_not(first_ray)
        pixel = jnp.sum(jnp.where(mask, drawn, 0.0), axis=1, keepdims=True)
        miss = pixel - targets[0:3, r : r + 1]
        scale = rweight[0:1, r : r + 1]
        loss = loss + scale * jnp.sum(miss * miss, axis=0, keepdims=True)
        d_pixel = d_pixel + jnp.where(mask, 2.0 * scale * miss, 0.0)
    place = iota((8, 128), 1) + 128 * iota((8, 128), 0)
    loss_s[...] += jnp.where(place == 0, loss, 0.0) + jnp.where(
        place == 1, rweight[0:1, 0:1] + rweight[0:1, 1:2], 0.0
    )

    d_render = jnp.sum(d_pixel * colour, axis=0, keepdims=True)
    d_colour = d_pixel * render
    d_before = -render * d_render
    d_optical = through * gone * d_render + jnp.sum(
        dot(exact_rows(d_before), tri, NT), axis=0, keepdims=True
    )
    dz = d_optical * delta * sigmoid
    gs2[...] += act * dz
    gdd[...] += jnp.where(iota((8, n), 0) == 0, dz, 0.0)
    d_pre = s2 * dz * s_slope
    gd1[...] += d_pre
    g16[293:309, :] += widen(dot_right(mixed_low, d_pre, NT))
    d_mixed = dot_right(s1b, d_pre, NN)
    g16[229:293, :] += widen(dot_right(attended, d_mixed, NT))
    d_att = dot_right(wob, d_mixed, NN)
    d_query = []
    d_kk = jnp.zeros((RAY, 128), F32)
    d_vv = jnp.zeros((RAY, 128), F32)
    for head in range(4):
        prob = probs[head]
        d_head = parts(spread(d_att, head), PASSES)
        d_prob = sum(dot(vv, piece) for piece in d_head)
        low = prob.astype(BF16)
        d_vv = d_vv + sum(dot(low, piece, NT) for piece in d_head)
        d_score = prob * (d_prob - jnp.sum(prob * d_prob, axis=0, keepdims=True)) * 0.25
        pieces = parts(d_score, PASSES)
        d_query.append(fold(sum(dot(head_rows(kkt, head), piece) for piece in pieces)))
        d_kk = d_kk + sum(dot(piece, query_of[head], NT) for piece in pieces)
    d_query = jnp.concatenate(d_query, axis=0)
    gq = dot_right(token_low, d_query, NT)
    gk = [dot_right(halves[r], d_kk, TN) for r in range(2)]
    gv = [dot_right(halves[r], d_vv, TN) for r in range(2)]
    wide = jnp.concatenate([widen(gq), gk[0] + roll(gk[1], 64), gv[0] + roll(gv[1], 64)], axis=0)
    for a in range(4):
        at = pl.ds(37 + a, 48, stride=4)
        g16[at, :] += jnp.where(keep16, roll(wide, -16 * a), 0.0)
    d_halves = [
        dot_left(d_kk, wk_of[r], NT) + dot_left(d_vv, wv_of[r], NT) for r in range(2)
    ]
    d_tokens = d_mixed + dot_right(wqb, d_query, NN) + jnp.concatenate(d_halves, axis=0).T
    d_num = d_tokens * inv
    d_den = -d_num * tokens
    d_col = d_colour * inv[0:1]
    d_den0 = -jnp.sum(d_col * colour, axis=0, keepdims=True)
    row16 = iota((16, n), 0)
    d_den = d_den + jnp.where(row16 == 0, d_den0, 0.0)

    d_average = jnp.zeros((32, n), F32)
    d_shared = jnp.zeros((32, n), F32)
    sum_c2 = jnp.zeros((16, n), F32)
    grad_u2 = jnp.zeros((32, 16), F32)
    grad_u1 = jnp.zeros((32, 32), F32)
    for view in range(SEEN_VIEWS):
        strip = seen_of(view)
        e = ee[view]
        feature = ff[view]
        d_e = d_num * feature[:16] + d_den
        d_e = d_e + jnp.where(
            row16 == 0, jnp.sum(d_col * strip[32:35], axis=0, keepdims=True), 0.0
        )
        d_logit = d_e * e
        sum_c2 = sum_c2 + d_logit
        pieces = parts(d_logit, PASSES)
        grad_u2 = grad_u2 + sum(dot(ib[view], piece, NT) for piece in pieces)
        d_inner = sum(dot(u2b, piece) for piece in pieces) * ie[view]
        d_shared = d_shared + d_inner
        pieces = parts(d_inner, PASSES)
        grad_u1 = grad_u1 + sum(dot(jb[view], piece, NT) for piece in pieces)
        d_joined = sum(dot(u1b[:32], piece) for piece in pieces)
        d_average = d_average - d_joined
        ee[view] = d_num * e
        ie[view] = d_joined
    pieces = parts(d_shared, PASSES)
    d_variance = sum(dot(u1b[32:], piece) for piece in pieces)
    g16[4:36, :] += widen(grad_u2)
    g32[65:97, :] += widen(grad_u1)
    g32[97:129, :] += widen(sum(dot(variance_low, piece, NT) for piece in pieces))
    gc1[...] += d_shared
    gc2[...] += sum_c2
    inv_seen = 1.0 / seen
    d_square = d_variance * inv_seen
    d_sum = (d_average - 2.0 * average * d_variance) * inv_seen

    grad_w2 = jnp.zeros((64, 32), F32)
    sum_b2 = jnp.zeros((32, n), F32)
    for group in range(-(-SEEN_VIEWS // views)):
        count = min(views, SEEN_VIEWS - group * views)
        d_hidden = []
        for local in range(count):
            view = group * views + local
            vis = seen_of(view)[CHANNELS + 1 : CHANNELS + 2]
            d_feature = ie[view] + vis * (d_sum + 2.0 * ff[view] * d_square)
            d_feature = d_feature + jnp.concatenate([ee[view], jnp.zeros((16, n), F32)], axis=0)
            d_feature = d_feature * fe[view]
            sum_b2 = sum_b2 + d_feature
            pieces = parts(d_feature, PASSES)
            grad_w2 = grad_w2 + sum(dot(hb[view], piece, NT) for piece in pieces)
            d_hidden.append(sum(dot(w2b, piece) for piece in pieces) * he[view])
        d_hidden = jnp.concatenate(d_hidden, axis=0)
        gw1[:, 0 : 64 * count] += dot_right(xs[group], d_hidden, NT)
    g32[0:64, :] += widen(grad_w2)
    gb2[...] += sum_b2

    @pl.when(step == pl.num_programs(0) - 1)
    def _():
        ones = jnp.ones((8, n), BF16)
        row_of = lambda ref: widen(dot_right(ones, ref[...], NT, 3)[0:1])
        g32[64:65, :] = row_of(gb2)
        g32[129:130, :] = row_of(gc1)
        g16[36:37, :] = row_of(gc2)
        g16[309:310, :] = row_of(gd1)
        g16[310:311, :] = row_of(gs2)
        g16[311:312, :] = jnp.where(iota((1, 128), 1) == 0, row_of(gdd), 0.0)
        total = gw1[0:36, 0:128]
        total = total + roll(gw1[STRIP : STRIP + 36, 0:128], 64)
        total = total + gw1[2 * STRIP : 2 * STRIP + 36, 128:256]
        g64[0:36, :] = jnp.where(iota((36, 128), 1) < 64, total, 0.0)
        out_ref[...] = jnp.zeros_like(out_ref)
        out_ref[0:18, :] = sum(roll(g64[pl.ds(b, 18, stride=2), :], 64 * b) for b in range(2))
        out_ref[18:51, :] += sum(roll(g32[pl.ds(b, 33, stride=4), :], 32 * b) for b in range(4))
        out_ref[50:89, :] += sum(roll(g16[pl.ds(b, 39, stride=8), :], 16 * b) for b in range(8))
        out_ref[96:104, :] = loss_s[...]


def widen(value):
    rows, width = value.shape
    return jnp.concatenate([value, jnp.zeros((rows, 128 - width), F32)], axis=1)


def run_main(me, blocks, pieces, shard, deltas, targets, ray_weight):
    rows, points = blocks[0].shape[1:]
    views = rows // STRIP
    n = CHUNK
    steps = points // n
    v = SEEN_VIEWS
    whole = deltas.shape[0] // 2
    pairs = deltas.reshape(whole, 1, n)
    target_pairs = jnp.pad(
        targets.reshape(whole, 2, 3).transpose(0, 2, 1), ((0, 0), (0, 5), (0, 126))
    )
    weight_pairs = jnp.pad(ray_weight.reshape(whole, 1, 2), ((0, 0), (0, 7), (0, 126)))
    vm = pltpu.VMEM
    own = lambda t, me: (me[0] * steps + t, 0, 0)
    block = pl.BlockSpec((1, rows, n), lambda t, me: (0, 0, t))
    piece = pl.BlockSpec(pieces.shape, lambda t, me: (0, 0, 0))
    return pl.pallas_call(
        lambda *refs: main_kernel(views, shard, *refs),
        out_shape=jax.ShapeDtypeStruct((104, 128), F32),
        grid_spec=pltpu.PrefetchScalarGridSpec(
            num_scalar_prefetch=1,
            grid=(steps,),
            in_specs=[piece]
            + [block] * 4
            + [
                pl.BlockSpec((1, 1, n), own),
                pl.BlockSpec((1, 8, 128), own),
                pl.BlockSpec((1, 8, 128), own),
            ],
            out_specs=pl.BlockSpec((104, 128), lambda t, me: (0, 0)),
            scratch_shapes=[
                vm((120, 128), F32),
                vm((40, 128), F32),
                vm((144, 128), F32),
                vm((320, 128), F32),
                vm((4, rows, n), BF16),
                vm((v, 64, n), BF16),
                vm((v, 64, n), F32),
                vm((v, 32, n), F32),
                vm((v, 32, n), F32),
                vm((v, 32, n), BF16),
                vm((v, 32, n), BF16),
                vm((v, 32, n), F32),
                vm((v, 16, n), F32),
                vm((64 * views, 128), BF16),
                vm((8, 128), BF16),
                vm((8, 128), BF16),
                vm((n, n), BF16),
                vm((40, 128), F32),
                vm((136, 128), F32),
                vm((312, 128), F32),
                vm((rows, 256), F32),
                vm((32, n), F32),
                vm((32, n), F32),
                vm((16, n), F32),
                vm((16, n), F32),
                vm((16, n), F32),
                vm((8, n), F32),
                vm((8, 128), F32),
            ],
        ),
        compiler_params=pltpu.CompilerParams(vmem_limit_bytes=48 * 1024 * 1024),
    )(me, pieces, *blocks, pairs, target_pairs, weight_pairs)


def adamw(master, first_moment, second_moment, gradient, step_count):
    step_float = step_count[0].astype(F32)
    first_new = MOMENT_DECAY * first_moment + (1.0 - MOMENT_DECAY) * gradient
    second_new = SQUARE_DECAY * second_moment + (1.0 - SQUARE_DECAY) * gradient * gradient
    first_fix = 1.0 - jnp.power(MOMENT_DECAY, step_float)
    second_fix = 1.0 - jnp.power(SQUARE_DECAY, step_float)
    update = first_new / first_fix / (jnp.sqrt(second_new / second_fix) + EPSILON)
    master_new = master - LEARNING_RATE * (update + WEIGHT_DECAY * master)
    return (master_new, first_new, second_new)


def body(
    master,
    first_moment,
    second_moment,
    step_count,
    feature_maps,
    pixel_index,
    visible,
    deltas,
    targets,
    scene_id,
    scene_weight,
):
    group = lax.axis_size("views")
    shards = lax.axis_size("rays")
    assert feature_maps.shape[2] <= SEEN_BIT
    shard = master.shape[0]
    spots = [lax.axis_index("views"), lax.axis_index("rays")]
    me = jnp.stack(spots).astype(jnp.int32)
    swap = lambda size, k: [(i, i ^ k) for i in range(size)]
    rows = -(-shard // 2048) * 16
    piece = jnp.pad(master.astype(BF16), (0, rows * 128 - shard)).reshape(rows, 128)
    packed = pixel_index.T + (visible.T << SEEN_SHIFT)
    held = piece[None]
    links = shards.bit_length() - 1
    for link in range(links):
        held = jnp.concatenate([held, lax.ppermute(held, "rays", swap(shards, 1 << link))])
    far = gather_rows(packed, feature_maps, me, group, (3, 2))
    three = lax.ppermute(far[0], "views", swap(group, 3))
    two = lax.ppermute(far[1], "views", swap(group, 2))
    near = gather_rows(packed, feature_maps, me, group, (1,))
    one = lax.ppermute(near[0], "views", swap(group, 1))
    mine = gather_rows(packed, feature_maps, me, group, (0,))
    hits = (scene_id[:, None] == jnp.arange(scene_weight.shape[0])[None, :]).astype(F32)
    ray_weight = jnp.sum(hits * scene_weight.astype(F32)[None, :], axis=1)
    result = run_main(me, [mine[0], one, two, three], held, shard, deltas, targets, ray_weight)
    summed = result[:89].reshape(-1)
    size = shards * shard
    if summed.shape[0] < size:
        summed = jnp.pad(summed, (0, size - summed.shape[0]))
    extra = jnp.broadcast_to(result[96, :2][None], (shards, 2))
    send = jnp.concatenate([summed[:size].reshape(shards, shard), extra], axis=1)
    got = lax.all_to_all(send, "rays", 0, 0, tiled=True)
    partial = jnp.sum(got, axis=0)
    whole = partial
    for k in range(1, group):
        whole = whole + lax.ppermute(partial, "views", [(i, i ^ k) for i in range(group)])
    seed = 1.0 / whole[shard + 1]
    loss = whole[shard] * seed
    gradient = whole[:shard] * seed
    return (loss, *adamw(master, first_moment, second_moment, gradient, step_count))


def solution(mesh):
    placed = (
        P("rays"),
        P("rays"),
        P("rays"),
        P(),
        P("views", None, None),
        P("rays", "views"),
        P("rays", "views"),
        P("rays", None),
        P("rays", None),
        P("rays"),
        P(),
    )
    return jax.shard_map(
        body,
        mesh=mesh,
        in_specs=placed,
        out_specs=(P(), P("rays"), P("rays"), P("rays")),
        check_vma=False,
    )
```

```python
import jax
import jax.numpy as jnp
from jax import lax
from jax.experimental import pallas as pl
from jax.experimental.pallas import tpu as pltpu
from jax.sharding import PartitionSpec as P


F32 = jnp.float32
BF16 = jnp.bfloat16
SEEN_VIEWS = 10
CHANNELS = 35
STRIP = 40
BAND = 40
SEEN_SHIFT = 14
SEEN_BIT = 1 << SEEN_SHIFT
GATHER_TILE = 256
RAY = 192
CHUNK = 2 * RAY
PASSES = 1
MOMENT_DECAY = 0.5
SQUARE_DECAY = 0.5
LEARNING_RATE = 0.05
WEIGHT_DECAY = 0.01
EPSILON = 1e-08
NN = (((1,), (0,)), ((), ()))
NT = (((1,), (1,)), ((), ()))
TN = (((0,), (0,)), ((), ()))


def dot(left, right, dims=NN):
    return lax.dot_general(left, right, dims, preferred_element_type=F32)


def parts(value, count):
    out = []
    for step in range(count):
        piece = value.astype(BF16)
        out.append(piece)
        if step + 1 < count:
            value = value - piece.astype(F32)
    return out


def dot_left(value, right, dims, count=PASSES):
    return sum(dot(piece, right, dims) for piece in parts(value, count))


def dot_right(left, value, dims, count=PASSES):
    return sum(dot(left, piece, dims) for piece in parts(value, count))


def elu_pair(value):
    slope = jnp.exp(jnp.minimum(value, 0.0))
    return jnp.maximum(value, 0.0) + (slope - 1.0), slope


def iota(shape, axis):
    return lax.broadcasted_iota(jnp.int32, shape, axis)


def stack_maps(map_ref, stacked):
    views, channels, pixels = map_ref.shape
    blocks = pixels // 256
    for view in range(views):
        for block in range(0, blocks, 2):
            strips = []
            for part in range(block, min(block + 2, blocks)):
                strips.append(map_ref[view, :, 256 * part : 256 * (part + 1)].astype(F32))
                strips.append(jnp.zeros((BAND - channels, 256), F32))
            strips = jnp.concatenate(strips, axis=0)
            stacked[view, BAND * block : BAND * block + strips.shape[0], :] = strips.astype(BF16)


def gather_kernel(views, tile, count, *refs):
    packed_refs, source = refs[1 : 1 + count], refs[1 + count]
    outs, stacked = refs[2 + count : -1], refs[-1]
    blocks = stacked.shape[1] // BAND

    @pl.when(pl.program_id(0) == 0)
    def _():
        stack_maps(source, stacked)

    row = iota((8, tile), 0) + 8 * (CHANNELS // 8)
    for packed_ref, out_ref in zip(packed_refs, outs):
        strips = []
        for view in range(views):
            packed = packed_ref[view : view + 1, :]
            index = packed & (SEEN_BIT - 1)
            high = jnp.broadcast_to(index >> 8, (8, tile))
            low = jnp.broadcast_to(index & 255, (256, tile))
            picked = (iota((256, tile), 0) == low).astype(F32).astype(BF16)
            found = dot(stacked[view], picked)
            totals = [jnp.zeros((8, tile), F32)] * (STRIP // 8)
            for block in range(blocks):
                here = high == block
                for part in range(STRIP // 8):
                    at = BAND * block + 8 * part
                    totals[part] = jnp.where(here, found[at : at + 8], totals[part])
            seen = jnp.broadcast_to((packed >> SEEN_SHIFT).astype(F32), (8, tile))
            last = jnp.where(row == CHANNELS, 1.0, totals[-1])
            last = jnp.where(row == CHANNELS + 1, seen, last)
            totals[-1] = jnp.where(row > CHANNELS + 1, 0.0, last)
            strips += totals
        out_ref[0] = jnp.concatenate(strips, axis=0).astype(BF16)


def gather_rows(packed, source, me, group, ways):
    views, points = packed.shape
    tile = GATHER_TILE
    own = points // group
    tiles = own // tile
    count = len(ways)
    part = lambda k: pl.BlockSpec((views, tile), lambda t, me: (0, (me[0] ^ k) * tiles + t))
    whole = lambda shape: pl.BlockSpec(shape, lambda t, me: (0, 0, 0))
    outs = [jax.ShapeDtypeStruct((1, views * STRIP, own), BF16)] * count
    out_specs = [pl.BlockSpec((1, views * STRIP, tile), lambda t, me: (0, 0, t))] * count
    table = (views, BAND * (source.shape[2] // 256), 256)
    flops = 2 * views * own * count * table[1] * 256
    return pl.pallas_call(
        lambda *refs: gather_kernel(views, tile, count, *refs),
        out_shape=outs,
        grid_spec=pltpu.PrefetchScalarGridSpec(
            num_scalar_prefetch=1,
            grid=(tiles,),
            in_specs=[part(k) for k in ways] + [whole(source.shape)],
            out_specs=out_specs,
            scratch_shapes=[pltpu.VMEM(table, BF16)],
        ),
        compiler_params=pltpu.CompilerParams(vmem_limit_bytes=32 * 1024 * 1024),
        cost_estimate=pl.CostEstimate(
            flops=flops, bytes_accessed=source.size * 2, transcendentals=0
        ),
    )(me, *([packed] * count), source)


def roll(value, shift):
    return pltpu.roll(value, shift % 128, 1)


def unpack(a_ref, r64, r32, r16):
    for b in range(2):
        r64[pl.ds(b, 18, stride=2), :] = roll(a_ref[0:18, :], -64 * b)
    for b in range(4):
        r32[pl.ds(b, 33, stride=4), :] = roll(a_ref[18:51, :], -32 * b)
    for b in range(8):
        r16[pl.ds(b, 39, stride=8), :] = roll(a_ref[50:89, :], -16 * b)


def assemble(place, shard, shard_refs, a_ref):
    a_ref[...] = jnp.zeros_like(a_ref)
    shards, rows, _ = shard_refs.shape
    for k in range(shards):
        start = (place ^ k) * shard
        shift = start & 127
        value = pltpu.roll(shard_refs[k].astype(F32), shift, 1)
        keep = iota((rows, 128), 1) >= shift
        first = start >> 7
        a_ref[pl.ds(first, rows), :] += jnp.where(keep, value, 0.0)
        a_ref[pl.ds(first + 1, rows), :] += jnp.where(keep, 0.0, value)


def repeat(weight, out_ref, times):
    out_ref[...] = jnp.zeros_like(out_ref)
    rows, width = weight.shape
    wide = widen(weight)
    for part in range(times):
        tile, shift = divmod(width * part, 128)
        out_ref[rows * part : rows * (part + 1), 128 * tile : 128 * (tile + 1)] = roll(
            wide, shift
        ).astype(BF16)


def blocks_sum(ref, rows, width, times):
    total = sum(
        roll(ref[rows * part : rows * (part + 1), :], -width * part) for part in range(times)
    )
    return jnp.where(iota((rows, 128), 1) < width, total, 0.0)


def column(rows):
    return rows.T[:, 0:1]


def main_kernel(views, shard, me_ref, *refs):
    shard_refs, refs = refs[0], refs[1:]
    (
    x0,
    x1,
    x2,
    x3,
    delta_ref,
    target_ref,
    weight_ref,
    out_ref,
    a_ref,
    r64,
    r32,
    r16,
    xs,
    hb,
    he,
    ff,
    fe,
    jb,
    ib,
    ie,
    ee,
    blk,
    w2t_s,
    w2_s,
    u1t_s,
    u1_s,
    u2t_s,
    u2_s,
    tri_s,
    g64,
    g32,
    g16,
    gw1,
    gw2,
    gu1,
    gu2,
    gb2,
    gc1,
    gc2,
    gd1,
    gs2,
    gdd,
    loss_s,
    ) = refs
    step = pl.program_id(0)
    n = CHUNK
    lane = iota((1, n), 1)
    first_ray = lane < RAY
    me = me_ref[0]

    @pl.when(step == 0)
    def _():
        assemble(me_ref[1], shard, shard_refs, a_ref)
        unpack(a_ref, r64, r32, r16)
        for ref in (g64, g32, g16, gw1, gw2, gu1, gu2, gb2, gc1, gc2, gd1, gs2, gdd, loss_s):
            ref[...] = jnp.zeros_like(ref)
        before = (iota((n, n), 0) < iota((n, n), 1)) & (
            (iota((n, n), 0) < RAY) == (iota((n, n), 1) < RAY)
        )
        tri_s[...] = before.astype(F32).astype(BF16)
        w1t = jnp.where(iota((64, 128), 1) < 36, 1.0, 0.0) * jnp.concatenate(
            [r64[0:36, :], jnp.zeros((92, 128), F32)], axis=0
        ).T[:64]
        for view in range(views):
            blk[64 * view : 64 * (view + 1), :] = roll(w1t, STRIP * view).astype(BF16)
        w2 = r32[0:64, :][:, :32]
        u1a = r32[65:97, :][:, :32]
        u2 = r16[4:36, :][:, :16]
        repeat(w2.T, w2t_s, views)
        repeat(w2, w2_s, views)
        repeat(u1a.T, u1t_s, views)
        repeat(u1a, u1_s, views)
        repeat(u2.T, u2t_s, views)
        repeat(u2, u2_s, views)

    for k, ref in enumerate((x0, x1, x2, x3)):
        xs[me ^ k] = ref[0]

    b2 = column(r32[64:72, :])[:32]
    u1b = r32[97:129, :][:, :32]
    u1bt = u1b.T.astype(BF16)
    u1b = u1b.astype(BF16)
    c1 = column(r32[129:137, :])[:32]
    c2 = column(r16[36:44, :])[:16]
    keep16 = iota((48, 128), 1) < 16
    qkv = sum(
        roll(jnp.where(keep16, r16[pl.ds(37 + a, 48, stride=4), :], 0.0), 16 * a) for a in range(4)
    )
    wq, wk, wv = qkv[0:16], qkv[16:32], qkv[32:48]
    wqb = wq[:, :64].astype(BF16)
    wqt = wq[:, :64].T.astype(BF16)
    wk_of = [roll(wk, 64 * r).astype(BF16) for r in range(2)]
    wv_of = [roll(wv, 64 * r).astype(BF16) for r in range(2)]
    wo = r16[229:293, :][:, :16]
    wob = wo.astype(BF16)
    wot = wo.T.astype(BF16)
    s1 = r16[293:309, :][:, :16]
    s1b = s1.astype(BF16)
    s1t = s1.T.astype(BF16)
    d1 = column(r16[309:317, :])[:16]
    s2 = column(r16[310:318, :])[:16]
    d2 = r16[311:312, 0:1]

    def strip_of(group, local):
        at = STRIP * local + 32
        strip = xs[group, at : at + 8, :].astype(F32)
        return strip[0:3], strip[4:5]

    def stack(values):
        return jnp.concatenate(values, axis=0) if len(values) > 1 else values[0]

    def cut(value, rows, local):
        return value[rows * local : rows * (local + 1)]

    counts = [min(views, SEEN_VIEWS - at) for at in range(0, SEEN_VIEWS, views)]

    sum1 = jnp.zeros((32, n), F32)
    sum2 = jnp.zeros((32, n), F32)
    seen = jnp.zeros((1, n), F32)
    for group, count in enumerate(counts):
        wide, thin = 64 * count, 32 * count
        value, slope = elu_pair(dot(blk[0:wide, 0 : views * STRIP], xs[group]))
        hidden = value.astype(BF16)
        hb[group, 0:wide] = hidden
        he[group, 0:wide] = slope
        value, slope = elu_pair(dot(w2t_s[0:thin, 0:wide], hidden) + stack([b2] * count))
        ff[group, 0:thin] = value
        fe[group, 0:thin] = slope
        for local in range(count):
            vis = strip_of(group, local)[1]
            one = cut(value, 32, local)
            part = vis * one
            sum1 = sum1 + part
            sum2 = sum2 + part * one
            seen = seen + vis
    average = sum1 / seen
    variance = sum2 / seen - average * average
    variance_low = variance.astype(BF16)
    shared = dot(u1bt, variance_low) + c1
    num = jnp.zeros((16, n), F32)
    den = jnp.zeros((16, n), F32)
    col = jnp.zeros((3, n), F32)
    for group, count in enumerate(counts):
        thin, low = 32 * count, 16 * count
        feature = ff[group, 0:thin]
        joined = (feature - stack([average] * count)).astype(BF16)
        jb[group, 0:thin] = joined
        value, slope = elu_pair(dot(u1t_s[0:thin, 0:thin], joined) + stack([shared] * count))
        inner = value.astype(BF16)
        ib[group, 0:thin] = inner
        ie[group, 0:thin] = slope
        raw = jnp.exp(dot(u2t_s[0:low, 0:thin], inner) + stack([c2] * count))
        for local in range(count):
            rgb, vis = strip_of(group, local)
            e = vis * cut(raw, 16, local)
            ee[group, 16 * local : 16 * (local + 1)] = e
            num = num + e * feature[32 * local : 32 * local + 16]
            den = den + e
            col = col + e[0:1] * rgb

    inv = 1.0 / den
    tokens = num / den
    colour = col / den[0:1]
    token_low = tokens.astype(BF16)
    token_t = tokens.T.astype(BF16)
    halves = [token_t[RAY * r : RAY * (r + 1)] for r in range(2)]
    query = dot(wqt, token_low).astype(BF16)
    kk_f = dot(halves[0], wk_of[0]) + dot(halves[1], wk_of[1])
    vv_f = dot(halves[0], wv_of[0]) + dot(halves[1], wv_of[1])
    kk = kk_f.astype(BF16)
    vv = vv_f.astype(BF16)
    kkt = kk.astype(F32).T.astype(BF16)
    vvt = vv.astype(F32).T.astype(BF16)
    row64 = iota((64, n), 0)

    def spread(value, head):
        mine = jnp.where((row64 >> 4) == head, value.astype(F32), 0.0)
        one = jnp.where(first_ray, mine, 0.0)
        return jnp.concatenate([one, mine - one], axis=0)

    def fold(value):
        return jnp.where(first_ray, value[:16], value[16:])

    def head_rows(value, head):
        at = 16 * head
        return jnp.concatenate([value[at : at + 16], value[64 + at : 80 + at]], axis=0)

    probs = []
    attended = []
    query_of = []
    for head in range(4):
        q_head = spread(query, head).astype(BF16)
        query_of.append(q_head)
        score = dot(kk, q_head) * 0.25
        score = jnp.exp(score - jnp.max(score, axis=0, keepdims=True))
        prob = score / jnp.sum(score, axis=0, keepdims=True)
        probs.append(prob)
        attended.append(fold(dot(head_rows(vvt, head), prob.astype(BF16))))
    attended = jnp.concatenate(attended, axis=0).astype(BF16)
    mixed = tokens + dot(wot, attended)
    mixed_low = mixed.astype(BF16)
    value, s_slope = elu_pair(dot(s1t, mixed_low) + d1)
    act = value.astype(BF16).astype(F32)
    z = jnp.sum(act * s2, axis=0, keepdims=True) + d2
    delta = delta_ref[0]
    ez = jnp.exp(-jnp.abs(z))
    density = jnp.maximum(z, 0.0) + jnp.log1p(ez)
    sigmoid = jnp.where(z >= 0.0, 1.0, ez) / (1.0 + ez)
    optical = density * delta
    tri = tri_s[...]

    def exact_rows(value):
        pad = jnp.zeros((13, n), F32)
        return jnp.concatenate([p.astype(F32) for p in parts(value, 3)] + [pad], axis=0).astype(BF16)

    before = jnp.sum(dot(exact_rows(optical), tri), axis=0, keepdims=True)
    through = jnp.exp(-before)
    gone = jnp.exp(-optical)
    render = through * (1.0 - gone)
    drawn = render * colour
    targets = target_ref[0]
    rweight = weight_ref[0]
    d_pixel = jnp.zeros((3, n), F32)
    loss = jnp.zeros((1, 1), F32)
    for r in range(2):
        mask = first_ray if r == 0 else jnp.logical_not(first_ray)
        pixel = jnp.sum(jnp.where(mask, drawn, 0.0), axis=1, keepdims=True)
        miss = pixel - targets[0:3, r : r + 1]
        scale = rweight[0:1, r : r + 1]
        loss = loss + scale * jnp.sum(miss * miss, axis=0, keepdims=True)
        d_pixel = d_pixel + jnp.where(mask, 2.0 * scale * miss, 0.0)
    place = iota((8, 128), 1) + 128 * iota((8, 128), 0)
    loss_s[...] += jnp.where(place == 0, loss, 0.0) + jnp.where(
        place == 1, rweight[0:1, 0:1] + rweight[0:1, 1:2], 0.0
    )

    d_render = jnp.sum(d_pixel * colour, axis=0, keepdims=True)
    d_colour = d_pixel * render
    d_before = -render * d_render
    d_optical = through * gone * d_render + jnp.sum(
        dot(exact_rows(d_before), tri, NT), axis=0, keepdims=True
    )
    dz = d_optical * delta * sigmoid
    gs2[...] += act * dz
    gdd[...] += jnp.where(iota((8, n), 0) == 0, dz, 0.0)
    d_pre = s2 * dz * s_slope
    gd1[...] += d_pre
    g16[293:309, :] += widen(dot_right(mixed_low, d_pre, NT))
    d_mixed = dot_right(s1b, d_pre, NN)
    g16[229:293, :] += widen(dot_right(attended, d_mixed, NT))
    d_att = dot_right(wob, d_mixed, NN)
    d_query = []
    d_kk = jnp.zeros((RAY, 128), F32)
    d_vv = jnp.zeros((RAY, 128), F32)
    for head in range(4):
        prob = probs[head]
        d_head = parts(spread(d_att, head), PASSES)
        d_prob = sum(dot(vv, piece) for piece in d_head)
        low = prob.astype(BF16)
        d_vv = d_vv + sum(dot(low, piece, NT) for piece in d_head)
        d_score = prob * (d_prob - jnp.sum(prob * d_prob, axis=0, keepdims=True)) * 0.25
        pieces = parts(d_score, PASSES)
        d_query.append(fold(sum(dot(head_rows(kkt, head), piece) for piece in pieces)))
        d_kk = d_kk + sum(dot(piece, query_of[head], NT) for piece in pieces)
    d_query = jnp.concatenate(d_query, axis=0)
    gq = dot_right(token_low, d_query, NT)
    gk = [dot_right(halves[r], d_kk, TN) for r in range(2)]
    gv = [dot_right(halves[r], d_vv, TN) for r in range(2)]
    wide = jnp.concatenate([widen(gq), gk[0] + roll(gk[1], 64), gv[0] + roll(gv[1], 64)], axis=0)
    for a in range(4):
        at = pl.ds(37 + a, 48, stride=4)
        g16[at, :] += jnp.where(keep16, roll(wide, -16 * a), 0.0)
    d_halves = [
        dot_left(d_kk, wk_of[r], NT) + dot_left(d_vv, wv_of[r], NT) for r in range(2)
    ]
    d_tokens = d_mixed + dot_right(wqb, d_query, NN) + jnp.concatenate(d_halves, axis=0).T
    d_num = d_tokens * inv
    d_den = -d_num * tokens
    d_col = d_colour * inv[0:1]
    d_den0 = -jnp.sum(d_col * colour, axis=0, keepdims=True)
    row16 = iota((16, n), 0)
    d_den = d_den + jnp.where(row16 == 0, d_den0, 0.0)

    d_average = jnp.zeros((32, n), F32)
    d_shared = jnp.zeros((32, n), F32)
    sum_c2 = jnp.zeros((16, n), F32)
    for group, count in enumerate(counts):
        thin, low = 32 * count, 16 * count
        d_logit = []
        for local in range(count):
            rgb, _ = strip_of(group, local)
            e = ee[group, 16 * local : 16 * (local + 1)]
            d_e = d_num * ff[group, 32 * local : 32 * local + 16] + d_den
            d_e = d_e + jnp.where(row16 == 0, jnp.sum(d_col * rgb, axis=0, keepdims=True), 0.0)
            d_logit.append(d_e * e)
            sum_c2 = sum_c2 + d_logit[-1]
            ee[group, 16 * local : 16 * (local + 1)] = d_num * e
        pieces = parts(stack(d_logit), PASSES)
        gu2[0:thin, 0:low] += sum(dot(ib[group, 0:thin], piece, NT) for piece in pieces)
        d_inner = sum(dot(u2_s[0:thin, 0:low], piece) for piece in pieces) * ie[group, 0:thin]
        pieces = parts(d_inner, PASSES)
        gu1[0:thin, 0:thin] += sum(dot(jb[group, 0:thin], piece, NT) for piece in pieces)
        d_joined = sum(dot(u1_s[0:thin, 0:thin], piece) for piece in pieces)
        ie[group, 0:thin] = d_joined
        for local in range(count):
            d_shared = d_shared + cut(d_inner, 32, local)
            d_average = d_average - cut(d_joined, 32, local)
    pieces = parts(d_shared, PASSES)
    d_variance = sum(dot(u1b, piece) for piece in pieces)
    g32[97:129, :] += widen(sum(dot(variance_low, piece, NT) for piece in pieces))
    gc1[...] += d_shared
    gc2[...] += sum_c2
    inv_seen = 1.0 / seen
    d_square = d_variance * inv_seen
    d_sum = (d_average - 2.0 * average * d_variance) * inv_seen

    sum_b2 = jnp.zeros((32, n), F32)
    for group, count in enumerate(counts):
        wide, thin = 64 * count, 32 * count
        d_feature = []
        for local in range(count):
            at = slice(32 * local, 32 * (local + 1))
            vis = strip_of(group, local)[1]
            d_one = ie[group, at] + vis * (d_sum + 2.0 * ff[group, at] * d_square)
            kept = ee[group, 16 * local : 16 * (local + 1)]
            d_one = jnp.concatenate([d_one[:16] + kept, d_one[16:]], axis=0) * fe[group, at]
            sum_b2 = sum_b2 + d_one
            d_feature.append(d_one)
        pieces = parts(stack(d_feature), PASSES)
        gw2[0:wide, 0:thin] += sum(dot(hb[group, 0:wide], piece, NT) for piece in pieces)
        d_hidden = sum(dot(w2_s[0:wide, 0:thin], piece) for piece in pieces) * he[group, 0:wide]
        gw1[:, 0:wide] += dot_right(xs[group], d_hidden, NT)
    gb2[...] += sum_b2

    @pl.when(step == pl.num_programs(0) - 1)
    def _():
        ones = jnp.ones((8, n), BF16)
        row_of = lambda ref: widen(dot_right(ones, ref[...], NT, 3)[0:1])
        g32[0:64, :] = blocks_sum(gw2, 64, 32, views)
        g32[65:97, :] = blocks_sum(gu1, 32, 32, views)
        g16[4:36, :] = blocks_sum(gu2, 32, 16, views)
        g32[64:65, :] = row_of(gb2)
        g32[129:130, :] = row_of(gc1)
        g16[36:37, :] = row_of(gc2)
        g16[309:310, :] = row_of(gd1)
        g16[310:311, :] = row_of(gs2)
        g16[311:312, :] = jnp.where(iota((1, 128), 1) == 0, row_of(gdd), 0.0)
        total = gw1[0:36, 0:128]
        total = total + roll(gw1[STRIP : STRIP + 36, 0:128], 64)
        total = total + gw1[2 * STRIP : 2 * STRIP + 36, 128:256]
        g64[0:36, :] = jnp.where(iota((36, 128), 1) < 64, total, 0.0)
        out_ref[...] = jnp.zeros_like(out_ref)
        out_ref[0:18, :] = sum(roll(g64[pl.ds(b, 18, stride=2), :], 64 * b) for b in range(2))
        out_ref[18:51, :] += sum(roll(g32[pl.ds(b, 33, stride=4), :], 32 * b) for b in range(4))
        out_ref[50:89, :] += sum(roll(g16[pl.ds(b, 39, stride=8), :], 16 * b) for b in range(8))
        out_ref[96:104, :] = loss_s[...]


def widen(value):
    rows, width = value.shape
    return jnp.concatenate([value, jnp.zeros((rows, 128 - width), F32)], axis=1)


def run_main(me, blocks, pieces, shard, deltas, targets, ray_weight):
    rows, points = blocks[0].shape[1:]
    views = rows // STRIP
    n = CHUNK
    steps = points // n
    whole = deltas.shape[0] // 2
    pairs = deltas.reshape(whole, 1, n)
    target_pairs = jnp.pad(
        targets.reshape(whole, 2, 3).transpose(0, 2, 1), ((0, 0), (0, 5), (0, 126))
    )
    weight_pairs = jnp.pad(ray_weight.reshape(whole, 1, 2), ((0, 0), (0, 7), (0, 126)))
    vm = pltpu.VMEM
    own = lambda t, me: (me[0] * steps + t, 0, 0)
    block = pl.BlockSpec((1, rows, n), lambda t, me: (0, 0, t))
    piece = pl.BlockSpec(pieces.shape, lambda t, me: (0, 0, 0))
    return pl.pallas_call(
        lambda *refs: main_kernel(views, shard, *refs),
        out_shape=jax.ShapeDtypeStruct((104, 128), F32),
        grid_spec=pltpu.PrefetchScalarGridSpec(
            num_scalar_prefetch=1,
            grid=(steps,),
            in_specs=[piece]
            + [block] * 4
            + [
                pl.BlockSpec((1, 1, n), own),
                pl.BlockSpec((1, 8, 128), own),
                pl.BlockSpec((1, 8, 128), own),
            ],
            out_specs=pl.BlockSpec((104, 128), lambda t, me: (0, 0)),
            scratch_shapes=[
                vm((120, 128), F32),
                vm((40, 128), F32),
                vm((144, 128), F32),
                vm((320, 128), F32),
                vm((4, rows, n), BF16),
                vm((4, 64 * views, n), BF16),
                vm((4, 64 * views, n), F32),
                vm((4, 32 * views, n), F32),
                vm((4, 32 * views, n), F32),
                vm((4, 32 * views, n), BF16),
                vm((4, 32 * views, n), BF16),
                vm((4, 32 * views, n), F32),
                vm((4, 16 * views, n), F32),
                vm((64 * views, 128), BF16),
                vm((32 * views, 256), BF16),
                vm((64 * views, 128), BF16),
                vm((32 * views, 128), BF16),
                vm((32 * views, 128), BF16),
                vm((16 * views, 128), BF16),
                vm((32 * views, 128), BF16),
                vm((n, n), BF16),
                vm((40, 128), F32),
                vm((136, 128), F32),
                vm((312, 128), F32),
                vm((rows, 256), F32),
                vm((64 * views, 128), F32),
                vm((32 * views, 128), F32),
                vm((32 * views, 128), F32),
                vm((32, n), F32),
                vm((32, n), F32),
                vm((16, n), F32),
                vm((16, n), F32),
                vm((16, n), F32),
                vm((8, n), F32),
                vm((8, 128), F32),
            ],
        ),
        compiler_params=pltpu.CompilerParams(vmem_limit_bytes=48 * 1024 * 1024),
    )(me, pieces, *blocks, pairs, target_pairs, weight_pairs)


def adamw(master, first_moment, second_moment, gradient, step_count):
    step_float = step_count[0].astype(F32)
    first_new = MOMENT_DECAY * first_moment + (1.0 - MOMENT_DECAY) * gradient
    second_new = SQUARE_DECAY * second_moment + (1.0 - SQUARE_DECAY) * gradient * gradient
    first_fix = 1.0 - jnp.power(MOMENT_DECAY, step_float)
    second_fix = 1.0 - jnp.power(SQUARE_DECAY, step_float)
    update = first_new / first_fix / (jnp.sqrt(second_new / second_fix) + EPSILON)
    master_new = master - LEARNING_RATE * (update + WEIGHT_DECAY * master)
    return (master_new, first_new, second_new)


def body(
    master,
    first_moment,
    second_moment,
    step_count,
    feature_maps,
    pixel_index,
    visible,
    deltas,
    targets,
    scene_id,
    scene_weight,
):
    group = lax.axis_size("views")
    shards = lax.axis_size("rays")
    assert feature_maps.shape[2] <= SEEN_BIT
    shard = master.shape[0]
    spots = [lax.axis_index("views"), lax.axis_index("rays")]
    me = jnp.stack(spots).astype(jnp.int32)
    swap = lambda size, k: [(i, i ^ k) for i in range(size)]
    rows = -(-shard // 2048) * 16
    piece = jnp.pad(master.astype(BF16), (0, rows * 128 - shard)).reshape(rows, 128)
    packed = pixel_index.T + (visible.T << SEEN_SHIFT)
    held = piece[None]
    links = shards.bit_length() - 1
    for link in range(links):
        held = jnp.concatenate([held, lax.ppermute(held, "rays", swap(shards, 1 << link))])
    far = gather_rows(packed, feature_maps, me, group, (3, 2))
    three = lax.ppermute(far[0], "views", swap(group, 3))
    two = lax.ppermute(far[1], "views", swap(group, 2))
    near = gather_rows(packed, feature_maps, me, group, (1,))
    one = lax.ppermute(near[0], "views", swap(group, 1))
    mine = gather_rows(packed, feature_maps, me, group, (0,))
    hits = (scene_id[:, None] == jnp.arange(scene_weight.shape[0])[None, :]).astype(F32)
    ray_weight = jnp.sum(hits * scene_weight.astype(F32)[None, :], axis=1)
    result = run_main(me, [mine[0], one, two, three], held, shard, deltas, targets, ray_weight)
    summed = result[:89].reshape(-1)
    size = shards * shard
    if summed.shape[0] < size:
        summed = jnp.pad(summed, (0, size - summed.shape[0]))
    extra = jnp.broadcast_to(result[96, :2][None], (shards, 2))
    send = jnp.concatenate([summed[:size].reshape(shards, shard), extra], axis=1)
    got = lax.all_to_all(send, "rays", 0, 0, tiled=True)
    partial = jnp.sum(got, axis=0)
    whole = partial
    for k in range(1, group):
        whole = whole + lax.ppermute(partial, "views", [(i, i ^ k) for i in range(group)])
    seed = 1.0 / whole[shard + 1]
    loss = whole[shard] * seed
    gradient = whole[:shard] * seed
    return (loss, *adamw(master, first_moment, second_moment, gradient, step_count))


def solution(mesh):
    placed = (
        P("rays"),
        P("rays"),
        P("rays"),
        P(),
        P("views", None, None),
        P("rays", "views"),
        P("rays", "views"),
        P("rays", None),
        P("rays", None),
        P("rays"),
        P(),
    )
    return jax.shard_map(
        body,
        mesh=mesh,
        in_specs=placed,
        out_specs=(P(), P("rays"), P("rays"), P("rays")),
        check_vma=False,
    )
```

```python
import jax
import jax.numpy as jnp
from jax import lax
from jax.experimental import pallas as pl
from jax.experimental.pallas import tpu as pltpu
from jax.sharding import PartitionSpec as P


F32 = jnp.float32
BF16 = jnp.bfloat16
SEEN_VIEWS = 10
CHANNELS = 35
STRIP = 40
BAND = 40
SEEN_SHIFT = 14
SEEN_BIT = 1 << SEEN_SHIFT
GATHER_TILE = 256
RAY = 192
CHUNK = 2 * RAY
PASSES = 1
TILE = 128
MOMENT_DECAY = 0.5
SQUARE_DECAY = 0.5
LEARNING_RATE = 0.05
WEIGHT_DECAY = 0.01
EPSILON = 1e-08
NN = (((1,), (0,)), ((), ()))
NT = (((1,), (1,)), ((), ()))
TN = (((0,), (0,)), ((), ()))


def dot(left, right, dims=NN):
    return lax.dot_general(left, right, dims, preferred_element_type=F32)


def parts(value, count):
    out = []
    for step in range(count):
        piece = value.astype(BF16)
        out.append(piece)
        if step + 1 < count:
            value = value - piece.astype(F32)
    return out


def dot_left(value, right, dims, count=PASSES):
    return sum(dot(piece, right, dims) for piece in parts(value, count))


def dot_right(left, value, dims, count=PASSES):
    return sum(dot(left, piece, dims) for piece in parts(value, count))


def elu_pair(value):
    slope = jnp.exp(jnp.minimum(value, 0.0))
    return jnp.maximum(value, 0.0) + (slope - 1.0), slope


def iota(shape, axis):
    return lax.broadcasted_iota(jnp.int32, shape, axis)


def stack_maps(map_ref, stacked):
    views, channels, pixels = map_ref.shape
    blocks = pixels // 256
    for view in range(views):
        for block in range(0, blocks, 2):
            strips = []
            for part in range(block, min(block + 2, blocks)):
                strips.append(map_ref[view, :, 256 * part : 256 * (part + 1)].astype(F32))
                strips.append(jnp.zeros((BAND - channels, 256), F32))
            strips = jnp.concatenate(strips, axis=0)
            stacked[view, BAND * block : BAND * block + strips.shape[0], :] = strips.astype(BF16)


def gather_kernel(views, tile, count, *refs):
    packed_refs, source = refs[1 : 1 + count], refs[1 + count]
    outs, stacked = refs[2 + count : -1], refs[-1]
    blocks = stacked.shape[1] // BAND

    @pl.when(pl.program_id(0) == 0)
    def _():
        stack_maps(source, stacked)

    row = iota((8, tile), 0) + 8 * (CHANNELS // 8)
    for packed_ref, out_ref in zip(packed_refs, outs):
        strips = []
        for view in range(views):
            packed = packed_ref[view : view + 1, :]
            index = packed & (SEEN_BIT - 1)
            high = jnp.broadcast_to(index >> 8, (8, tile))
            low = jnp.broadcast_to(index & 255, (256, tile))
            picked = (iota((256, tile), 0) == low).astype(F32).astype(BF16)
            found = dot(stacked[view], picked)
            totals = [jnp.zeros((8, tile), F32)] * (STRIP // 8)
            for block in range(blocks):
                here = high == block
                for part in range(STRIP // 8):
                    at = BAND * block + 8 * part
                    totals[part] = jnp.where(here, found[at : at + 8], totals[part])
            seen = jnp.broadcast_to((packed >> SEEN_SHIFT).astype(F32), (8, tile))
            last = jnp.where(row == CHANNELS, 1.0, totals[-1])
            last = jnp.where(row == CHANNELS + 1, seen, last)
            totals[-1] = jnp.where(row > CHANNELS + 1, 0.0, last)
            strips += totals
        out_ref[0] = jnp.concatenate(strips, axis=0).astype(BF16)


def gather_rows(packed, source, me, group, ways):
    views, points = packed.shape
    tile = GATHER_TILE
    own = points // group
    tiles = own // tile
    count = len(ways)
    part = lambda k: pl.BlockSpec((views, tile), lambda t, me: (0, (me[0] ^ k) * tiles + t))
    whole = lambda shape: pl.BlockSpec(shape, lambda t, me: (0, 0, 0))
    outs = [jax.ShapeDtypeStruct((1, views * STRIP, own), BF16)] * count
    out_specs = [pl.BlockSpec((1, views * STRIP, tile), lambda t, me: (0, 0, t))] * count
    table = (views, BAND * (source.shape[2] // 256), 256)
    flops = 2 * views * own * count * table[1] * 256
    return pl.pallas_call(
        lambda *refs: gather_kernel(views, tile, count, *refs),
        out_shape=outs,
        grid_spec=pltpu.PrefetchScalarGridSpec(
            num_scalar_prefetch=1,
            grid=(tiles,),
            in_specs=[part(k) for k in ways] + [whole(source.shape)],
            out_specs=out_specs,
            scratch_shapes=[pltpu.VMEM(table, BF16)],
        ),
        compiler_params=pltpu.CompilerParams(vmem_limit_bytes=32 * 1024 * 1024),
        cost_estimate=pl.CostEstimate(
            flops=flops, bytes_accessed=source.size * 2, transcendentals=0
        ),
    )(me, *([packed] * count), source)


def roll(value, shift):
    return pltpu.roll(value, shift % 128, 1)


def unpack(a_ref, r64, r32, r16):
    for b in range(2):
        r64[pl.ds(b, 18, stride=2), :] = roll(a_ref[0:18, :], -64 * b)
    for b in range(4):
        r32[pl.ds(b, 33, stride=4), :] = roll(a_ref[18:51, :], -32 * b)
    for b in range(8):
        r16[pl.ds(b, 39, stride=8), :] = roll(a_ref[50:89, :], -16 * b)


def assemble(place, shard, shard_refs, a_ref):
    a_ref[...] = jnp.zeros_like(a_ref)
    shards, rows, _ = shard_refs.shape
    for k in range(shards):
        start = (place ^ k) * shard
        shift = start & 127
        value = pltpu.roll(shard_refs[k].astype(F32), shift, 1)
        keep = iota((rows, 128), 1) >= shift
        first = start >> 7
        a_ref[pl.ds(first, rows), :] += jnp.where(keep, value, 0.0)
        a_ref[pl.ds(first + 1, rows), :] += jnp.where(keep, 0.0, value)


def repeat(weight, out_ref, times):
    out_ref[...] = jnp.zeros_like(out_ref)
    rows, width = weight.shape
    wide = widen(weight)
    for part in range(times):
        tile, shift = divmod(width * part, 128)
        out_ref[rows * part : rows * (part + 1), 128 * tile : 128 * (tile + 1)] = roll(
            wide, shift
        ).astype(BF16)


def blocks_sum(ref, rows, width, times):
    total = sum(
        roll(ref[rows * part : rows * (part + 1), :], -width * part) for part in range(times)
    )
    return jnp.where(iota((rows, 128), 1) < width, total, 0.0)


def column(rows):
    return rows.T[:, 0:1]


def main_kernel(views, shard, me_ref, *refs):
    shard_refs, refs = refs[0], refs[1:]
    (
    x0,
    x1,
    x2,
    x3,
    delta_ref,
    target_ref,
    weight_ref,
    out_ref,
    a_ref,
    r64,
    r32,
    r16,
    xs,
    hb,
    he,
    ff,
    fe,
    jb,
    ib,
    ie,
    ee,
    dl,
    di,
    df,
    dh,
    blk,
    w2t_s,
    w2_s,
    u1t_s,
    u1_s,
    u2t_s,
    u2_s,
    tri_s,
    g64,
    g32,
    g16,
    gw1,
    gw2,
    gu1,
    gu2,
    gb2,
    gc1,
    gc2,
    gd1,
    gs2,
    gdd,
    loss_s,
    ) = refs
    step = pl.program_id(0)
    n = CHUNK
    lane = iota((1, n), 1)
    first_ray = lane < RAY
    me = me_ref[0]

    @pl.when(step == 0)
    def _():
        assemble(me_ref[1], shard, shard_refs, a_ref)
        unpack(a_ref, r64, r32, r16)
        for ref in (g64, g32, g16, gw1, gw2, gu1, gu2, gb2, gc1, gc2, gd1, gs2, gdd, loss_s):
            ref[...] = jnp.zeros_like(ref)
        before = (iota((n, n), 0) < iota((n, n), 1)) & (
            (iota((n, n), 0) < RAY) == (iota((n, n), 1) < RAY)
        )
        tri_s[...] = before.astype(F32).astype(BF16)
        w1t = jnp.where(iota((64, 128), 1) < 36, 1.0, 0.0) * jnp.concatenate(
            [r64[0:36, :], jnp.zeros((92, 128), F32)], axis=0
        ).T[:64]
        for view in range(views):
            blk[64 * view : 64 * (view + 1), :] = roll(w1t, STRIP * view).astype(BF16)
        w2 = r32[0:64, :][:, :32]
        u1a = r32[65:97, :][:, :32]
        u2 = r16[4:36, :][:, :16]
        repeat(w2.T, w2t_s, views)
        repeat(w2, w2_s, views)
        repeat(u1a.T, u1t_s, views)
        repeat(u1a, u1_s, views)
        repeat(u2.T, u2t_s, views)
        repeat(u2, u2_s, views)

    for k, ref in enumerate((x0, x1, x2, x3)):
        xs[me ^ k] = ref[0]

    b2 = column(r32[64:72, :])[:32]
    u1b = r32[97:129, :][:, :32]
    u1bt = u1b.T.astype(BF16)
    u1b = u1b.astype(BF16)
    c1 = column(r32[129:137, :])[:32]
    c2 = column(r16[36:44, :])[:16]
    keep16 = iota((48, 128), 1) < 16
    qkv = sum(
        roll(jnp.where(keep16, r16[pl.ds(37 + a, 48, stride=4), :], 0.0), 16 * a) for a in range(4)
    )
    wq, wk, wv = qkv[0:16], qkv[16:32], qkv[32:48]
    wqb = wq[:, :64].astype(BF16)
    wqt = wq[:, :64].T.astype(BF16)
    wk_of = [roll(wk, 64 * r).astype(BF16) for r in range(2)]
    wv_of = [roll(wv, 64 * r).astype(BF16) for r in range(2)]
    wo = r16[229:293, :][:, :16]
    wob = wo.astype(BF16)
    wot = wo.T.astype(BF16)
    s1 = r16[293:309, :][:, :16]
    s1b = s1.astype(BF16)
    s1t = s1.T.astype(BF16)
    d1 = column(r16[309:317, :])[:16]
    s2 = column(r16[310:318, :])[:16]
    d2 = r16[311:312, 0:1]

    def strip_of(group, local, lanes):
        at = STRIP * local + 32
        strip = xs[group, at : at + 8, lanes].astype(F32)
        return strip[0:3], strip[4:5]

    def stack(values):
        return jnp.concatenate(values, axis=0) if len(values) > 1 else values[0]

    def cut(value, rows, local):
        return value[rows * local : rows * (local + 1)]

    counts = [min(views, SEEN_VIEWS - at) for at in range(0, SEEN_VIEWS, views)]

    m = TILE
    lane_tiles = [slice(at, at + m) for at in range(0, n, m)]
    join = lambda values: jnp.concatenate(values, axis=1) if len(values) > 1 else values[0]

    def forward_tile(lanes):
        sum1 = jnp.zeros((32, m), F32)
        sum2 = jnp.zeros((32, m), F32)
        seen = jnp.zeros((1, m), F32)
        for group, count in enumerate(counts):
            wide, thin = 64 * count, 32 * count
            value, slope = elu_pair(dot(blk[0:wide, 0 : views * STRIP], xs[group, :, lanes]))
            hidden = value.astype(BF16)
            hb[group, 0:wide, lanes] = hidden
            he[group, 0:wide, lanes] = slope
            value, slope = elu_pair(dot(w2t_s[0:thin, 0:wide], hidden) + stack([b2] * count))
            ff[group, 0:thin, lanes] = value
            fe[group, 0:thin, lanes] = slope
            for local in range(count):
                vis = strip_of(group, local, lanes)[1]
                one = cut(value, 32, local)
                part = vis * one
                sum1 = sum1 + part
                sum2 = sum2 + part * one
                seen = seen + vis
        average = sum1 / seen
        variance = sum2 / seen - average * average
        variance_low = variance.astype(BF16)
        shared = dot(u1bt, variance_low) + c1
        num = jnp.zeros((16, m), F32)
        den = jnp.zeros((16, m), F32)
        col = jnp.zeros((3, m), F32)
        for group, count in enumerate(counts):
            thin, low = 32 * count, 16 * count
            feature = ff[group, 0:thin, lanes]
            joined = (feature - stack([average] * count)).astype(BF16)
            jb[group, 0:thin, lanes] = joined
            value, slope = elu_pair(dot(u1t_s[0:thin, 0:thin], joined) + stack([shared] * count))
            inner = value.astype(BF16)
            ib[group, 0:thin, lanes] = inner
            ie[group, 0:thin, lanes] = slope
            raw = jnp.exp(dot(u2t_s[0:low, 0:thin], inner) + stack([c2] * count))
            for local in range(count):
                rgb, vis = strip_of(group, local, lanes)
                e = vis * cut(raw, 16, local)
                ee[group, 16 * local : 16 * (local + 1), lanes] = e
                num = num + e * feature[32 * local : 32 * local + 16]
                den = den + e
                col = col + e[0:1] * rgb
        return average, 1.0 / seen, variance_low, num, den, col

    done = [forward_tile(lanes) for lanes in lane_tiles]
    average, inv_seen, variance_low, num, den, col = [join(list(x)) for x in zip(*done)]

    inv = 1.0 / den
    tokens = num / den
    colour = col / den[0:1]
    token_low = tokens.astype(BF16)
    token_t = tokens.T.astype(BF16)
    halves = [token_t[RAY * r : RAY * (r + 1)] for r in range(2)]
    query = dot(wqt, token_low).astype(BF16).astype(F32) * 0.25
    kk_f = dot(halves[0], wk_of[0]) + dot(halves[1], wk_of[1])
    vv_f = dot(halves[0], wv_of[0]) + dot(halves[1], wv_of[1])
    kk = kk_f.astype(BF16)
    vv = vv_f.astype(BF16)
    kkt = kk.astype(F32).T.astype(BF16)
    vvt = vv.astype(F32).T.astype(BF16)

    def spread(value, head):
        mine = value[16 * head : 16 * (head + 1)].astype(F32)
        one = jnp.where(first_ray, mine, 0.0)
        rows = []
        for part in (one, mine - one):
            rows += [jnp.zeros((16 * head, n), BF16)] if head else []
            rows.append(part.astype(BF16))
            rows += [jnp.zeros((48 - 16 * head, n), BF16)] if head < 3 else []
        return jnp.concatenate(rows, axis=0)

    def fold(value):
        return jnp.where(first_ray, value[:16], value[16:])

    def head_rows(value, head):
        at = 16 * head
        return jnp.concatenate([value[at : at + 16], value[64 + at : 80 + at]], axis=0)

    probs = []
    lows = []
    attended = []
    query_of = []
    for head in range(4):
        q_head = spread(query, head)
        query_of.append(q_head)
        tiles = []
        for at in range(0, n, 128):
            score = dot(kk, q_head[:, at : at + 128])
            score = jnp.exp(score - jnp.max(score, axis=0, keepdims=True))
            tiles.append(score * (1.0 / jnp.sum(score, axis=0, keepdims=True)))
        probs.append(tiles)
        low = jnp.concatenate([tile.astype(BF16) for tile in tiles], axis=1)
        lows.append(low)
        attended.append(fold(dot(head_rows(vvt, head), low)))
    raw_attended = attended
    attended = jnp.concatenate(attended, axis=0).astype(BF16)
    mixed = tokens + dot(wot, attended)
    mixed_low = mixed.astype(BF16)
    value, s_slope = elu_pair(dot(s1t, mixed_low) + d1)
    act = value.astype(BF16).astype(F32)
    z = jnp.sum(act * s2, axis=0, keepdims=True) + d2
    delta = delta_ref[0]
    ez = jnp.exp(-jnp.abs(z))
    density = jnp.maximum(z, 0.0) + jnp.log1p(ez)
    sigmoid = jnp.where(z >= 0.0, 1.0, ez) / (1.0 + ez)
    optical = density * delta
    tri = tri_s[...]

    def exact_rows(value):
        pad = jnp.zeros((13, n), F32)
        return jnp.concatenate([p.astype(F32) for p in parts(value, 3)] + [pad], axis=0).astype(BF16)

    before = jnp.sum(dot(exact_rows(optical), tri), axis=0, keepdims=True)
    through = jnp.exp(-before)
    gone = jnp.exp(-optical)
    render = through * (1.0 - gone)
    drawn = render * colour
    targets = target_ref[0]
    rweight = weight_ref[0]
    d_pixel = jnp.zeros((3, n), F32)
    loss = jnp.zeros((1, 1), F32)
    for r in range(2):
        mask = first_ray if r == 0 else jnp.logical_not(first_ray)
        pixel = jnp.sum(jnp.where(mask, drawn, 0.0), axis=1, keepdims=True)
        miss = pixel - targets[0:3, r : r + 1]
        scale = rweight[0:1, r : r + 1]
        loss = loss + scale * jnp.sum(miss * miss, axis=0, keepdims=True)
        d_pixel = d_pixel + jnp.where(mask, 2.0 * scale * miss, 0.0)
    place = iota((8, 128), 1) + 128 * iota((8, 128), 0)
    loss_s[...] += jnp.where(place == 0, loss, 0.0) + jnp.where(
        place == 1, rweight[0:1, 0:1] + rweight[0:1, 1:2], 0.0
    )

    d_render = jnp.sum(d_pixel * colour, axis=0, keepdims=True)
    d_colour = d_pixel * render
    d_before = -render * d_render
    d_optical = through * gone * d_render + jnp.sum(
        dot(exact_rows(d_before), tri, NT), axis=0, keepdims=True
    )
    dz = d_optical * delta * sigmoid
    gs2[...] += act * dz
    gdd[...] += jnp.where(iota((8, n), 0) == 0, dz, 0.0)
    d_pre = s2 * dz * s_slope
    gd1[...] += d_pre
    g16[293:309, :] += widen(dot_right(mixed_low, d_pre, NT))
    d_mixed = dot_right(s1b, d_pre, NN)
    g16[229:293, :] += widen(dot_right(attended, d_mixed, NT))
    d_att = dot_right(wob, d_mixed, NN)
    d_query = []
    d_kk = jnp.zeros((RAY, 128), F32)
    d_vv = jnp.zeros((RAY, 128), F32)
    for head in range(4):
        mine = d_att[16 * head : 16 * (head + 1)]
        shift = jnp.sum(mine * raw_attended[head], axis=0, keepdims=True)
        d_head = spread(d_att, head)
        d_vv = d_vv + dot(lows[head], d_head, NT)
        tiles = []
        for place, prob in enumerate(probs[head]):
            at = slice(128 * place, 128 * (place + 1))
            tiles.append((prob * (dot(vv, d_head[:, at]) - shift[:, at])).astype(BF16))
        d_score = jnp.concatenate(tiles, axis=1)
        d_query.append(fold(dot(head_rows(kkt, head), d_score)) * 0.25)
        d_kk = d_kk + dot(d_score, query_of[head], NT)
    d_query = jnp.concatenate(d_query, axis=0)
    gq = dot_right(token_low, d_query, NT)
    gk = [dot_right(halves[r], d_kk, TN) for r in range(2)]
    gv = [dot_right(halves[r], d_vv, TN) for r in range(2)]
    wide = jnp.concatenate([widen(gq), gk[0] + roll(gk[1], 64), gv[0] + roll(gv[1], 64)], axis=0)
    for a in range(4):
        at = pl.ds(37 + a, 48, stride=4)
        g16[at, :] += jnp.where(keep16, roll(wide, -16 * a), 0.0)
    d_halves = [
        dot_left(d_kk, wk_of[r], NT) + dot_left(d_vv, wv_of[r], NT) for r in range(2)
    ]
    d_tokens = d_mixed + dot_right(wqb, d_query, NN) + jnp.concatenate(d_halves, axis=0).T
    d_num = d_tokens * inv
    d_den = -d_num * tokens
    d_col = d_colour * inv[0:1]
    d_den0 = -jnp.sum(d_col * colour, axis=0, keepdims=True)
    row16 = iota((16, n), 0)
    d_den = d_den + jnp.where(row16 == 0, d_den0, 0.0)

    def backward_tile(lanes):
        own_num, own_den, own_col = d_num[:, lanes], d_den[:, lanes], d_col[:, lanes]
        d_average = jnp.zeros((32, m), F32)
        d_shared = jnp.zeros((32, m), F32)
        sum_c2 = jnp.zeros((16, m), F32)
        for group, count in enumerate(counts):
            thin, low = 32 * count, 16 * count
            d_logit = []
            for local in range(count):
                at = slice(16 * local, 16 * (local + 1))
                rgb, _ = strip_of(group, local, lanes)
                e = ee[group, at, lanes]
                d_e = own_num * ff[group, 32 * local : 32 * local + 16, lanes] + own_den
                shade = jnp.sum(own_col * rgb, axis=0, keepdims=True)
                d_e = d_e + jnp.where(row16[:, :m] == 0, shade, 0.0)
                d_logit.append(d_e * e)
                sum_c2 = sum_c2 + d_logit[-1]
                ee[group, at, lanes] = own_num * e
            piece = stack(d_logit).astype(BF16)
            dl[group, 0:low, lanes] = piece
            d_inner = dot(u2_s[0:thin, 0:low], piece) * ie[group, 0:thin, lanes]
            piece = d_inner.astype(BF16)
            di[group, 0:thin, lanes] = piece
            d_joined = dot(u1_s[0:thin, 0:thin], piece)
            ie[group, 0:thin, lanes] = d_joined
            for local in range(count):
                d_shared = d_shared + cut(d_inner, 32, local)
                d_average = d_average - cut(d_joined, 32, local)
        shared_low = d_shared.astype(BF16)
        d_variance = dot(u1b, shared_low)
        gc1[:, lanes] += d_shared
        gc2[:, lanes] += sum_c2
        d_square = d_variance * inv_seen[:, lanes]
        d_sum = (d_average - 2.0 * average[:, lanes] * d_variance) * inv_seen[:, lanes]
        sum_b2 = jnp.zeros((32, m), F32)
        for group, count in enumerate(counts):
            wide, thin = 64 * count, 32 * count
            d_feature = []
            for local in range(count):
                at = slice(32 * local, 32 * (local + 1))
                vis = strip_of(group, local, lanes)[1]
                feature = ff[group, at, lanes]
                d_one = ie[group, at, lanes] + vis * (d_sum + 2.0 * feature * d_square)
                kept = ee[group, 16 * local : 16 * (local + 1), lanes]
                d_one = jnp.concatenate([d_one[:16] + kept, d_one[16:]], axis=0)
                d_one = d_one * fe[group, at, lanes]
                sum_b2 = sum_b2 + d_one
                d_feature.append(d_one)
            piece = stack(d_feature).astype(BF16)
            df[group, 0:thin, lanes] = piece
            d_hidden = dot(w2_s[0:wide, 0:thin], piece) * he[group, 0:wide, lanes]
            dh[group, 0:wide, lanes] = d_hidden.astype(BF16)
        gb2[:, lanes] += sum_b2
        return shared_low

    shared_low = join([backward_tile(lanes) for lanes in lane_tiles])
    g32[97:129, :] += widen(dot(variance_low, shared_low, NT))
    for group, count in enumerate(counts):
        wide, thin, low = 64 * count, 32 * count, 16 * count
        gu2[0:thin, 0:low] += dot(ib[group, 0:thin], dl[group, 0:low], NT)
        gu1[0:thin, 0:thin] += dot(jb[group, 0:thin], di[group, 0:thin], NT)
        gw2[0:wide, 0:thin] += dot(hb[group, 0:wide], df[group, 0:thin], NT)
        gw1[:, 0:wide] += dot(xs[group], dh[group, 0:wide], NT)

    @pl.when(step == pl.num_programs(0) - 1)
    def _():
        ones = jnp.ones((8, n), BF16)
        row_of = lambda ref: widen(dot_right(ones, ref[...], NT, 3)[0:1])
        g32[0:64, :] = blocks_sum(gw2, 64, 32, views)
        g32[65:97, :] = blocks_sum(gu1, 32, 32, views)
        g16[4:36, :] = blocks_sum(gu2, 32, 16, views)
        g32[64:65, :] = row_of(gb2)
        g32[129:130, :] = row_of(gc1)
        g16[36:37, :] = row_of(gc2)
        g16[309:310, :] = row_of(gd1)
        g16[310:311, :] = row_of(gs2)
        g16[311:312, :] = jnp.where(iota((1, 128), 1) == 0, row_of(gdd), 0.0)
        total = gw1[0:36, 0:128]
        total = total + roll(gw1[STRIP : STRIP + 36, 0:128], 64)
        total = total + gw1[2 * STRIP : 2 * STRIP + 36, 128:256]
        g64[0:36, :] = jnp.where(iota((36, 128), 1) < 64, total, 0.0)
        out_ref[...] = jnp.zeros_like(out_ref)
        out_ref[0:18, :] = sum(roll(g64[pl.ds(b, 18, stride=2), :], 64 * b) for b in range(2))
        out_ref[18:51, :] += sum(roll(g32[pl.ds(b, 33, stride=4), :], 32 * b) for b in range(4))
        out_ref[50:89, :] += sum(roll(g16[pl.ds(b, 39, stride=8), :], 16 * b) for b in range(8))
        out_ref[96:104, :] = loss_s[...]


def widen(value):
    rows, width = value.shape
    return jnp.concatenate([value, jnp.zeros((rows, 128 - width), F32)], axis=1)


def run_main(me, blocks, pieces, shard, deltas, targets, ray_weight):
    rows, points = blocks[0].shape[1:]
    views = rows // STRIP
    n = CHUNK
    steps = points // n
    whole = deltas.shape[0] // 2
    pairs = deltas.reshape(whole, 1, n)
    target_pairs = jnp.pad(
        targets.reshape(whole, 2, 3).transpose(0, 2, 1), ((0, 0), (0, 5), (0, 126))
    )
    weight_pairs = jnp.pad(ray_weight.reshape(whole, 1, 2), ((0, 0), (0, 7), (0, 126)))
    vm = pltpu.VMEM
    own = lambda t, me: (me[0] * steps + t, 0, 0)
    block = pl.BlockSpec((1, rows, n), lambda t, me: (0, 0, t))
    piece = pl.BlockSpec(pieces.shape, lambda t, me: (0, 0, 0))
    return pl.pallas_call(
        lambda *refs: main_kernel(views, shard, *refs),
        out_shape=jax.ShapeDtypeStruct((104, 128), F32),
        grid_spec=pltpu.PrefetchScalarGridSpec(
            num_scalar_prefetch=1,
            grid=(steps,),
            in_specs=[piece]
            + [block] * 4
            + [
                pl.BlockSpec((1, 1, n), own),
                pl.BlockSpec((1, 8, 128), own),
                pl.BlockSpec((1, 8, 128), own),
            ],
            out_specs=pl.BlockSpec((104, 128), lambda t, me: (0, 0)),
            scratch_shapes=[
                vm((120, 128), F32),
                vm((40, 128), F32),
                vm((144, 128), F32),
                vm((320, 128), F32),
                vm((4, rows, n), BF16),
                vm((4, 64 * views, n), BF16),
                vm((4, 64 * views, n), F32),
                vm((4, 32 * views, n), F32),
                vm((4, 32 * views, n), F32),
                vm((4, 32 * views, n), BF16),
                vm((4, 32 * views, n), BF16),
                vm((4, 32 * views, n), F32),
                vm((4, 16 * views, n), F32),
                vm((4, 16 * views, n), BF16),
                vm((4, 32 * views, n), BF16),
                vm((4, 32 * views, n), BF16),
                vm((4, 64 * views, n), BF16),
                vm((64 * views, 128), BF16),
                vm((32 * views, 256), BF16),
                vm((64 * views, 128), BF16),
                vm((32 * views, 128), BF16),
                vm((32 * views, 128), BF16),
                vm((16 * views, 128), BF16),
                vm((32 * views, 128), BF16),
                vm((n, n), BF16),
                vm((40, 128), F32),
                vm((136, 128), F32),
                vm((312, 128), F32),
                vm((rows, 256), F32),
                vm((64 * views, 128), F32),
                vm((32 * views, 128), F32),
                vm((32 * views, 128), F32),
                vm((32, n), F32),
                vm((32, n), F32),
                vm((16, n), F32),
                vm((16, n), F32),
                vm((16, n), F32),
                vm((8, n), F32),
                vm((8, 128), F32),
            ],
        ),
        compiler_params=pltpu.CompilerParams(vmem_limit_bytes=48 * 1024 * 1024),
    )(me, pieces, *blocks, pairs, target_pairs, weight_pairs)


def adamw(master, first_moment, second_moment, gradient, step_count):
    step_float = step_count[0].astype(F32)
    first_new = MOMENT_DECAY * first_moment + (1.0 - MOMENT_DECAY) * gradient
    second_new = SQUARE_DECAY * second_moment + (1.0 - SQUARE_DECAY) * gradient * gradient
    first_fix = 1.0 - jnp.power(MOMENT_DECAY, step_float)
    second_fix = 1.0 - jnp.power(SQUARE_DECAY, step_float)
    update = first_new / first_fix / (jnp.sqrt(second_new / second_fix) + EPSILON)
    master_new = master - LEARNING_RATE * (update + WEIGHT_DECAY * master)
    return (master_new, first_new, second_new)


def body(
    master,
    first_moment,
    second_moment,
    step_count,
    feature_maps,
    pixel_index,
    visible,
    deltas,
    targets,
    scene_id,
    scene_weight,
):
    group = lax.axis_size("views")
    shards = lax.axis_size("rays")
    assert feature_maps.shape[2] <= SEEN_BIT
    shard = master.shape[0]
    spots = [lax.axis_index("views"), lax.axis_index("rays")]
    me = jnp.stack(spots).astype(jnp.int32)
    swap = lambda size, k: [(i, i ^ k) for i in range(size)]
    rows = -(-shard // 2048) * 16
    piece = jnp.pad(master.astype(BF16), (0, rows * 128 - shard)).reshape(rows, 128)
    packed = pixel_index.T + (visible.T << SEEN_SHIFT)
    held = piece[None]
    links = shards.bit_length() - 1
    for link in range(links):
        held = jnp.concatenate([held, lax.ppermute(held, "rays", swap(shards, 1 << link))])
    far = gather_rows(packed, feature_maps, me, group, (3, 2))
    three = lax.ppermute(far[0], "views", swap(group, 3))
    two = lax.ppermute(far[1], "views", swap(group, 2))
    near = gather_rows(packed, feature_maps, me, group, (1,))
    one = lax.ppermute(near[0], "views", swap(group, 1))
    mine = gather_rows(packed, feature_maps, me, group, (0,))
    hits = (scene_id[:, None] == jnp.arange(scene_weight.shape[0])[None, :]).astype(F32)
    ray_weight = jnp.sum(hits * scene_weight.astype(F32)[None, :], axis=1)
    result = run_main(me, [mine[0], one, two, three], held, shard, deltas, targets, ray_weight)
    summed = result[:89].reshape(-1)
    size = shards * shard
    if summed.shape[0] < size:
        summed = jnp.pad(summed, (0, size - summed.shape[0]))
    extra = jnp.broadcast_to(result[96, :2][None], (shards, 2))
    send = jnp.concatenate([summed[:size].reshape(shards, shard), extra], axis=1)
    got = lax.all_to_all(send, "rays", 0, 0, tiled=True)
    partial = jnp.sum(got, axis=0)
    whole = partial
    for k in range(1, group):
        whole = whole + lax.ppermute(partial, "views", [(i, i ^ k) for i in range(group)])
    seed = 1.0 / whole[shard + 1]
    loss = whole[shard] * seed
    gradient = whole[:shard] * seed
    return (loss, *adamw(master, first_moment, second_moment, gradient, step_count))


def solution(mesh):
    placed = (
        P("rays"),
        P("rays"),
        P("rays"),
        P(),
        P("views", None, None),
        P("rays", "views"),
        P("rays", "views"),
        P("rays", None),
        P("rays", None),
        P("rays"),
        P(),
    )
    return jax.shard_map(
        body,
        mesh=mesh,
        in_specs=placed,
        out_specs=(P(), P("rays"), P("rays"), P("rays")),
        check_vma=False,
    )
```

```python
import jax
import jax.numpy as jnp
from jax import lax
from jax.experimental import pallas as pl
from jax.experimental.pallas import tpu as pltpu
from jax.sharding import PartitionSpec as P


F32 = jnp.float32
BF16 = jnp.bfloat16
SEEN_VIEWS = 10
CHANNELS = 35
STRIP = 40
BAND = 40
SEEN_SHIFT = 14
SEEN_BIT = 1 << SEEN_SHIFT
GATHER_TILE = 256
RAY = 192
CHUNK = 2 * RAY
PASSES = 1
TILE = 128
MOMENT_DECAY = 0.5
SQUARE_DECAY = 0.5
LEARNING_RATE = 0.05
WEIGHT_DECAY = 0.01
EPSILON = 1e-08
NN = (((1,), (0,)), ((), ()))
NT = (((1,), (1,)), ((), ()))
TN = (((0,), (0,)), ((), ()))


def dot(left, right, dims=NN):
    return lax.dot_general(left, right, dims, preferred_element_type=F32)


def parts(value, count):
    out = []
    for step in range(count):
        piece = value.astype(BF16)
        out.append(piece)
        if step + 1 < count:
            value = value - piece.astype(F32)
    return out


def dot_left(value, right, dims, count=PASSES):
    return sum(dot(piece, right, dims) for piece in parts(value, count))


def dot_right(left, value, dims, count=PASSES):
    return sum(dot(left, piece, dims) for piece in parts(value, count))


def elu_pair(value):
    slope = jnp.exp(jnp.minimum(value, 0.0))
    return jnp.maximum(value, 0.0) + (slope - 1.0), slope


def iota(shape, axis):
    return lax.broadcasted_iota(jnp.int32, shape, axis)


def stack_maps(map_ref, stacked, view):
    channels, pixels = map_ref.shape[1:]
    blocks = pixels // 256
    for block in range(0, blocks, 2):
        strips = []
        for part in range(block, min(block + 2, blocks)):
            strips.append(map_ref[view, :, 256 * part : 256 * (part + 1)].astype(F32))
            strips.append(jnp.zeros((BAND - channels, 256), F32))
        strips = jnp.concatenate(strips, axis=0)
        stacked[view, BAND * block : BAND * block + strips.shape[0], :] = strips.astype(BF16)


def gather_kernel(views, tile, count, *refs):
    packed_refs, source = refs[1 : 1 + count], refs[1 + count]
    outs, stacked = refs[2 + count : -1], refs[-1]
    blocks = stacked.shape[1] // BAND

    @pl.when(pl.program_id(0) == 0)
    def _():
        for view in range(views):
            stack_maps(source, stacked, view)

    row = iota((8, tile), 0) + 8 * (CHANNELS // 8)
    for packed_ref, out_ref in zip(packed_refs, outs):
        strips = []
        for view in range(views):
            packed = packed_ref[view : view + 1, :]
            index = packed & (SEEN_BIT - 1)
            high = jnp.broadcast_to(index >> 8, (8, tile))
            low = jnp.broadcast_to(index & 255, (256, tile))
            picked = (iota((256, tile), 0) == low).astype(F32).astype(BF16)
            found = dot(stacked[view], picked)
            totals = [jnp.zeros((8, tile), F32)] * (STRIP // 8)
            for block in range(blocks):
                here = high == block
                for part in range(STRIP // 8):
                    at = BAND * block + 8 * part
                    totals[part] = jnp.where(here, found[at : at + 8], totals[part])
            seen = jnp.broadcast_to((packed >> SEEN_SHIFT).astype(F32), (8, tile))
            last = jnp.where(row == CHANNELS, 1.0, totals[-1])
            last = jnp.where(row == CHANNELS + 1, seen, last)
            totals[-1] = jnp.where(row > CHANNELS + 1, 0.0, last)
            strips += totals
        out_ref[0] = jnp.concatenate(strips, axis=0).astype(BF16)


def gather_rows(packed, source, me, group, ways):
    views, points = packed.shape
    tile = GATHER_TILE
    own = points // group
    tiles = own // tile
    count = len(ways)
    part = lambda k: pl.BlockSpec((views, tile), lambda t, me: (0, (me[0] ^ k) * tiles + t))
    whole = lambda shape: pl.BlockSpec(shape, lambda t, me: (0, 0, 0))
    outs = [jax.ShapeDtypeStruct((1, views * STRIP, own), BF16)] * count
    out_specs = [pl.BlockSpec((1, views * STRIP, tile), lambda t, me: (0, 0, t))] * count
    table = (views, BAND * (source.shape[2] // 256), 256)
    flops = 2 * views * own * count * table[1] * 256
    return pl.pallas_call(
        lambda *refs: gather_kernel(views, tile, count, *refs),
        out_shape=outs,
        grid_spec=pltpu.PrefetchScalarGridSpec(
            num_scalar_prefetch=1,
            grid=(tiles,),
            in_specs=[part(k) for k in ways] + [whole(source.shape)],
            out_specs=out_specs,
            scratch_shapes=[pltpu.VMEM(table, BF16)],
        ),
        compiler_params=pltpu.CompilerParams(vmem_limit_bytes=32 * 1024 * 1024),
        cost_estimate=pl.CostEstimate(
            flops=flops, bytes_accessed=source.size * 2, transcendentals=0
        ),
    )(me, *([packed] * count), source)


def roll(value, shift):
    return pltpu.roll(value, shift % 128, 1)


def unpack(a_ref, r64, r32, r16):
    for b in range(2):
        r64[pl.ds(b, 18, stride=2), :] = roll(a_ref[0:18, :], -64 * b)
    for b in range(4):
        r32[pl.ds(b, 33, stride=4), :] = roll(a_ref[18:51, :], -32 * b)
    for b in range(8):
        r16[pl.ds(b, 39, stride=8), :] = roll(a_ref[50:89, :], -16 * b)


def assemble(place, shard, shard_refs, a_ref):
    a_ref[...] = jnp.zeros_like(a_ref)
    shards, rows, _ = shard_refs.shape
    for k in range(shards):
        start = (place ^ k) * shard
        shift = start & 127
        value = pltpu.roll(shard_refs[k].astype(F32), shift, 1)
        keep = iota((rows, 128), 1) >= shift
        first = start >> 7
        a_ref[pl.ds(first, rows), :] += jnp.where(keep, value, 0.0)
        a_ref[pl.ds(first + 1, rows), :] += jnp.where(keep, 0.0, value)


def repeat(weight, out_ref, times):
    out_ref[...] = jnp.zeros_like(out_ref)
    rows, width = weight.shape
    wide = widen(weight)
    for part in range(times):
        tile, shift = divmod(width * part, 128)
        out_ref[rows * part : rows * (part + 1), 128 * tile : 128 * (tile + 1)] = roll(
            wide, shift
        ).astype(BF16)


def blocks_sum(ref, rows, width, times):
    total = sum(
        roll(ref[rows * part : rows * (part + 1), :], -width * part) for part in range(times)
    )
    return jnp.where(iota((rows, 128), 1) < width, total, 0.0)


def column(rows):
    return rows.T[:, 0:1]


def main_kernel(views, shard, me_ref, *refs):
    shard_refs, refs = refs[0], refs[1:]
    (
    x0,
    x1,
    x2,
    x3,
    delta_ref,
    target_ref,
    weight_ref,
    out_ref,
    sums_ref,
    a_ref,
    r64,
    r32,
    r16,
    xs,
    hb,
    he,
    ff,
    fe,
    jb,
    ib,
    ie,
    ee,
    dl,
    di,
    df,
    dh,
    blk,
    w2t_s,
    w2_s,
    u1t_s,
    u1_s,
    u2t_s,
    u2_s,
    tri_s,
    g64,
    g32,
    g16,
    gw1,
    gw2,
    gu1,
    gu2,
    gb2,
    gc1,
    gc2,
    gd1,
    gs2,
    gdd,
    loss_s,
    ) = refs
    step = pl.program_id(0)
    n = CHUNK
    lane = iota((1, n), 1)
    first_ray = lane < RAY
    me = me_ref[0]

    @pl.when(step == 0)
    def _():
        assemble(me_ref[1], shard, shard_refs, a_ref)
        unpack(a_ref, r64, r32, r16)
        for ref in (g64, g32, g16, gw1, gw2, gu1, gu2, gb2, gc1, gc2, gd1, gs2, gdd, loss_s):
            ref[...] = jnp.zeros_like(ref)
        before = (iota((n, n), 0) < iota((n, n), 1)) & (
            (iota((n, n), 0) < RAY) == (iota((n, n), 1) < RAY)
        )
        tri_s[...] = before.astype(F32).astype(BF16)
        w1t = jnp.where(iota((64, 128), 1) < 36, 1.0, 0.0) * jnp.concatenate(
            [r64[0:36, :], jnp.zeros((92, 128), F32)], axis=0
        ).T[:64]
        for view in range(views):
            blk[64 * view : 64 * (view + 1), :] = roll(w1t, STRIP * view).astype(BF16)
        w2 = r32[0:64, :][:, :32]
        u1a = r32[65:97, :][:, :32]
        u2 = r16[4:36, :][:, :16]
        repeat(w2.T, w2t_s, views)
        repeat(w2, w2_s, views)
        repeat(u1a.T, u1t_s, views)
        repeat(u1a, u1_s, views)
        repeat(u2.T, u2t_s, views)
        repeat(u2, u2_s, views)

    for k, ref in enumerate((x0, x1, x2, x3)):
        xs[me ^ k] = ref[0]

    b2 = column(r32[64:72, :])[:32]
    u1b = r32[97:129, :][:, :32]
    u1bt = u1b.T.astype(BF16)
    u1b = u1b.astype(BF16)
    c1 = column(r32[129:137, :])[:32]
    c2 = column(r16[36:44, :])[:16]
    keep16 = iota((48, 128), 1) < 16
    qkv = sum(
        roll(jnp.where(keep16, r16[pl.ds(37 + a, 48, stride=4), :], 0.0), 16 * a) for a in range(4)
    )
    wq, wk, wv = qkv[0:16], qkv[16:32], qkv[32:48]
    wqb = wq[:, :64].astype(BF16)
    wqt = wq[:, :64].T.astype(BF16)
    wk_of = [roll(wk, 64 * r).astype(BF16) for r in range(2)]
    wv_of = [roll(wv, 64 * r).astype(BF16) for r in range(2)]
    wo = r16[229:293, :][:, :16]
    wob = wo.astype(BF16)
    wot = wo.T.astype(BF16)
    s1 = r16[293:309, :][:, :16]
    s1b = s1.astype(BF16)
    s1t = s1.T.astype(BF16)
    d1 = column(r16[309:317, :])[:16]
    s2 = column(r16[310:318, :])[:16]
    d2 = r16[311:312, 0:1]

    def strip_of(group, local, lanes):
        at = STRIP * local + 32
        strip = xs[group, at : at + 8, lanes].astype(F32)
        return strip[0:3], strip[4:5]

    def stack(values):
        return jnp.concatenate(values, axis=0) if len(values) > 1 else values[0]

    def cut(value, rows, local):
        return value[rows * local : rows * (local + 1)]

    counts = [min(views, SEEN_VIEWS - at) for at in range(0, SEEN_VIEWS, views)]

    m = TILE
    lane_tiles = [slice(at, at + m) for at in range(0, n, m)]
    join = lambda values: jnp.concatenate(values, axis=1) if len(values) > 1 else values[0]

    def forward_tile(lanes):
        sum1 = jnp.zeros((32, m), F32)
        sum2 = jnp.zeros((32, m), F32)
        seen = jnp.zeros((1, m), F32)
        for group, count in enumerate(counts):
            wide, thin = 64 * count, 32 * count
            value, slope = elu_pair(dot(blk[0:wide, 0 : views * STRIP], xs[group, :, lanes]))
            hidden = value.astype(BF16)
            hb[group, 0:wide, lanes] = hidden
            he[group, 0:wide, lanes] = slope
            value, slope = elu_pair(dot(w2t_s[0:thin, 0:wide], hidden) + stack([b2] * count))
            ff[group, 0:thin, lanes] = value
            fe[group, 0:thin, lanes] = slope
            for local in range(count):
                vis = strip_of(group, local, lanes)[1]
                one = cut(value, 32, local)
                part = vis * one
                sum1 = sum1 + part
                sum2 = sum2 + part * one
                seen = seen + vis
        average = sum1 / seen
        variance = sum2 / seen - average * average
        variance_low = variance.astype(BF16)
        shared = dot(u1bt, variance_low) + c1
        num = jnp.zeros((16, m), F32)
        den = jnp.zeros((16, m), F32)
        col = jnp.zeros((3, m), F32)
        for group, count in enumerate(counts):
            thin, low = 32 * count, 16 * count
            feature = ff[group, 0:thin, lanes]
            joined = (feature - stack([average] * count)).astype(BF16)
            jb[group, 0:thin, lanes] = joined
            value, slope = elu_pair(dot(u1t_s[0:thin, 0:thin], joined) + stack([shared] * count))
            inner = value.astype(BF16)
            ib[group, 0:thin, lanes] = inner
            ie[group, 0:thin, lanes] = slope
            raw = jnp.exp(dot(u2t_s[0:low, 0:thin], inner) + stack([c2] * count))
            for local in range(count):
                rgb, vis = strip_of(group, local, lanes)
                e = vis * cut(raw, 16, local)
                ee[group, 16 * local : 16 * (local + 1), lanes] = e
                num = num + e * feature[32 * local : 32 * local + 16]
                den = den + e
                col = col + e[0:1] * rgb
        return average, 1.0 / seen, variance_low, num, den, col

    done = [forward_tile(lanes) for lanes in lane_tiles]
    average, inv_seen, variance_low, num, den, col = [join(list(x)) for x in zip(*done)]

    inv = 1.0 / den
    tokens = num / den
    colour = col / den[0:1]
    token_low = tokens.astype(BF16)
    token_t = tokens.T.astype(BF16)
    halves = [token_t[RAY * r : RAY * (r + 1)] for r in range(2)]
    query = dot(wqt, token_low).astype(BF16).astype(F32) * 0.25
    kk_f = dot(halves[0], wk_of[0]) + dot(halves[1], wk_of[1])
    vv_f = dot(halves[0], wv_of[0]) + dot(halves[1], wv_of[1])
    kk = kk_f.astype(BF16)
    vv = vv_f.astype(BF16)
    kkt = kk.astype(F32).T.astype(BF16)
    vvt = vv.astype(F32).T.astype(BF16)

    def spread(value, head):
        mine = value[16 * head : 16 * (head + 1)].astype(F32)
        one = jnp.where(first_ray, mine, 0.0)
        rows = []
        for part in (one, mine - one):
            rows += [jnp.zeros((16 * head, n), BF16)] if head else []
            rows.append(part.astype(BF16))
            rows += [jnp.zeros((48 - 16 * head, n), BF16)] if head < 3 else []
        return jnp.concatenate(rows, axis=0)

    def fold(value):
        return jnp.where(first_ray, value[:16], value[16:])

    def head_rows(value, head):
        at = 16 * head
        return jnp.concatenate([value[at : at + 16], value[64 + at : 80 + at]], axis=0)

    probs = []
    lows = []
    attended = []
    query_of = []
    for head in range(4):
        q_head = spread(query, head)
        query_of.append(q_head)
        tiles = []
        for at in range(0, n, 128):
            score = dot(kk, q_head[:, at : at + 128])
            score = jnp.exp(score - jnp.max(score, axis=0, keepdims=True))
            tiles.append(score * (1.0 / jnp.sum(score, axis=0, keepdims=True)))
        probs.append(tiles)
        low = jnp.concatenate([tile.astype(BF16) for tile in tiles], axis=1)
        lows.append(low)
        attended.append(fold(dot(head_rows(vvt, head), low)))
    raw_attended = attended
    attended = jnp.concatenate(attended, axis=0).astype(BF16)
    mixed = tokens + dot(wot, attended)
    mixed_low = mixed.astype(BF16)
    value, s_slope = elu_pair(dot(s1t, mixed_low) + d1)
    act = value.astype(BF16).astype(F32)
    z = jnp.sum(act * s2, axis=0, keepdims=True) + d2
    delta = delta_ref[0]
    ez = jnp.exp(-jnp.abs(z))
    density = jnp.maximum(z, 0.0) + jnp.log1p(ez)
    sigmoid = jnp.where(z >= 0.0, 1.0, ez) / (1.0 + ez)
    optical = density * delta
    tri = tri_s[...]

    def exact_rows(value):
        pad = jnp.zeros((13, n), F32)
        return jnp.concatenate([p.astype(F32) for p in parts(value, 3)] + [pad], axis=0).astype(BF16)

    before = jnp.sum(dot(exact_rows(optical), tri), axis=0, keepdims=True)
    through = jnp.exp(-before)
    gone = jnp.exp(-optical)
    render = through * (1.0 - gone)
    drawn = render * colour
    targets = target_ref[0]
    rweight = weight_ref[0]
    d_pixel = jnp.zeros((3, n), F32)
    loss = jnp.zeros((1, 1), F32)
    for r in range(2):
        mask = first_ray if r == 0 else jnp.logical_not(first_ray)
        pixel = jnp.sum(jnp.where(mask, drawn, 0.0), axis=1, keepdims=True)
        miss = pixel - targets[0:3, r : r + 1]
        scale = rweight[0:1, r : r + 1]
        loss = loss + scale * jnp.sum(miss * miss, axis=0, keepdims=True)
        d_pixel = d_pixel + jnp.where(mask, 2.0 * scale * miss, 0.0)
    place = iota((8, 128), 1) + 128 * iota((8, 128), 0)
    loss_s[...] += jnp.where(place == 0, loss, 0.0) + jnp.where(
        place == 1, rweight[0:1, 0:1] + rweight[0:1, 1:2], 0.0
    )

    d_render = jnp.sum(d_pixel * colour, axis=0, keepdims=True)
    d_colour = d_pixel * render
    d_before = -render * d_render
    d_optical = through * gone * d_render + jnp.sum(
        dot(exact_rows(d_before), tri, NT), axis=0, keepdims=True
    )
    dz = d_optical * delta * sigmoid
    gs2[...] += act * dz
    gdd[...] += jnp.where(iota((8, n), 0) == 0, dz, 0.0)
    d_pre = s2 * dz * s_slope
    gd1[...] += d_pre
    g16[293:309, :] += widen(dot_right(mixed_low, d_pre, NT))
    d_mixed = dot_right(s1b, d_pre, NN)
    g16[229:293, :] += widen(dot_right(attended, d_mixed, NT))
    d_att = dot_right(wob, d_mixed, NN)
    d_query = []
    d_kk = jnp.zeros((RAY, 128), F32)
    d_vv = jnp.zeros((RAY, 128), F32)
    for head in range(4):
        mine = d_att[16 * head : 16 * (head + 1)]
        shift = jnp.sum(mine * raw_attended[head], axis=0, keepdims=True)
        d_head = spread(d_att, head)
        d_vv = d_vv + dot(lows[head], d_head, NT)
        tiles = []
        for place, prob in enumerate(probs[head]):
            at = slice(128 * place, 128 * (place + 1))
            tiles.append((prob * (dot(vv, d_head[:, at]) - shift[:, at])).astype(BF16))
        d_score = jnp.concatenate(tiles, axis=1)
        d_query.append(fold(dot(head_rows(kkt, head), d_score)) * 0.25)
        d_kk = d_kk + dot(d_score, query_of[head], NT)
    d_query = jnp.concatenate(d_query, axis=0)
    gq = dot_right(token_low, d_query, NT)
    gk = [dot_right(halves[r], d_kk, TN) for r in range(2)]
    gv = [dot_right(halves[r], d_vv, TN) for r in range(2)]
    wide = jnp.concatenate([widen(gq), gk[0] + roll(gk[1], 64), gv[0] + roll(gv[1], 64)], axis=0)
    for a in range(4):
        at = pl.ds(37 + a, 48, stride=4)
        g16[at, :] += jnp.where(keep16, roll(wide, -16 * a), 0.0)
    d_halves = [
        dot_left(d_kk, wk_of[r], NT) + dot_left(d_vv, wv_of[r], NT) for r in range(2)
    ]
    d_tokens = d_mixed + dot_right(wqb, d_query, NN) + jnp.concatenate(d_halves, axis=0).T
    d_num = d_tokens * inv
    d_den = -d_num * tokens
    d_col = d_colour * inv[0:1]
    d_den0 = -jnp.sum(d_col * colour, axis=0, keepdims=True)
    row16 = iota((16, n), 0)
    d_den = d_den + jnp.where(row16 == 0, d_den0, 0.0)

    def backward_tile(lanes):
        own_num, own_den, own_col = d_num[:, lanes], d_den[:, lanes], d_col[:, lanes]
        d_average = jnp.zeros((32, m), F32)
        d_shared = jnp.zeros((32, m), F32)
        sum_c2 = jnp.zeros((16, m), F32)
        for group, count in enumerate(counts):
            thin, low = 32 * count, 16 * count
            d_logit = []
            for local in range(count):
                at = slice(16 * local, 16 * (local + 1))
                rgb, _ = strip_of(group, local, lanes)
                e = ee[group, at, lanes]
                d_e = own_num * ff[group, 32 * local : 32 * local + 16, lanes] + own_den
                shade = jnp.sum(own_col * rgb, axis=0, keepdims=True)
                d_e = d_e + jnp.where(row16[:, :m] == 0, shade, 0.0)
                d_logit.append(d_e * e)
                sum_c2 = sum_c2 + d_logit[-1]
                ee[group, at, lanes] = own_num * e
            piece = stack(d_logit).astype(BF16)
            dl[group, 0:low, lanes] = piece
            d_inner = dot(u2_s[0:thin, 0:low], piece) * ie[group, 0:thin, lanes]
            piece = d_inner.astype(BF16)
            di[group, 0:thin, lanes] = piece
            d_joined = dot(u1_s[0:thin, 0:thin], piece)
            ie[group, 0:thin, lanes] = d_joined
            for local in range(count):
                d_shared = d_shared + cut(d_inner, 32, local)
                d_average = d_average - cut(d_joined, 32, local)
        shared_low = d_shared.astype(BF16)
        d_variance = dot(u1b, shared_low)
        gc1[:, lanes] += d_shared
        gc2[:, lanes] += sum_c2
        d_square = d_variance * inv_seen[:, lanes]
        d_sum = (d_average - 2.0 * average[:, lanes] * d_variance) * inv_seen[:, lanes]
        sum_b2 = jnp.zeros((32, m), F32)
        for group, count in enumerate(counts):
            wide, thin = 64 * count, 32 * count
            d_feature = []
            for local in range(count):
                at = slice(32 * local, 32 * (local + 1))
                vis = strip_of(group, local, lanes)[1]
                feature = ff[group, at, lanes]
                d_one = ie[group, at, lanes] + vis * (d_sum + 2.0 * feature * d_square)
                kept = ee[group, 16 * local : 16 * (local + 1), lanes]
                d_one = jnp.concatenate([d_one[:16] + kept, d_one[16:]], axis=0)
                d_one = d_one * fe[group, at, lanes]
                sum_b2 = sum_b2 + d_one
                d_feature.append(d_one)
            piece = stack(d_feature).astype(BF16)
            df[group, 0:thin, lanes] = piece
            d_hidden = dot(w2_s[0:wide, 0:thin], piece) * he[group, 0:wide, lanes]
            dh[group, 0:wide, lanes] = d_hidden.astype(BF16)
        gb2[:, lanes] += sum_b2
        return shared_low

    shared_low = join([backward_tile(lanes) for lanes in lane_tiles])
    g32[97:129, :] += widen(dot(variance_low, shared_low, NT))
    for group, count in enumerate(counts):
        wide, thin, low = 64 * count, 32 * count, 16 * count
        gu2[0:thin, 0:low] += dot(ib[group, 0:thin], dl[group, 0:low], NT)
        gu1[0:thin, 0:thin] += dot(jb[group, 0:thin], di[group, 0:thin], NT)
        gw2[0:wide, 0:thin] += dot(hb[group, 0:wide], df[group, 0:thin], NT)
        gw1[:, 0:wide] += dot(xs[group], dh[group, 0:wide], NT)

    @pl.when(step == pl.num_programs(0) - 1)
    def _():
        ones = jnp.ones((8, n), BF16)
        row_of = lambda ref: widen(dot_right(ones, ref[...], NT, 3)[0:1])
        g32[0:64, :] = blocks_sum(gw2, 64, 32, views)
        g32[65:97, :] = blocks_sum(gu1, 32, 32, views)
        g16[4:36, :] = blocks_sum(gu2, 32, 16, views)
        g32[64:65, :] = row_of(gb2)
        g32[129:130, :] = row_of(gc1)
        g16[36:37, :] = row_of(gc2)
        g16[309:310, :] = row_of(gd1)
        g16[310:311, :] = row_of(gs2)
        g16[311:312, :] = jnp.where(iota((1, 128), 1) == 0, row_of(gdd), 0.0)
        total = gw1[0:36, 0:128]
        total = total + roll(gw1[STRIP : STRIP + 36, 0:128], 64)
        total = total + gw1[2 * STRIP : 2 * STRIP + 36, 128:256]
        g64[0:36, :] = jnp.where(iota((36, 128), 1) < 64, total, 0.0)
        out_ref[...] = jnp.zeros_like(out_ref)
        out_ref[0:18, :] = sum(roll(g64[pl.ds(b, 18, stride=2), :], 64 * b) for b in range(2))
        out_ref[18:51, :] += sum(roll(g32[pl.ds(b, 33, stride=4), :], 32 * b) for b in range(4))
        out_ref[50:89, :] += sum(roll(g16[pl.ds(b, 39, stride=8), :], 16 * b) for b in range(8))
        sums_ref[...] = jnp.where(
            iota(sums_ref.shape, 1) == 0, loss_s[0:1, 0:1], loss_s[0:1, 1:2]
        )


def widen(value):
    rows, width = value.shape
    return jnp.concatenate([value, jnp.zeros((rows, 128 - width), F32)], axis=1)


def run_main(me, blocks, pieces, shard, deltas, targets, ray_weight):
    rows, points = blocks[0].shape[1:]
    views = rows // STRIP
    n = CHUNK
    steps = points // n
    shards = pieces.shape[0]
    sums = (shards, -(-(shard + 2) // 128) * 128)
    whole = deltas.shape[0] // 2
    pairs = deltas.reshape(whole, 1, n)
    target_pairs = jnp.pad(
        targets.reshape(whole, 2, 3).transpose(0, 2, 1), ((0, 0), (0, 5), (0, 126))
    )
    weight_pairs = jnp.pad(ray_weight.reshape(whole, 1, 2), ((0, 0), (0, 7), (0, 126)))
    vm = pltpu.VMEM
    own = lambda t, me: (me[0] * steps + t, 0, 0)
    block = pl.BlockSpec((1, rows, n), lambda t, me: (0, 0, t))
    piece = pl.BlockSpec(pieces.shape, lambda t, me: (0, 0, 0))
    return pl.pallas_call(
        lambda *refs: main_kernel(views, shard, *refs),
        out_shape=[
            jax.ShapeDtypeStruct((96, 128), F32),
            jax.ShapeDtypeStruct(sums, F32),
        ],
        grid_spec=pltpu.PrefetchScalarGridSpec(
            num_scalar_prefetch=1,
            grid=(steps,),
            in_specs=[piece]
            + [block] * 4
            + [
                pl.BlockSpec((1, 1, n), own),
                pl.BlockSpec((1, 8, 128), own),
                pl.BlockSpec((1, 8, 128), own),
            ],
            out_specs=[
                pl.BlockSpec((96, 128), lambda t, me: (0, 0)),
                pl.BlockSpec(sums, lambda t, me: (0, 0)),
            ],
            scratch_shapes=[
                vm((120, 128), F32),
                vm((40, 128), F32),
                vm((144, 128), F32),
                vm((320, 128), F32),
                vm((4, rows, n), BF16),
                vm((4, 64 * views, n), BF16),
                vm((4, 64 * views, n), F32),
                vm((4, 32 * views, n), F32),
                vm((4, 32 * views, n), F32),
                vm((4, 32 * views, n), BF16),
                vm((4, 32 * views, n), BF16),
                vm((4, 32 * views, n), F32),
                vm((4, 16 * views, n), F32),
                vm((4, 16 * views, n), BF16),
                vm((4, 32 * views, n), BF16),
                vm((4, 32 * views, n), BF16),
                vm((4, 64 * views, n), BF16),
                vm((64 * views, 128), BF16),
                vm((32 * views, 256), BF16),
                vm((64 * views, 128), BF16),
                vm((32 * views, 128), BF16),
                vm((32 * views, 128), BF16),
                vm((16 * views, 128), BF16),
                vm((32 * views, 128), BF16),
                vm((n, n), BF16),
                vm((40, 128), F32),
                vm((136, 128), F32),
                vm((312, 128), F32),
                vm((rows, 256), F32),
                vm((64 * views, 128), F32),
                vm((32 * views, 128), F32),
                vm((32 * views, 128), F32),
                vm((32, n), F32),
                vm((32, n), F32),
                vm((16, n), F32),
                vm((16, n), F32),
                vm((16, n), F32),
                vm((8, n), F32),
                vm((8, 128), F32),
            ],
        ),
        compiler_params=pltpu.CompilerParams(vmem_limit_bytes=48 * 1024 * 1024),
    )(me, pieces, *blocks, pairs, target_pairs, weight_pairs)


def adamw(master, first_moment, second_moment, gradient, step_count):
    step_float = step_count[0].astype(F32)
    first_new = MOMENT_DECAY * first_moment + (1.0 - MOMENT_DECAY) * gradient
    second_new = SQUARE_DECAY * second_moment + (1.0 - SQUARE_DECAY) * gradient * gradient
    first_fix = 1.0 - jnp.power(MOMENT_DECAY, step_float)
    second_fix = 1.0 - jnp.power(SQUARE_DECAY, step_float)
    update = first_new / first_fix / (jnp.sqrt(second_new / second_fix) + EPSILON)
    master_new = master - LEARNING_RATE * (update + WEIGHT_DECAY * master)
    return (master_new, first_new, second_new)


def body(
    master,
    first_moment,
    second_moment,
    step_count,
    feature_maps,
    pixel_index,
    visible,
    deltas,
    targets,
    scene_id,
    scene_weight,
):
    group = lax.axis_size("views")
    shards = lax.axis_size("rays")
    assert feature_maps.shape[2] <= SEEN_BIT
    shard = master.shape[0]
    spots = [lax.axis_index("views"), lax.axis_index("rays")]
    me = jnp.stack(spots).astype(jnp.int32)
    swap = lambda size, k: [(i, i ^ k) for i in range(size)]
    rows = -(-shard // 2048) * 16
    piece = jnp.pad(master.astype(BF16), (0, rows * 128 - shard)).reshape(rows, 128)
    packed = pixel_index.T + (visible.T << SEEN_SHIFT)
    held = piece[None]
    links = shards.bit_length() - 1
    for link in range(links):
        held = jnp.concatenate([held, lax.ppermute(held, "rays", swap(shards, 1 << link))])
    far = gather_rows(packed, feature_maps, me, group, (3, 2))
    three = lax.ppermute(far[0], "views", swap(group, 3))
    two = lax.ppermute(far[1], "views", swap(group, 2))
    near = gather_rows(packed, feature_maps, me, group, (1,))
    one = lax.ppermute(near[0], "views", swap(group, 1))
    mine = gather_rows(packed, feature_maps, me, group, (0,))
    hits = (scene_id[:, None] == jnp.arange(scene_weight.shape[0])[None, :]).astype(F32)
    ray_weight = jnp.sum(hits * scene_weight.astype(F32)[None, :], axis=1)
    result, sums = run_main(me, [mine[0], one, two, three], held, shard, deltas, targets, ray_weight)
    summed = result[:89].reshape(-1)
    size = shards * shard
    if summed.shape[0] < size:
        summed = jnp.pad(summed, (0, size - summed.shape[0]))
    loss_at, far_at = shard, shard + 1
    send = jnp.concatenate([summed[:size].reshape(shards, shard), sums], axis=1)
    got = lax.all_to_all(send, "rays", 0, 0, tiled=True)
    partial = jnp.sum(got, axis=0)
    whole = partial
    for k in range(1, group):
        whole = whole + lax.ppermute(partial, "views", [(i, i ^ k) for i in range(group)])
    scaled = whole[: shard + 1] / whole[far_at : far_at + shard + 1]
    loss = scaled[loss_at]
    gradient = scaled[:shard]
    return (loss, *adamw(master, first_moment, second_moment, gradient, step_count))


def solution(mesh):
    placed = (
        P("rays"),
        P("rays"),
        P("rays"),
        P(),
        P("views", None, None),
        P("rays", "views"),
        P("rays", "views"),
        P("rays", None),
        P("rays", None),
        P("rays"),
        P(),
    )
    return jax.shard_map(
        body,
        mesh=mesh,
        in_specs=placed,
        out_specs=(P(), P("rays"), P("rays"), P("rays")),
        check_vma=False,
    )
```

```python
import jax
import jax.numpy as jnp
from jax import lax
from jax.experimental import pallas as pl
from jax.experimental.pallas import tpu as pltpu
from jax.sharding import PartitionSpec as P


F32 = jnp.float32
BF16 = jnp.bfloat16
SEEN_VIEWS = 10
CHANNELS = 35
STRIP = 40
BAND = 32
SEEN_SHIFT = 14
SEEN_BIT = 1 << SEEN_SHIFT
GATHER_TILE = 768
RAY = 192
CHUNK = 2 * RAY
PASSES = 1
TILE = 128
MOMENT_DECAY = 0.5
SQUARE_DECAY = 0.5
LEARNING_RATE = 0.05
WEIGHT_DECAY = 0.01
EPSILON = 1e-08
NN = (((1,), (0,)), ((), ()))
NT = (((1,), (1,)), ((), ()))
TN = (((0,), (0,)), ((), ()))


def dot(left, right, dims=NN):
    return lax.dot_general(left, right, dims, preferred_element_type=F32)


def parts(value, count):
    out = []
    for step in range(count):
        piece = value.astype(BF16)
        out.append(piece)
        if step + 1 < count:
            value = value - piece.astype(F32)
    return out


def dot_left(value, right, dims, count=PASSES):
    return sum(dot(piece, right, dims) for piece in parts(value, count))


def dot_right(left, value, dims, count=PASSES):
    return sum(dot(left, piece, dims) for piece in parts(value, count))


def elu_pair(value):
    slope = jnp.exp(jnp.minimum(value, 0.0))
    return jnp.maximum(value, 0.0) + (slope - 1.0), slope


def iota(shape, axis):
    return lax.broadcasted_iota(jnp.int32, shape, axis)


def table_rows(blocks):
    return BAND * blocks + 16 * (-(-blocks // 4))


def stack_maps(map_ref, stacked, view):
    channels, pixels = map_ref.shape[1:]
    blocks = pixels // 256
    blank = jnp.zeros((4, 256), F32)
    for block in range(blocks):
        lanes = slice(256 * block, 256 * (block + 1))
        stacked[view, BAND * block : BAND * (block + 1), :] = map_ref[view, 0:BAND, lanes]
    for first in range(0, blocks, 4):
        strips = []
        for block in range(first, first + 4):
            if block < blocks:
                lanes = slice(256 * block, 256 * (block + 1))
                strips.append(map_ref[view, BAND:channels, lanes].astype(F32))
                strips.append(blank[: BAND + 4 - channels])
            else:
                strips.append(blank)
        at = BAND * blocks + 4 * first
        stacked[view, at : at + 16, :] = jnp.concatenate(strips, axis=0).astype(BF16)


def gather_kernel(views, tile, count, *refs):
    packed_refs, source = refs[1 : 1 + count], refs[1 + count]
    outs, stacked = refs[2 + count : -1], refs[-1]
    blocks = source.shape[2] // 256

    @pl.when(pl.program_id(0) == 0)
    def _():
        for view in range(views):
            stack_maps(source, stacked, view)

    row = iota((8, tile), 0)
    upper = jnp.where(row < 4, 0, 1)
    for packed_ref, out_ref in zip(packed_refs, outs):
        strips = []
        for view in range(views):
            packed = packed_ref[view : view + 1, :]
            index = packed & (SEEN_BIT - 1)
            high = jnp.broadcast_to(index >> 8, (8, tile))
            low = jnp.broadcast_to(index & 255, (256, tile))
            picked = (iota((256, tile), 0) == low).astype(F32).astype(BF16)
            found = dot(stacked[view], picked)
            totals = [jnp.zeros((8, tile), F32)] * (BAND // 8)
            for block in range(blocks):
                here = high == block
                for part in range(BAND // 8):
                    at = BAND * block + 8 * part
                    totals[part] = jnp.where(here, found[at : at + 8], totals[part])
            last = jnp.zeros((8, tile), F32)
            half = high - upper
            for pair in range(-(-blocks // 2)):
                at = BAND * blocks + 8 * pair
                last = jnp.where(half == 2 * pair, found[at : at + 8], last)
            last = last + pltpu.roll(last, 4, 0)
            seen = jnp.broadcast_to((packed >> SEEN_SHIFT).astype(F32), (8, tile))
            last = jnp.where(row == CHANNELS - BAND, 1.0, last)
            last = jnp.where(row == CHANNELS - BAND + 1, seen, last)
            strips += totals + [jnp.where(row > CHANNELS - BAND + 1, 0.0, last)]
        out_ref[0] = jnp.concatenate(strips, axis=0).astype(BF16)


def gather_rows(packed, source, me, group, ways):
    views, points = packed.shape
    tile = GATHER_TILE
    own = points // group
    tiles = own // tile
    count = len(ways)
    part = lambda k: pl.BlockSpec((views, tile), lambda t, me: (0, (me[0] ^ k) * tiles + t))
    whole = lambda shape: pl.BlockSpec(shape, lambda t, me: (0, 0, 0))
    outs = [jax.ShapeDtypeStruct((1, views * STRIP, own), BF16)] * count
    out_specs = [pl.BlockSpec((1, views * STRIP, tile), lambda t, me: (0, 0, t))] * count
    table = (views, table_rows(source.shape[2] // 256), 256)
    flops = 2 * views * own * count * table[1] * 256
    return pl.pallas_call(
        lambda *refs: gather_kernel(views, tile, count, *refs),
        out_shape=outs,
        grid_spec=pltpu.PrefetchScalarGridSpec(
            num_scalar_prefetch=1,
            grid=(tiles,),
            in_specs=[part(k) for k in ways] + [whole(source.shape)],
            out_specs=out_specs,
            scratch_shapes=[pltpu.VMEM(table, BF16)],
        ),
        compiler_params=pltpu.CompilerParams(vmem_limit_bytes=32 * 1024 * 1024),
        cost_estimate=pl.CostEstimate(
            flops=flops, bytes_accessed=source.size * 2, transcendentals=0
        ),
    )(me, *([packed] * count), source)


def roll(value, shift):
    return pltpu.roll(value, shift % 128, 1)


def unpack(a_ref, r64, r32, r16):
    for b in range(2):
        r64[pl.ds(b, 18, stride=2), :] = roll(a_ref[0:18, :], -64 * b)
    for b in range(4):
        r32[pl.ds(b, 33, stride=4), :] = roll(a_ref[18:51, :], -32 * b)
    for b in range(8):
        r16[pl.ds(b, 39, stride=8), :] = roll(a_ref[50:89, :], -16 * b)


def assemble(place, shard, shard_refs, a_ref):
    a_ref[...] = jnp.zeros_like(a_ref)
    shards, rows, _ = shard_refs.shape
    for k in range(shards):
        start = (place ^ k) * shard
        shift = start & 127
        value = pltpu.roll(shard_refs[k].astype(F32), shift, 1)
        keep = iota((rows, 128), 1) >= shift
        first = start >> 7
        a_ref[pl.ds(first, rows), :] += jnp.where(keep, value, 0.0)
        a_ref[pl.ds(first + 1, rows), :] += jnp.where(keep, 0.0, value)


def repeat(weight, out_ref, times):
    out_ref[...] = jnp.zeros_like(out_ref)
    rows, width = weight.shape
    wide = widen(weight)
    for part in range(times):
        tile, shift = divmod(width * part, 128)
        out_ref[rows * part : rows * (part + 1), 128 * tile : 128 * (tile + 1)] = roll(
            wide, shift
        ).astype(BF16)


def blocks_sum(ref, rows, width, times):
    total = sum(
        roll(ref[rows * part : rows * (part + 1), :], -width * part) for part in range(times)
    )
    return jnp.where(iota((rows, 128), 1) < width, total, 0.0)


def column(rows):
    return rows.T[:, 0:1]


def main_kernel(views, shard, me_ref, *refs):
    shard_refs, refs = refs[0], refs[1:]
    (
    x0,
    x1,
    x2,
    x3,
    delta_ref,
    target_ref,
    weight_ref,
    out_ref,
    sums_ref,
    a_ref,
    r64,
    r32,
    r16,
    xs,
    hb,
    he,
    ff,
    fe,
    jb,
    ib,
    ie,
    ee,
    dl,
    di,
    df,
    dh,
    blk,
    w2t_s,
    w2_s,
    u1t_s,
    u1_s,
    u2t_s,
    u2_s,
    tri_s,
    g64,
    g32,
    g16,
    gw1,
    gw2,
    gu1,
    gu2,
    gb2,
    gc1,
    gc2,
    gd1,
    gs2,
    gdd,
    loss_s,
    ) = refs
    step = pl.program_id(0)
    n = CHUNK
    lane = iota((1, n), 1)
    first_ray = lane < RAY
    me = me_ref[0]

    @pl.when(step == 0)
    def _():
        assemble(me_ref[1], shard, shard_refs, a_ref)
        unpack(a_ref, r64, r32, r16)
        for ref in (g64, g32, g16, gw1, gw2, gu1, gu2, gb2, gc1, gc2, gd1, gs2, gdd, loss_s):
            ref[...] = jnp.zeros_like(ref)
        before = (iota((n, n), 0) < iota((n, n), 1)) & (
            (iota((n, n), 0) < RAY) == (iota((n, n), 1) < RAY)
        )
        tri_s[...] = before.astype(F32).astype(BF16)
        w1t = jnp.where(iota((64, 128), 1) < 36, 1.0, 0.0) * jnp.concatenate(
            [r64[0:36, :], jnp.zeros((92, 128), F32)], axis=0
        ).T[:64]
        for view in range(views):
            blk[64 * view : 64 * (view + 1), :] = roll(w1t, STRIP * view).astype(BF16)
        w2 = r32[0:64, :][:, :32]
        u1a = r32[65:97, :][:, :32]
        u2 = r16[4:36, :][:, :16]
        repeat(w2.T, w2t_s, views)
        repeat(w2, w2_s, views)
        repeat(u1a.T, u1t_s, views)
        repeat(u1a, u1_s, views)
        repeat(u2.T, u2t_s, views)
        repeat(u2, u2_s, views)

    for k, ref in enumerate((x0, x1, x2, x3)):
        xs[me ^ k] = ref[0]

    b2 = column(r32[64:72, :])[:32]
    u1b = r32[97:129, :][:, :32]
    u1bt = u1b.T.astype(BF16)
    u1b = u1b.astype(BF16)
    c1 = column(r32[129:137, :])[:32]
    c2 = column(r16[36:44, :])[:16]
    keep16 = iota((48, 128), 1) < 16
    qkv = sum(
        roll(jnp.where(keep16, r16[pl.ds(37 + a, 48, stride=4), :], 0.0), 16 * a) for a in range(4)
    )
    wq, wk, wv = qkv[0:16], qkv[16:32], qkv[32:48]
    wqb = wq[:, :64].astype(BF16)
    wqt = wq[:, :64].T.astype(BF16)
    wk_of = [roll(wk, 64 * r).astype(BF16) for r in range(2)]
    wv_of = [roll(wv, 64 * r).astype(BF16) for r in range(2)]
    wo = r16[229:293, :][:, :16]
    wob = wo.astype(BF16)
    wot = wo.T.astype(BF16)
    s1 = r16[293:309, :][:, :16]
    s1b = s1.astype(BF16)
    s1t = s1.T.astype(BF16)
    d1 = column(r16[309:317, :])[:16]
    s2 = column(r16[310:318, :])[:16]
    d2 = r16[311:312, 0:1]

    def strip_of(group, local, lanes):
        at = STRIP * local + 32
        strip = xs[group, at : at + 8, lanes].astype(F32)
        return strip[0:3], strip[4:5]

    def stack(values):
        return jnp.concatenate(values, axis=0) if len(values) > 1 else values[0]

    def cut(value, rows, local):
        return value[rows * local : rows * (local + 1)]

    counts = [min(views, SEEN_VIEWS - at) for at in range(0, SEEN_VIEWS, views)]

    m = TILE
    lane_tiles = [slice(at, at + m) for at in range(0, n, m)]
    join = lambda values: jnp.concatenate(values, axis=1) if len(values) > 1 else values[0]

    def forward_tile(lanes):
        sum1 = jnp.zeros((32, m), F32)
        sum2 = jnp.zeros((32, m), F32)
        seen = jnp.zeros((1, m), F32)
        for group, count in enumerate(counts):
            wide, thin = 64 * count, 32 * count
            value, slope = elu_pair(dot(blk[0:wide, 0 : views * STRIP], xs[group, :, lanes]))
            hidden = value.astype(BF16)
            hb[group, 0:wide, lanes] = hidden
            he[group, 0:wide, lanes] = slope
            value, slope = elu_pair(dot(w2t_s[0:thin, 0:wide], hidden) + stack([b2] * count))
            ff[group, 0:thin, lanes] = value
            fe[group, 0:thin, lanes] = slope
            for local in range(count):
                vis = strip_of(group, local, lanes)[1]
                one = cut(value, 32, local)
                part = vis * one
                sum1 = sum1 + part
                sum2 = sum2 + part * one
                seen = seen + vis
        average = sum1 / seen
        variance = sum2 / seen - average * average
        variance_low = variance.astype(BF16)
        shared = dot(u1bt, variance_low) + c1
        num = jnp.zeros((16, m), F32)
        den = jnp.zeros((16, m), F32)
        col = jnp.zeros((3, m), F32)
        for group, count in enumerate(counts):
            thin, low = 32 * count, 16 * count
            feature = ff[group, 0:thin, lanes]
            joined = (feature - stack([average] * count)).astype(BF16)
            jb[group, 0:thin, lanes] = joined
            value, slope = elu_pair(dot(u1t_s[0:thin, 0:thin], joined) + stack([shared] * count))
            inner = value.astype(BF16)
            ib[group, 0:thin, lanes] = inner
            ie[group, 0:thin, lanes] = slope
            raw = jnp.exp(dot(u2t_s[0:low, 0:thin], inner) + stack([c2] * count))
            for local in range(count):
                rgb, vis = strip_of(group, local, lanes)
                e = vis * cut(raw, 16, local)
                ee[group, 16 * local : 16 * (local + 1), lanes] = e
                num = num + e * feature[32 * local : 32 * local + 16]
                den = den + e
                col = col + e[0:1] * rgb
        return average, 1.0 / seen, variance_low, num, den, col

    done = [forward_tile(lanes) for lanes in lane_tiles]
    average, inv_seen, variance_low, num, den, col = [join(list(x)) for x in zip(*done)]

    inv = 1.0 / den
    tokens = num / den
    colour = col / den[0:1]
    token_low = tokens.astype(BF16)
    token_t = tokens.T.astype(BF16)
    halves = [token_t[RAY * r : RAY * (r + 1)] for r in range(2)]
    query = dot(wqt, token_low).astype(BF16).astype(F32) * 0.25
    kk_f = dot(halves[0], wk_of[0]) + dot(halves[1], wk_of[1])
    vv_f = dot(halves[0], wv_of[0]) + dot(halves[1], wv_of[1])
    kk = kk_f.astype(BF16)
    vv = vv_f.astype(BF16)
    kkt = kk.astype(F32).T.astype(BF16)
    vvt = vv.astype(F32).T.astype(BF16)

    def spread(value, head):
        mine = value[16 * head : 16 * (head + 1)].astype(F32)
        one = jnp.where(first_ray, mine, 0.0)
        rows = []
        for part in (one, mine - one):
            rows += [jnp.zeros((16 * head, n), BF16)] if head else []
            rows.append(part.astype(BF16))
            rows += [jnp.zeros((48 - 16 * head, n), BF16)] if head < 3 else []
        return jnp.concatenate(rows, axis=0)

    def fold(value):
        return jnp.where(first_ray, value[:16], value[16:])

    def head_rows(value, head):
        at = 16 * head
        return jnp.concatenate([value[at : at + 16], value[64 + at : 80 + at]], axis=0)

    probs = []
    lows = []
    attended = []
    query_of = []
    for head in range(4):
        q_head = spread(query, head)
        query_of.append(q_head)
        tiles = []
        for at in range(0, n, 128):
            score = dot(kk, q_head[:, at : at + 128])
            score = jnp.exp(score - jnp.max(score, axis=0, keepdims=True))
            tiles.append(score * (1.0 / jnp.sum(score, axis=0, keepdims=True)))
        probs.append(tiles)
        low = jnp.concatenate([tile.astype(BF16) for tile in tiles], axis=1)
        lows.append(low)
        attended.append(fold(dot(head_rows(vvt, head), low)))
    raw_attended = attended
    attended = jnp.concatenate(attended, axis=0).astype(BF16)
    mixed = tokens + dot(wot, attended)
    mixed_low = mixed.astype(BF16)
    value, s_slope = elu_pair(dot(s1t, mixed_low) + d1)
    act = value.astype(BF16).astype(F32)
    z = jnp.sum(act * s2, axis=0, keepdims=True) + d2
    delta = delta_ref[0]
    ez = jnp.exp(-jnp.abs(z))
    density = jnp.maximum(z, 0.0) + jnp.log1p(ez)
    sigmoid = jnp.where(z >= 0.0, 1.0, ez) / (1.0 + ez)
    optical = density * delta
    tri = tri_s[...]

    def exact_rows(value):
        pad = jnp.zeros((13, n), F32)
        return jnp.concatenate([p.astype(F32) for p in parts(value, 3)] + [pad], axis=0).astype(BF16)

    before = jnp.sum(dot(exact_rows(optical), tri), axis=0, keepdims=True)
    through = jnp.exp(-before)
    gone = jnp.exp(-optical)
    render = through * (1.0 - gone)
    drawn = render * colour
    targets = target_ref[0]
    rweight = weight_ref[0]
    d_pixel = jnp.zeros((3, n), F32)
    loss = jnp.zeros((1, 1), F32)
    for r in range(2):
        mask = first_ray if r == 0 else jnp.logical_not(first_ray)
        pixel = jnp.sum(jnp.where(mask, drawn, 0.0), axis=1, keepdims=True)
        miss = pixel - targets[0:3, r : r + 1]
        scale = rweight[0:1, r : r + 1]
        loss = loss + scale * jnp.sum(miss * miss, axis=0, keepdims=True)
        d_pixel = d_pixel + jnp.where(mask, 2.0 * scale * miss, 0.0)
    place = iota((8, 128), 1) + 128 * iota((8, 128), 0)
    loss_s[...] += jnp.where(place == 0, loss, 0.0) + jnp.where(
        place == 1, rweight[0:1, 0:1] + rweight[0:1, 1:2], 0.0
    )

    d_render = jnp.sum(d_pixel * colour, axis=0, keepdims=True)
    d_colour = d_pixel * render
    d_before = -render * d_render
    d_optical = through * gone * d_render + jnp.sum(
        dot(exact_rows(d_before), tri, NT), axis=0, keepdims=True
    )
    dz = d_optical * delta * sigmoid
    gs2[...] += act * dz
    gdd[...] += jnp.where(iota((8, n), 0) == 0, dz, 0.0)
    d_pre = s2 * dz * s_slope
    gd1[...] += d_pre
    g16[293:309, :] += widen(dot_right(mixed_low, d_pre, NT))
    d_mixed = dot_right(s1b, d_pre, NN)
    g16[229:293, :] += widen(dot_right(attended, d_mixed, NT))
    d_att = dot_right(wob, d_mixed, NN)
    d_query = []
    d_kk = jnp.zeros((RAY, 128), F32)
    d_vv = jnp.zeros((RAY, 128), F32)
    for head in range(4):
        mine = d_att[16 * head : 16 * (head + 1)]
        shift = jnp.sum(mine * raw_attended[head], axis=0, keepdims=True)
        d_head = spread(d_att, head)
        d_vv = d_vv + dot(lows[head], d_head, NT)
        tiles = []
        for place, prob in enumerate(probs[head]):
            at = slice(128 * place, 128 * (place + 1))
            tiles.append((prob * (dot(vv, d_head[:, at]) - shift[:, at])).astype(BF16))
        d_score = jnp.concatenate(tiles, axis=1)
        d_query.append(fold(dot(head_rows(kkt, head), d_score)) * 0.25)
        d_kk = d_kk + dot(d_score, query_of[head], NT)
    d_query = jnp.concatenate(d_query, axis=0)
    gq = dot_right(token_low, d_query, NT)
    gk = [dot_right(halves[r], d_kk, TN) for r in range(2)]
    gv = [dot_right(halves[r], d_vv, TN) for r in range(2)]
    wide = jnp.concatenate([widen(gq), gk[0] + roll(gk[1], 64), gv[0] + roll(gv[1], 64)], axis=0)
    for a in range(4):
        at = pl.ds(37 + a, 48, stride=4)
        g16[at, :] += jnp.where(keep16, roll(wide, -16 * a), 0.0)
    d_halves = [
        dot_left(d_kk, wk_of[r], NT) + dot_left(d_vv, wv_of[r], NT) for r in range(2)
    ]
    d_tokens = d_mixed + dot_right(wqb, d_query, NN) + jnp.concatenate(d_halves, axis=0).T
    d_num = d_tokens * inv
    d_den = -d_num * tokens
    d_col = d_colour * inv[0:1]
    d_den0 = -jnp.sum(d_col * colour, axis=0, keepdims=True)
    row16 = iota((16, n), 0)
    d_den = d_den + jnp.where(row16 == 0, d_den0, 0.0)

    def backward_tile(lanes):
        own_num, own_den, own_col = d_num[:, lanes], d_den[:, lanes], d_col[:, lanes]
        d_average = jnp.zeros((32, m), F32)
        d_shared = jnp.zeros((32, m), F32)
        sum_c2 = jnp.zeros((16, m), F32)
        for group, count in enumerate(counts):
            thin, low = 32 * count, 16 * count
            d_logit = []
            for local in range(count):
                at = slice(16 * local, 16 * (local + 1))
                rgb, _ = strip_of(group, local, lanes)
                e = ee[group, at, lanes]
                d_e = own_num * ff[group, 32 * local : 32 * local + 16, lanes] + own_den
                shade = jnp.sum(own_col * rgb, axis=0, keepdims=True)
                d_e = d_e + jnp.where(row16[:, :m] == 0, shade, 0.0)
                d_logit.append(d_e * e)
                sum_c2 = sum_c2 + d_logit[-1]
                ee[group, at, lanes] = own_num * e
            piece = stack(d_logit).astype(BF16)
            dl[group, 0:low, lanes] = piece
            d_inner = dot(u2_s[0:thin, 0:low], piece) * ie[group, 0:thin, lanes]
            piece = d_inner.astype(BF16)
            di[group, 0:thin, lanes] = piece
            d_joined = dot(u1_s[0:thin, 0:thin], piece)
            ie[group, 0:thin, lanes] = d_joined
            for local in range(count):
                d_shared = d_shared + cut(d_inner, 32, local)
                d_average = d_average - cut(d_joined, 32, local)
        shared_low = d_shared.astype(BF16)
        d_variance = dot(u1b, shared_low)
        gc1[:, lanes] += d_shared
        gc2[:, lanes] += sum_c2
        d_square = d_variance * inv_seen[:, lanes]
        d_sum = (d_average - 2.0 * average[:, lanes] * d_variance) * inv_seen[:, lanes]
        sum_b2 = jnp.zeros((32, m), F32)
        for group, count in enumerate(counts):
            wide, thin = 64 * count, 32 * count
            d_feature = []
            for local in range(count):
                at = slice(32 * local, 32 * (local + 1))
                vis = strip_of(group, local, lanes)[1]
                feature = ff[group, at, lanes]
                d_one = ie[group, at, lanes] + vis * (d_sum + 2.0 * feature * d_square)
                kept = ee[group, 16 * local : 16 * (local + 1), lanes]
                d_one = jnp.concatenate([d_one[:16] + kept, d_one[16:]], axis=0)
                d_one = d_one * fe[group, at, lanes]
                sum_b2 = sum_b2 + d_one
                d_feature.append(d_one)
            piece = stack(d_feature).astype(BF16)
            df[group, 0:thin, lanes] = piece
            d_hidden = dot(w2_s[0:wide, 0:thin], piece) * he[group, 0:wide, lanes]
            dh[group, 0:wide, lanes] = d_hidden.astype(BF16)
        gb2[:, lanes] += sum_b2
        return shared_low

    shared_low = join([backward_tile(lanes) for lanes in lane_tiles])
    g32[97:129, :] += widen(dot(variance_low, shared_low, NT))
    for group, count in enumerate(counts):
        wide, thin, low = 64 * count, 32 * count, 16 * count
        gu2[0:thin, 0:low] += dot(ib[group, 0:thin], dl[group, 0:low], NT)
        gu1[0:thin, 0:thin] += dot(jb[group, 0:thin], di[group, 0:thin], NT)
        gw2[0:wide, 0:thin] += dot(hb[group, 0:wide], df[group, 0:thin], NT)
        gw1[:, 0:wide] += dot(xs[group], dh[group, 0:wide], NT)

    @pl.when(step == pl.num_programs(0) - 1)
    def _():
        ones = jnp.ones((8, n), BF16)
        row_of = lambda ref: widen(dot_right(ones, ref[...], NT, 3)[0:1])
        g32[0:64, :] = blocks_sum(gw2, 64, 32, views)
        g32[65:97, :] = blocks_sum(gu1, 32, 32, views)
        g16[4:36, :] = blocks_sum(gu2, 32, 16, views)
        g32[64:65, :] = row_of(gb2)
        g32[129:130, :] = row_of(gc1)
        g16[36:37, :] = row_of(gc2)
        g16[309:310, :] = row_of(gd1)
        g16[310:311, :] = row_of(gs2)
        g16[311:312, :] = jnp.where(iota((1, 128), 1) == 0, row_of(gdd), 0.0)
        total = gw1[0:36, 0:128]
        total = total + roll(gw1[STRIP : STRIP + 36, 0:128], 64)
        total = total + gw1[2 * STRIP : 2 * STRIP + 36, 128:256]
        g64[0:36, :] = jnp.where(iota((36, 128), 1) < 64, total, 0.0)
        out_ref[...] = jnp.zeros_like(out_ref)
        out_ref[0:18, :] = sum(roll(g64[pl.ds(b, 18, stride=2), :], 64 * b) for b in range(2))
        out_ref[18:51, :] += sum(roll(g32[pl.ds(b, 33, stride=4), :], 32 * b) for b in range(4))
        out_ref[50:89, :] += sum(roll(g16[pl.ds(b, 39, stride=8), :], 16 * b) for b in range(8))
        sums_ref[...] = jnp.where(
            iota(sums_ref.shape, 1) == 0, loss_s[0:1, 0:1], loss_s[0:1, 1:2]
        )


def widen(value):
    rows, width = value.shape
    return jnp.concatenate([value, jnp.zeros((rows, 128 - width), F32)], axis=1)


def run_main(me, blocks, pieces, shard, deltas, targets, ray_weight):
    rows, points = blocks[0].shape[1:]
    views = rows // STRIP
    n = CHUNK
    steps = points // n
    shards = pieces.shape[0]
    sums = (shards, -(-(shard + 2) // 128) * 128)
    whole = deltas.shape[0] // 2
    pairs = deltas.reshape(whole, 1, n)
    target_pairs = jnp.pad(
        targets.reshape(whole, 2, 3).transpose(0, 2, 1), ((0, 0), (0, 5), (0, 126))
    )
    weight_pairs = jnp.pad(ray_weight.reshape(whole, 1, 2), ((0, 0), (0, 7), (0, 126)))
    vm = pltpu.VMEM
    own = lambda t, me: (me[0] * steps + t, 0, 0)
    block = pl.BlockSpec((1, rows, n), lambda t, me: (0, 0, t))
    piece = pl.BlockSpec(pieces.shape, lambda t, me: (0, 0, 0))
    return pl.pallas_call(
        lambda *refs: main_kernel(views, shard, *refs),
        out_shape=[
            jax.ShapeDtypeStruct((96, 128), F32),
            jax.ShapeDtypeStruct(sums, F32),
        ],
        grid_spec=pltpu.PrefetchScalarGridSpec(
            num_scalar_prefetch=1,
            grid=(steps,),
            in_specs=[piece]
            + [block] * 4
            + [
                pl.BlockSpec((1, 1, n), own),
                pl.BlockSpec((1, 8, 128), own),
                pl.BlockSpec((1, 8, 128), own),
            ],
            out_specs=[
                pl.BlockSpec((96, 128), lambda t, me: (0, 0)),
                pl.BlockSpec(sums, lambda t, me: (0, 0)),
            ],
            scratch_shapes=[
                vm((120, 128), F32),
                vm((40, 128), F32),
                vm((144, 128), F32),
                vm((320, 128), F32),
                vm((4, rows, n), BF16),
                vm((4, 64 * views, n), BF16),
                vm((4, 64 * views, n), F32),
                vm((4, 32 * views, n), F32),
                vm((4, 32 * views, n), F32),
                vm((4, 32 * views, n), BF16),
                vm((4, 32 * views, n), BF16),
                vm((4, 32 * views, n), F32),
                vm((4, 16 * views, n), F32),
                vm((4, 16 * views, n), BF16),
                vm((4, 32 * views, n), BF16),
                vm((4, 32 * views, n), BF16),
                vm((4, 64 * views, n), BF16),
                vm((64 * views, 128), BF16),
                vm((32 * views, 256), BF16),
                vm((64 * views, 128), BF16),
                vm((32 * views, 128), BF16),
                vm((32 * views, 128), BF16),
                vm((16 * views, 128), BF16),
                vm((32 * views, 128), BF16),
                vm((n, n), BF16),
                vm((40, 128), F32),
                vm((136, 128), F32),
                vm((312, 128), F32),
                vm((rows, 256), F32),
                vm((64 * views, 128), F32),
                vm((32 * views, 128), F32),
                vm((32 * views, 128), F32),
                vm((32, n), F32),
                vm((32, n), F32),
                vm((16, n), F32),
                vm((16, n), F32),
                vm((16, n), F32),
                vm((8, n), F32),
                vm((8, 128), F32),
            ],
        ),
        compiler_params=pltpu.CompilerParams(vmem_limit_bytes=48 * 1024 * 1024),
    )(me, pieces, *blocks, pairs, target_pairs, weight_pairs)


def adamw(master, first_moment, second_moment, gradient, step_count):
    step_float = step_count[0].astype(F32)
    first_new = MOMENT_DECAY * first_moment + (1.0 - MOMENT_DECAY) * gradient
    second_new = SQUARE_DECAY * second_moment + (1.0 - SQUARE_DECAY) * gradient * gradient
    first_fix = 1.0 - jnp.power(MOMENT_DECAY, step_float)
    second_fix = 1.0 - jnp.power(SQUARE_DECAY, step_float)
    update = first_new / first_fix / (jnp.sqrt(second_new / second_fix) + EPSILON)
    master_new = master - LEARNING_RATE * (update + WEIGHT_DECAY * master)
    return (master_new, first_new, second_new)


def body(
    master,
    first_moment,
    second_moment,
    step_count,
    feature_maps,
    pixel_index,
    visible,
    deltas,
    targets,
    scene_id,
    scene_weight,
):
    group = lax.axis_size("views")
    shards = lax.axis_size("rays")
    assert feature_maps.shape[2] <= SEEN_BIT
    shard = master.shape[0]
    spots = [lax.axis_index("views"), lax.axis_index("rays")]
    me = jnp.stack(spots).astype(jnp.int32)
    swap = lambda size, k: [(i, i ^ k) for i in range(size)]
    rows = -(-shard // 2048) * 16
    piece = jnp.pad(master.astype(BF16), (0, rows * 128 - shard)).reshape(rows, 128)
    packed = pixel_index.T + (visible.T << SEEN_SHIFT)
    held = piece[None]
    links = shards.bit_length() - 1
    for link in range(links):
        held = jnp.concatenate([held, lax.ppermute(held, "rays", swap(shards, 1 << link))])
    far = gather_rows(packed, feature_maps, me, group, (3, 2))
    three = lax.ppermute(far[0], "views", swap(group, 3))
    two = lax.ppermute(far[1], "views", swap(group, 2))
    near = gather_rows(packed, feature_maps, me, group, (1,))
    one = lax.ppermute(near[0], "views", swap(group, 1))
    mine = gather_rows(packed, feature_maps, me, group, (0,))
    hits = (scene_id[:, None] == jnp.arange(scene_weight.shape[0])[None, :]).astype(F32)
    ray_weight = jnp.sum(hits * scene_weight.astype(F32)[None, :], axis=1)
    result, sums = run_main(me, [mine[0], one, two, three], held, shard, deltas, targets, ray_weight)
    summed = result[:89].reshape(-1)
    size = shards * shard
    if summed.shape[0] < size:
        summed = jnp.pad(summed, (0, size - summed.shape[0]))
    loss_at, far_at = shard, shard + 1
    send = jnp.concatenate([summed[:size].reshape(shards, shard), sums], axis=1)
    got = lax.all_to_all(send, "rays", 0, 0, tiled=True)
    partial = jnp.sum(got, axis=0)
    whole = partial
    for k in range(1, group):
        whole = whole + lax.ppermute(partial, "views", [(i, i ^ k) for i in range(group)])
    scaled = whole[: shard + 1] / whole[far_at : far_at + shard + 1]
    loss = scaled[loss_at]
    gradient = scaled[:shard]
    return (loss, *adamw(master, first_moment, second_moment, gradient, step_count))


def solution(mesh):
    placed = (
        P("rays"),
        P("rays"),
        P("rays"),
        P(),
        P("views", None, None),
        P("rays", "views"),
        P("rays", "views"),
        P("rays", None),
        P("rays", None),
        P("rays"),
        P(),
    )
    return jax.shard_map(
        body,
        mesh=mesh,
        in_specs=placed,
        out_specs=(P(), P("rays"), P("rays"), P("rays")),
        check_vma=False,
    )
```

```python
import jax
import jax.numpy as jnp
from jax import lax
from jax.experimental import pallas as pl
from jax.experimental.pallas import tpu as pltpu
from jax.sharding import PartitionSpec as P


F32 = jnp.float32
BF16 = jnp.bfloat16
SEEN_VIEWS = 10
CHANNELS = 35
STRIP = 40
BAND = 32
SEEN_SHIFT = 14
SEEN_BIT = 1 << SEEN_SHIFT
GATHER_TILE = 768
RAY = 192
CHUNK = 2 * RAY
PASSES = 1
TILE = 128
MOMENT_DECAY = 0.5
SQUARE_DECAY = 0.5
LEARNING_RATE = 0.05
WEIGHT_DECAY = 0.01
EPSILON = 1e-08
NN = (((1,), (0,)), ((), ()))
NT = (((1,), (1,)), ((), ()))
TN = (((0,), (0,)), ((), ()))


def dot(left, right, dims=NN):
    return lax.dot_general(left, right, dims, preferred_element_type=F32)


def parts(value, count):
    out = []
    for step in range(count):
        piece = value.astype(BF16)
        out.append(piece)
        if step + 1 < count:
            value = value - piece.astype(F32)
    return out


def dot_left(value, right, dims, count=PASSES):
    return sum(dot(piece, right, dims) for piece in parts(value, count))


def dot_right(left, value, dims, count=PASSES):
    return sum(dot(left, piece, dims) for piece in parts(value, count))


def elu_pair(value):
    slope = jnp.exp(jnp.minimum(value, 0.0))
    return jnp.maximum(value, 0.0) + (slope - 1.0), slope


def iota(shape, axis):
    return lax.broadcasted_iota(jnp.int32, shape, axis)


def table_rows(blocks):
    return BAND * blocks + 16 * (-(-blocks // 4))


def stack_maps(map_ref, stacked, view):
    channels, pixels = map_ref.shape[1:]
    blocks = pixels // 256
    blank = jnp.zeros((4, 256), F32)
    for block in range(blocks):
        lanes = slice(256 * block, 256 * (block + 1))
        stacked[view, BAND * block : BAND * (block + 1), :] = map_ref[view, 0:BAND, lanes]
    for first in range(0, blocks, 4):
        strips = []
        for block in range(first, first + 4):
            if block < blocks:
                lanes = slice(256 * block, 256 * (block + 1))
                strips.append(map_ref[view, BAND:channels, lanes].astype(F32))
                strips.append(blank[: BAND + 4 - channels])
            else:
                strips.append(blank)
        at = BAND * blocks + 4 * first
        stacked[view, at : at + 16, :] = jnp.concatenate(strips, axis=0).astype(BF16)


def gather_kernel(views, tile, count, *refs):
    packed_refs, source = refs[1 : 1 + count], refs[1 + count]
    outs, stacked = refs[2 + count : -1], refs[-1]
    blocks = source.shape[2] // 256

    @pl.when(pl.program_id(0) == 0)
    def _():
        for view in range(views):
            stack_maps(source, stacked, view)

    row = iota((8, tile), 0)
    upper = jnp.where(row < 4, 0, 1)
    for packed_ref, out_ref in zip(packed_refs, outs):
        strips = []
        for view in range(views):
            packed = packed_ref[view : view + 1, :]
            index = packed & (SEEN_BIT - 1)
            high = jnp.broadcast_to(index >> 8, (8, tile))
            low = jnp.broadcast_to(index & 255, (256, tile))
            picked = (iota((256, tile), 0) == low).astype(F32).astype(BF16)
            found = dot(stacked[view], picked)
            totals = [jnp.zeros((8, tile), F32)] * (BAND // 8)
            for block in range(blocks):
                here = high == block
                for part in range(BAND // 8):
                    at = BAND * block + 8 * part
                    totals[part] = jnp.where(here, found[at : at + 8], totals[part])
            last = jnp.zeros((8, tile), F32)
            half = high - upper
            for pair in range(-(-blocks // 2)):
                at = BAND * blocks + 8 * pair
                last = jnp.where(half == 2 * pair, found[at : at + 8], last)
            last = last + pltpu.roll(last, 4, 0)
            seen = jnp.broadcast_to((packed >> SEEN_SHIFT).astype(F32), (8, tile))
            last = jnp.where(row == CHANNELS - BAND, 1.0, last)
            last = jnp.where(row == CHANNELS - BAND + 1, seen, last)
            strips += totals + [jnp.where(row > CHANNELS - BAND + 1, 0.0, last)]
        out_ref[0] = jnp.concatenate(strips, axis=0).astype(BF16)


def gather_rows(packed, source, me, group, ways):
    views, points = packed.shape
    tile = GATHER_TILE
    own = points // group
    tiles = own // tile
    count = len(ways)
    part = lambda k: pl.BlockSpec((views, tile), lambda t, me: (0, (me[0] ^ k) * tiles + t))
    whole = lambda shape: pl.BlockSpec(shape, lambda t, me: (0, 0, 0))
    outs = [jax.ShapeDtypeStruct((1, views * STRIP, own), BF16)] * count
    out_specs = [pl.BlockSpec((1, views * STRIP, tile), lambda t, me: (0, 0, t))] * count
    table = (views, table_rows(source.shape[2] // 256), 256)
    flops = 2 * views * own * count * table[1] * 256
    return pl.pallas_call(
        lambda *refs: gather_kernel(views, tile, count, *refs),
        out_shape=outs,
        grid_spec=pltpu.PrefetchScalarGridSpec(
            num_scalar_prefetch=1,
            grid=(tiles,),
            in_specs=[part(k) for k in ways] + [whole(source.shape)],
            out_specs=out_specs,
            scratch_shapes=[pltpu.VMEM(table, BF16)],
        ),
        compiler_params=pltpu.CompilerParams(vmem_limit_bytes=32 * 1024 * 1024),
        cost_estimate=pl.CostEstimate(
            flops=flops, bytes_accessed=source.size * 2, transcendentals=0
        ),
    )(me, *([packed] * count), source)


def roll(value, shift):
    return pltpu.roll(value, shift % 128, 1)


def unpack(a_ref, r64, r32, r16):
    for b in range(2):
        r64[pl.ds(b, 18, stride=2), :] = roll(a_ref[0:18, :], -64 * b)
    for b in range(4):
        r32[pl.ds(b, 33, stride=4), :] = roll(a_ref[18:51, :], -32 * b)
    for b in range(8):
        r16[pl.ds(b, 39, stride=8), :] = roll(a_ref[50:89, :], -16 * b)


def assemble(place, shard, shard_refs, a_ref):
    a_ref[...] = jnp.zeros_like(a_ref)
    shards, rows, _ = shard_refs.shape
    for k in range(shards):
        owner = sum(((k >> bit) & 1) * (shards >> (bit + 1)) for bit in range(shards.bit_length()))
        start = (place ^ owner) * shard
        shift = start & 127
        value = pltpu.roll(shard_refs[k].astype(F32), shift, 1)
        keep = iota((rows, 128), 1) >= shift
        first = start >> 7
        a_ref[pl.ds(first, rows), :] += jnp.where(keep, value, 0.0)
        a_ref[pl.ds(first + 1, rows), :] += jnp.where(keep, 0.0, value)


def repeat(weight, out_ref, times):
    out_ref[...] = jnp.zeros_like(out_ref)
    rows, width = weight.shape
    wide = widen(weight)
    for part in range(times):
        tile, shift = divmod(width * part, 128)
        out_ref[rows * part : rows * (part + 1), 128 * tile : 128 * (tile + 1)] = roll(
            wide, shift
        ).astype(BF16)


def blocks_sum(ref, rows, width, times):
    total = sum(
        roll(ref[rows * part : rows * (part + 1), :], -width * part) for part in range(times)
    )
    return jnp.where(iota((rows, 128), 1) < width, total, 0.0)


def column(rows):
    return rows.T[:, 0:1]


def main_kernel(views, shard, me_ref, *refs):
    shard_refs, refs = refs[0], refs[1:]
    (
    x0,
    x1,
    x2,
    x3,
    delta_ref,
    target_ref,
    weight_ref,
    out_ref,
    sums_ref,
    a_ref,
    r64,
    r32,
    r16,
    xs,
    hb,
    he,
    ff,
    fe,
    jb,
    ib,
    ie,
    ee,
    dl,
    di,
    df,
    dh,
    blk,
    w2t_s,
    w2_s,
    u1t_s,
    u1_s,
    u2t_s,
    u2_s,
    tri_s,
    g64,
    g32,
    g16,
    gw1,
    gw2,
    gu1,
    gu2,
    gb2,
    gc1,
    gc2,
    gd1,
    gs2,
    gdd,
    loss_s,
    ) = refs
    step = pl.program_id(0)
    n = CHUNK
    lane = iota((1, n), 1)
    first_ray = lane < RAY
    me = me_ref[0]

    @pl.when(step == 0)
    def _():
        assemble(me_ref[1], shard, shard_refs, a_ref)
        unpack(a_ref, r64, r32, r16)
        for ref in (g64, g32, g16, gw1, gw2, gu1, gu2, gb2, gc1, gc2, gd1, gs2, gdd, loss_s):
            ref[...] = jnp.zeros_like(ref)
        before = (iota((n, n), 0) < iota((n, n), 1)) & (
            (iota((n, n), 0) < RAY) == (iota((n, n), 1) < RAY)
        )
        tri_s[...] = before.astype(F32).astype(BF16)
        w1t = jnp.where(iota((64, 128), 1) < 36, 1.0, 0.0) * jnp.concatenate(
            [r64[0:36, :], jnp.zeros((92, 128), F32)], axis=0
        ).T[:64]
        for view in range(views):
            blk[64 * view : 64 * (view + 1), :] = roll(w1t, STRIP * view).astype(BF16)
        w2 = r32[0:64, :][:, :32]
        u1a = r32[65:97, :][:, :32]
        u2 = r16[4:36, :][:, :16]
        repeat(w2.T, w2t_s, views)
        repeat(w2, w2_s, views)
        repeat(u1a.T, u1t_s, views)
        repeat(u1a, u1_s, views)
        repeat(u2.T, u2t_s, views)
        repeat(u2, u2_s, views)

    for k, ref in enumerate((x0, x1, x2, x3)):
        xs[me ^ k] = ref[0]

    b2 = column(r32[64:72, :])[:32]
    u1b = r32[97:129, :][:, :32]
    u1bt = u1b.T.astype(BF16)
    u1b = u1b.astype(BF16)
    c1 = column(r32[129:137, :])[:32]
    c2 = column(r16[36:44, :])[:16]
    keep16 = iota((48, 128), 1) < 16
    qkv = sum(
        roll(jnp.where(keep16, r16[pl.ds(37 + a, 48, stride=4), :], 0.0), 16 * a) for a in range(4)
    )
    wq, wk, wv = qkv[0:16], qkv[16:32], qkv[32:48]
    wqb = wq[:, :64].astype(BF16)
    wqt = wq[:, :64].T.astype(BF16)
    wk_of = [roll(wk, 64 * r).astype(BF16) for r in range(2)]
    wv_of = [roll(wv, 64 * r).astype(BF16) for r in range(2)]
    wo = r16[229:293, :][:, :16]
    wob = wo.astype(BF16)
    wot = wo.T.astype(BF16)
    s1 = r16[293:309, :][:, :16]
    s1b = s1.astype(BF16)
    s1t = s1.T.astype(BF16)
    d1 = column(r16[309:317, :])[:16]
    s2 = column(r16[310:318, :])[:16]
    d2 = r16[311:312, 0:1]

    def strip_of(group, local, lanes):
        at = STRIP * local + 32
        strip = xs[group, at : at + 8, lanes].astype(F32)
        return strip[0:3], strip[4:5]

    def stack(values):
        return jnp.concatenate(values, axis=0) if len(values) > 1 else values[0]

    def cut(value, rows, local):
        return value[rows * local : rows * (local + 1)]

    counts = [min(views, SEEN_VIEWS - at) for at in range(0, SEEN_VIEWS, views)]

    m = TILE
    lane_tiles = [slice(at, at + m) for at in range(0, n, m)]
    join = lambda values: jnp.concatenate(values, axis=1) if len(values) > 1 else values[0]

    def forward_tile(lanes):
        sum1 = jnp.zeros((32, m), F32)
        sum2 = jnp.zeros((32, m), F32)
        seen = jnp.zeros((1, m), F32)
        for group, count in enumerate(counts):
            wide, thin = 64 * count, 32 * count
            value, slope = elu_pair(dot(blk[0:wide, 0 : views * STRIP], xs[group, :, lanes]))
            hidden = value.astype(BF16)
            hb[group, 0:wide, lanes] = hidden
            he[group, 0:wide, lanes] = slope
            value, slope = elu_pair(dot(w2t_s[0:thin, 0:wide], hidden) + stack([b2] * count))
            ff[group, 0:thin, lanes] = value
            fe[group, 0:thin, lanes] = slope
            for local in range(count):
                vis = strip_of(group, local, lanes)[1]
                one = cut(value, 32, local)
                part = vis * one
                sum1 = sum1 + part
                sum2 = sum2 + part * one
                seen = seen + vis
        average = sum1 / seen
        variance = sum2 / seen - average * average
        variance_low = variance.astype(BF16)
        shared = dot(u1bt, variance_low) + c1
        num = jnp.zeros((16, m), F32)
        den = jnp.zeros((16, m), F32)
        col = jnp.zeros((3, m), F32)
        for group, count in enumerate(counts):
            thin, low = 32 * count, 16 * count
            feature = ff[group, 0:thin, lanes]
            joined = (feature - stack([average] * count)).astype(BF16)
            jb[group, 0:thin, lanes] = joined
            value, slope = elu_pair(dot(u1t_s[0:thin, 0:thin], joined) + stack([shared] * count))
            inner = value.astype(BF16)
            ib[group, 0:thin, lanes] = inner
            ie[group, 0:thin, lanes] = slope
            raw = jnp.exp(dot(u2t_s[0:low, 0:thin], inner) + stack([c2] * count))
            for local in range(count):
                rgb, vis = strip_of(group, local, lanes)
                e = vis * cut(raw, 16, local)
                ee[group, 16 * local : 16 * (local + 1), lanes] = e
                num = num + e * feature[32 * local : 32 * local + 16]
                den = den + e
                col = col + e[0:1] * rgb
        return average, 1.0 / seen, variance_low, num, den, col

    done = [forward_tile(lanes) for lanes in lane_tiles]
    average, inv_seen, variance_low, num, den, col = [join(list(x)) for x in zip(*done)]

    inv = 1.0 / den
    tokens = num / den
    colour = col / den[0:1]
    token_low = tokens.astype(BF16)
    token_t = tokens.T.astype(BF16)
    halves = [token_t[RAY * r : RAY * (r + 1)] for r in range(2)]
    query = dot(wqt, token_low).astype(BF16).astype(F32) * 0.25
    kk_f = dot(halves[0], wk_of[0]) + dot(halves[1], wk_of[1])
    vv_f = dot(halves[0], wv_of[0]) + dot(halves[1], wv_of[1])
    kk = kk_f.astype(BF16)
    vv = vv_f.astype(BF16)
    kkt = kk.astype(F32).T.astype(BF16)
    vvt = vv.astype(F32).T.astype(BF16)

    def spread(value, head):
        mine = value[16 * head : 16 * (head + 1)].astype(F32)
        one = jnp.where(first_ray, mine, 0.0)
        rows = []
        for part in (one, mine - one):
            rows += [jnp.zeros((16 * head, n), BF16)] if head else []
            rows.append(part.astype(BF16))
            rows += [jnp.zeros((48 - 16 * head, n), BF16)] if head < 3 else []
        return jnp.concatenate(rows, axis=0)

    def fold(value):
        return jnp.where(first_ray, value[:16], value[16:])

    def head_rows(value, head):
        at = 16 * head
        return jnp.concatenate([value[at : at + 16], value[64 + at : 80 + at]], axis=0)

    probs = []
    lows = []
    attended = []
    query_of = []
    for head in range(4):
        q_head = spread(query, head)
        query_of.append(q_head)
        tiles = []
        for at in range(0, n, 128):
            score = dot(kk, q_head[:, at : at + 128])
            score = jnp.exp(score - jnp.max(score, axis=0, keepdims=True))
            tiles.append(score * (1.0 / jnp.sum(score, axis=0, keepdims=True)))
        probs.append(tiles)
        low = jnp.concatenate([tile.astype(BF16) for tile in tiles], axis=1)
        lows.append(low)
        attended.append(fold(dot(head_rows(vvt, head), low)))
    raw_attended = attended
    attended = jnp.concatenate(attended, axis=0).astype(BF16)
    mixed = tokens + dot(wot, attended)
    mixed_low = mixed.astype(BF16)
    value, s_slope = elu_pair(dot(s1t, mixed_low) + d1)
    act = value.astype(BF16).astype(F32)
    z = jnp.sum(act * s2, axis=0, keepdims=True) + d2
    delta = delta_ref[0]
    ez = jnp.exp(-jnp.abs(z))
    density = jnp.maximum(z, 0.0) + jnp.log1p(ez)
    sigmoid = jnp.where(z >= 0.0, 1.0, ez) / (1.0 + ez)
    optical = density * delta
    tri = tri_s[...]

    def exact_rows(value):
        pad = jnp.zeros((13, n), F32)
        return jnp.concatenate([p.astype(F32) for p in parts(value, 3)] + [pad], axis=0).astype(BF16)

    before = jnp.sum(dot(exact_rows(optical), tri), axis=0, keepdims=True)
    through = jnp.exp(-before)
    gone = jnp.exp(-optical)
    render = through * (1.0 - gone)
    drawn = render * colour
    targets = target_ref[0]
    rweight = weight_ref[0]
    d_pixel = jnp.zeros((3, n), F32)
    loss = jnp.zeros((1, 1), F32)
    for r in range(2):
        mask = first_ray if r == 0 else jnp.logical_not(first_ray)
        pixel = jnp.sum(jnp.where(mask, drawn, 0.0), axis=1, keepdims=True)
        miss = pixel - targets[0:3, r : r + 1]
        scale = rweight[0:1, r : r + 1]
        loss = loss + scale * jnp.sum(miss * miss, axis=0, keepdims=True)
        d_pixel = d_pixel + jnp.where(mask, 2.0 * scale * miss, 0.0)
    place = iota((8, 128), 1) + 128 * iota((8, 128), 0)
    loss_s[...] += jnp.where(place == 0, loss, 0.0) + jnp.where(
        place == 1, rweight[0:1, 0:1] + rweight[0:1, 1:2], 0.0
    )

    d_render = jnp.sum(d_pixel * colour, axis=0, keepdims=True)
    d_colour = d_pixel * render
    d_before = -render * d_render
    d_optical = through * gone * d_render + jnp.sum(
        dot(exact_rows(d_before), tri, NT), axis=0, keepdims=True
    )
    dz = d_optical * delta * sigmoid
    gs2[...] += act * dz
    gdd[...] += jnp.where(iota((8, n), 0) == 0, dz, 0.0)
    d_pre = s2 * dz * s_slope
    gd1[...] += d_pre
    g16[293:309, :] += widen(dot_right(mixed_low, d_pre, NT))
    d_mixed = dot_right(s1b, d_pre, NN)
    g16[229:293, :] += widen(dot_right(attended, d_mixed, NT))
    d_att = dot_right(wob, d_mixed, NN)
    d_query = []
    d_kk = jnp.zeros((RAY, 128), F32)
    d_vv = jnp.zeros((RAY, 128), F32)
    for head in range(4):
        mine = d_att[16 * head : 16 * (head + 1)]
        shift = jnp.sum(mine * raw_attended[head], axis=0, keepdims=True)
        d_head = spread(d_att, head)
        d_vv = d_vv + dot(lows[head], d_head, NT)
        tiles = []
        for place, prob in enumerate(probs[head]):
            at = slice(128 * place, 128 * (place + 1))
            tiles.append((prob * (dot(vv, d_head[:, at]) - shift[:, at])).astype(BF16))
        d_score = jnp.concatenate(tiles, axis=1)
        d_query.append(fold(dot(head_rows(kkt, head), d_score)) * 0.25)
        d_kk = d_kk + dot(d_score, query_of[head], NT)
    d_query = jnp.concatenate(d_query, axis=0)
    gq = dot_right(token_low, d_query, NT)
    gk = [dot_right(halves[r], d_kk, TN) for r in range(2)]
    gv = [dot_right(halves[r], d_vv, TN) for r in range(2)]
    wide = jnp.concatenate([widen(gq), gk[0] + roll(gk[1], 64), gv[0] + roll(gv[1], 64)], axis=0)
    for a in range(4):
        at = pl.ds(37 + a, 48, stride=4)
        g16[at, :] += jnp.where(keep16, roll(wide, -16 * a), 0.0)
    d_halves = [
        dot_left(d_kk, wk_of[r], NT) + dot_left(d_vv, wv_of[r], NT) for r in range(2)
    ]
    d_tokens = d_mixed + dot_right(wqb, d_query, NN) + jnp.concatenate(d_halves, axis=0).T
    d_num = d_tokens * inv
    d_den = -d_num * tokens
    d_col = d_colour * inv[0:1]
    d_den0 = -jnp.sum(d_col * colour, axis=0, keepdims=True)
    row16 = iota((16, n), 0)
    d_den = d_den + jnp.where(row16 == 0, d_den0, 0.0)

    def backward_tile(lanes):
        own_num, own_den, own_col = d_num[:, lanes], d_den[:, lanes], d_col[:, lanes]
        d_average = jnp.zeros((32, m), F32)
        d_shared = jnp.zeros((32, m), F32)
        sum_c2 = jnp.zeros((16, m), F32)
        for group, count in enumerate(counts):
            thin, low = 32 * count, 16 * count
            d_logit = []
            for local in range(count):
                at = slice(16 * local, 16 * (local + 1))
                rgb, _ = strip_of(group, local, lanes)
                e = ee[group, at, lanes]
                d_e = own_num * ff[group, 32 * local : 32 * local + 16, lanes] + own_den
                shade = jnp.sum(own_col * rgb, axis=0, keepdims=True)
                d_e = d_e + jnp.where(row16[:, :m] == 0, shade, 0.0)
                d_logit.append(d_e * e)
                sum_c2 = sum_c2 + d_logit[-1]
                ee[group, at, lanes] = own_num * e
            piece = stack(d_logit).astype(BF16)
            dl[group, 0:low, lanes] = piece
            d_inner = dot(u2_s[0:thin, 0:low], piece) * ie[group, 0:thin, lanes]
            piece = d_inner.astype(BF16)
            di[group, 0:thin, lanes] = piece
            d_joined = dot(u1_s[0:thin, 0:thin], piece)
            ie[group, 0:thin, lanes] = d_joined
            for local in range(count):
                d_shared = d_shared + cut(d_inner, 32, local)
                d_average = d_average - cut(d_joined, 32, local)
        shared_low = d_shared.astype(BF16)
        d_variance = dot(u1b, shared_low)
        gc1[:, lanes] += d_shared
        gc2[:, lanes] += sum_c2
        d_square = d_variance * inv_seen[:, lanes]
        d_sum = (d_average - 2.0 * average[:, lanes] * d_variance) * inv_seen[:, lanes]
        sum_b2 = jnp.zeros((32, m), F32)
        for group, count in enumerate(counts):
            wide, thin = 64 * count, 32 * count
            d_feature = []
            for local in range(count):
                at = slice(32 * local, 32 * (local + 1))
                vis = strip_of(group, local, lanes)[1]
                feature = ff[group, at, lanes]
                d_one = ie[group, at, lanes] + vis * (d_sum + 2.0 * feature * d_square)
                kept = ee[group, 16 * local : 16 * (local + 1), lanes]
                d_one = jnp.concatenate([d_one[:16] + kept, d_one[16:]], axis=0)
                d_one = d_one * fe[group, at, lanes]
                sum_b2 = sum_b2 + d_one
                d_feature.append(d_one)
            piece = stack(d_feature).astype(BF16)
            df[group, 0:thin, lanes] = piece
            d_hidden = dot(w2_s[0:wide, 0:thin], piece) * he[group, 0:wide, lanes]
            dh[group, 0:wide, lanes] = d_hidden.astype(BF16)
        gb2[:, lanes] += sum_b2
        return shared_low

    shared_low = join([backward_tile(lanes) for lanes in lane_tiles])
    g32[97:129, :] += widen(dot(variance_low, shared_low, NT))
    for group, count in enumerate(counts):
        wide, thin, low = 64 * count, 32 * count, 16 * count
        gu2[0:thin, 0:low] += dot(ib[group, 0:thin], dl[group, 0:low], NT)
        gu1[0:thin, 0:thin] += dot(jb[group, 0:thin], di[group, 0:thin], NT)
        gw2[0:wide, 0:thin] += dot(hb[group, 0:wide], df[group, 0:thin], NT)
        gw1[:, 0:wide] += dot(xs[group], dh[group, 0:wide], NT)

    @pl.when(step == pl.num_programs(0) - 1)
    def _():
        ones = jnp.ones((8, n), BF16)
        row_of = lambda ref: widen(dot_right(ones, ref[...], NT, 3)[0:1])
        g32[0:64, :] = blocks_sum(gw2, 64, 32, views)
        g32[65:97, :] = blocks_sum(gu1, 32, 32, views)
        g16[4:36, :] = blocks_sum(gu2, 32, 16, views)
        g32[64:65, :] = row_of(gb2)
        g32[129:130, :] = row_of(gc1)
        g16[36:37, :] = row_of(gc2)
        g16[309:310, :] = row_of(gd1)
        g16[310:311, :] = row_of(gs2)
        g16[311:312, :] = jnp.where(iota((1, 128), 1) == 0, row_of(gdd), 0.0)
        total = gw1[0:36, 0:128]
        total = total + roll(gw1[STRIP : STRIP + 36, 0:128], 64)
        total = total + gw1[2 * STRIP : 2 * STRIP + 36, 128:256]
        g64[0:36, :] = jnp.where(iota((36, 128), 1) < 64, total, 0.0)
        out_ref[...] = jnp.zeros_like(out_ref)
        out_ref[0:18, :] = sum(roll(g64[pl.ds(b, 18, stride=2), :], 64 * b) for b in range(2))
        out_ref[18:51, :] += sum(roll(g32[pl.ds(b, 33, stride=4), :], 32 * b) for b in range(4))
        out_ref[50:89, :] += sum(roll(g16[pl.ds(b, 39, stride=8), :], 16 * b) for b in range(8))
        sums_ref[...] = jnp.where(
            iota(sums_ref.shape, 1) == 0, loss_s[0:1, 0:1], loss_s[0:1, 1:2]
        )


def widen(value):
    rows, width = value.shape
    return jnp.concatenate([value, jnp.zeros((rows, 128 - width), F32)], axis=1)


def run_main(me, blocks, pieces, shard, deltas, targets, ray_weight):
    rows, points = blocks[0].shape[1:]
    views = rows // STRIP
    n = CHUNK
    steps = points // n
    shards = pieces.shape[0]
    sums = (shards, -(-(shard + 2) // 128) * 128)
    whole = deltas.shape[0] // 2
    pairs = deltas.reshape(whole, 1, n)
    target_pairs = jnp.pad(
        targets.reshape(whole, 2, 3).transpose(0, 2, 1), ((0, 0), (0, 5), (0, 126))
    )
    weight_pairs = jnp.pad(ray_weight.reshape(whole, 1, 2), ((0, 0), (0, 7), (0, 126)))
    vm = pltpu.VMEM
    own = lambda t, me: (me[0] * steps + t, 0, 0)
    block = pl.BlockSpec((1, rows, n), lambda t, me: (0, 0, t))
    piece = pl.BlockSpec(pieces.shape, lambda t, me: (0, 0, 0))
    return pl.pallas_call(
        lambda *refs: main_kernel(views, shard, *refs),
        out_shape=[
            jax.ShapeDtypeStruct((96, 128), F32),
            jax.ShapeDtypeStruct(sums, F32),
        ],
        grid_spec=pltpu.PrefetchScalarGridSpec(
            num_scalar_prefetch=1,
            grid=(steps,),
            in_specs=[piece]
            + [block] * 4
            + [
                pl.BlockSpec((1, 1, n), own),
                pl.BlockSpec((1, 8, 128), own),
                pl.BlockSpec((1, 8, 128), own),
            ],
            out_specs=[
                pl.BlockSpec((96, 128), lambda t, me: (0, 0)),
                pl.BlockSpec(sums, lambda t, me: (0, 0)),
            ],
            scratch_shapes=[
                vm((120, 128), F32),
                vm((40, 128), F32),
                vm((144, 128), F32),
                vm((320, 128), F32),
                vm((4, rows, n), BF16),
                vm((4, 64 * views, n), BF16),
                vm((4, 64 * views, n), F32),
                vm((4, 32 * views, n), F32),
                vm((4, 32 * views, n), F32),
                vm((4, 32 * views, n), BF16),
                vm((4, 32 * views, n), BF16),
                vm((4, 32 * views, n), F32),
                vm((4, 16 * views, n), F32),
                vm((4, 16 * views, n), BF16),
                vm((4, 32 * views, n), BF16),
                vm((4, 32 * views, n), BF16),
                vm((4, 64 * views, n), BF16),
                vm((64 * views, 128), BF16),
                vm((32 * views, 256), BF16),
                vm((64 * views, 128), BF16),
                vm((32 * views, 128), BF16),
                vm((32 * views, 128), BF16),
                vm((16 * views, 128), BF16),
                vm((32 * views, 128), BF16),
                vm((n, n), BF16),
                vm((40, 128), F32),
                vm((136, 128), F32),
                vm((312, 128), F32),
                vm((rows, 256), F32),
                vm((64 * views, 128), F32),
                vm((32 * views, 128), F32),
                vm((32 * views, 128), F32),
                vm((32, n), F32),
                vm((32, n), F32),
                vm((16, n), F32),
                vm((16, n), F32),
                vm((16, n), F32),
                vm((8, n), F32),
                vm((8, 128), F32),
            ],
        ),
        compiler_params=pltpu.CompilerParams(vmem_limit_bytes=48 * 1024 * 1024),
    )(me, pieces, *blocks, pairs, target_pairs, weight_pairs)


def adamw(master, first_moment, second_moment, gradient, step_count):
    step_float = step_count[0].astype(F32)
    first_new = MOMENT_DECAY * first_moment + (1.0 - MOMENT_DECAY) * gradient
    second_new = SQUARE_DECAY * second_moment + (1.0 - SQUARE_DECAY) * gradient * gradient
    first_fix = 1.0 - jnp.power(MOMENT_DECAY, step_float)
    second_fix = 1.0 - jnp.power(SQUARE_DECAY, step_float)
    update = first_new / first_fix / (jnp.sqrt(second_new / second_fix) + EPSILON)
    master_new = master - LEARNING_RATE * (update + WEIGHT_DECAY * master)
    return (master_new, first_new, second_new)


def body(
    master,
    first_moment,
    second_moment,
    step_count,
    feature_maps,
    pixel_index,
    visible,
    deltas,
    targets,
    scene_id,
    scene_weight,
):
    group = lax.axis_size("views")
    shards = lax.axis_size("rays")
    assert feature_maps.shape[2] <= SEEN_BIT
    shard = master.shape[0]
    spots = [lax.axis_index("views"), lax.axis_index("rays")]
    me = jnp.stack(spots).astype(jnp.int32)
    swap = lambda size, k: [(i, i ^ k) for i in range(size)]
    rows = -(-shard // 2048) * 16
    piece = jnp.pad(master.astype(BF16), (0, rows * 128 - shard)).reshape(rows, 128)
    packed = pixel_index.T + (visible.T << SEEN_SHIFT)
    held = piece[None]
    links = shards.bit_length() - 1
    for link in range(links):
        held = jnp.concatenate([held, lax.ppermute(held, "rays", swap(shards, shards >> (link + 1)))])
    far = gather_rows(packed, feature_maps, me, group, (3, 2))
    three = lax.ppermute(far[0], "views", swap(group, 3))
    two = lax.ppermute(far[1], "views", swap(group, 2))
    near = gather_rows(packed, feature_maps, me, group, (1,))
    one = lax.ppermute(near[0], "views", swap(group, 1))
    mine = gather_rows(packed, feature_maps, me, group, (0,))
    hits = (scene_id[:, None] == jnp.arange(scene_weight.shape[0])[None, :]).astype(F32)
    ray_weight = jnp.sum(hits * scene_weight.astype(F32)[None, :], axis=1)
    result, sums = run_main(me, [mine[0], one, two, three], held, shard, deltas, targets, ray_weight)
    summed = result[:89].reshape(-1)
    size = shards * shard
    if summed.shape[0] < size:
        summed = jnp.pad(summed, (0, size - summed.shape[0]))
    loss_at, far_at = shard, shard + 1
    send = jnp.concatenate([summed[:size].reshape(shards, shard), sums], axis=1)
    got = lax.all_to_all(send, "rays", 0, 0, tiled=True)
    partial = jnp.sum(got, axis=0)
    whole = partial
    for k in range(1, group):
        whole = whole + lax.ppermute(partial, "views", [(i, i ^ k) for i in range(group)])
    scaled = whole[: shard + 1] / whole[far_at : far_at + shard + 1]
    loss = scaled[loss_at]
    gradient = scaled[:shard]
    return (loss, *adamw(master, first_moment, second_moment, gradient, step_count))


def solution(mesh):
    placed = (
        P("rays"),
        P("rays"),
        P("rays"),
        P(),
        P("views", None, None),
        P("rays", "views"),
        P("rays", "views"),
        P("rays", None),
        P("rays", None),
        P("rays"),
        P(),
    )
    return jax.shard_map(
        body,
        mesh=mesh,
        in_specs=placed,
        out_specs=(P(), P("rays"), P("rays"), P("rays")),
        check_vma=False,
    )
```

```python
import jax
import jax.numpy as jnp
from jax import lax
from jax.experimental import pallas as pl
from jax.experimental.pallas import tpu as pltpu
from jax.sharding import PartitionSpec as P


F32 = jnp.float32
BF16 = jnp.bfloat16
SEEN_VIEWS = 10
CHANNELS = 35
STRIP = 40
BAND = 32
SEEN_SHIFT = 14
SEEN_BIT = 1 << SEEN_SHIFT
GATHER_TILE = 768
RAY = 192
CHUNK = 2 * RAY
PASSES = 1
TILE = 128
MOMENT_DECAY = 0.5
SQUARE_DECAY = 0.5
LEARNING_RATE = 0.05
WEIGHT_DECAY = 0.01
EPSILON = 1e-08
NN = (((1,), (0,)), ((), ()))
NT = (((1,), (1,)), ((), ()))
TN = (((0,), (0,)), ((), ()))


def dot(left, right, dims=NN):
    return lax.dot_general(left, right, dims, preferred_element_type=F32)


def parts(value, count):
    out = []
    for step in range(count):
        piece = value.astype(BF16)
        out.append(piece)
        if step + 1 < count:
            value = value - piece.astype(F32)
    return out


def dot_left(value, right, dims, count=PASSES):
    return sum(dot(piece, right, dims) for piece in parts(value, count))


def dot_right(left, value, dims, count=PASSES):
    return sum(dot(left, piece, dims) for piece in parts(value, count))


def elu_pair(value):
    slope = jnp.exp(jnp.minimum(value, 0.0))
    return jnp.maximum(value, 0.0) + (slope - 1.0), slope


def iota(shape, axis):
    return lax.broadcasted_iota(jnp.int32, shape, axis)


def table_rows(blocks):
    return BAND * blocks + 16 * (-(-blocks // 4))


def stack_maps(map_ref, stacked, view):
    channels, pixels = map_ref.shape[1:]
    blocks = pixels // 256
    blank = jnp.zeros((4, 256), F32)
    for block in range(blocks):
        lanes = slice(256 * block, 256 * (block + 1))
        stacked[view, BAND * block : BAND * (block + 1), :] = map_ref[view, 0:BAND, lanes]
    for first in range(0, blocks, 4):
        strips = []
        for block in range(first, first + 4):
            if block < blocks:
                lanes = slice(256 * block, 256 * (block + 1))
                strips.append(map_ref[view, BAND:channels, lanes].astype(F32))
                strips.append(blank[: BAND + 4 - channels])
            else:
                strips.append(blank)
        at = BAND * blocks + 4 * first
        stacked[view, at : at + 16, :] = jnp.concatenate(strips, axis=0).astype(BF16)


def gather_kernel(views, tile, count, *refs):
    packed_refs, source = refs[1 : 1 + count], refs[1 + count]
    outs, stacked = refs[2 + count : -1], refs[-1]
    blocks = source.shape[2] // 256

    @pl.when(pl.program_id(0) == 0)
    def _():
        for view in range(views):
            stack_maps(source, stacked, view)

    row = iota((8, tile), 0)
    upper = jnp.where(row < 4, 0, 1)
    for packed_ref, out_ref in zip(packed_refs, outs):
        strips = []
        for view in range(views):
            packed = packed_ref[view : view + 1, :]
            index = packed & (SEEN_BIT - 1)
            high = jnp.broadcast_to(index >> 8, (8, tile))
            low = jnp.broadcast_to(index & 255, (256, tile))
            picked = (iota((256, tile), 0) == low).astype(F32).astype(BF16)
            found = dot(stacked[view], picked)
            totals = [jnp.zeros((8, tile), F32)] * (BAND // 8)
            for block in range(blocks):
                here = high == block
                for part in range(BAND // 8):
                    at = BAND * block + 8 * part
                    totals[part] = jnp.where(here, found[at : at + 8], totals[part])
            last = jnp.zeros((8, tile), F32)
            half = high - upper
            for pair in range(-(-blocks // 2)):
                at = BAND * blocks + 8 * pair
                last = jnp.where(half == 2 * pair, found[at : at + 8], last)
            last = last + pltpu.roll(last, 4, 0)
            seen = jnp.broadcast_to((packed >> SEEN_SHIFT).astype(F32), (8, tile))
            last = jnp.where(row == CHANNELS - BAND, 1.0, last)
            last = jnp.where(row == CHANNELS - BAND + 1, seen, last)
            strips += totals + [jnp.where(row > CHANNELS - BAND + 1, 0.0, last)]
        out_ref[0] = jnp.concatenate(strips, axis=0).astype(BF16)


def gather_rows(packed, source, me, group, ways):
    views, points = packed.shape
    tile = GATHER_TILE
    own = points // group
    tiles = own // tile
    count = len(ways)
    part = lambda k: pl.BlockSpec((views, tile), lambda t, me: (0, (me[0] ^ k) * tiles + t))
    whole = lambda shape: pl.BlockSpec(shape, lambda t, me: (0, 0, 0))
    outs = [jax.ShapeDtypeStruct((1, views * STRIP, own), BF16)] * count
    out_specs = [pl.BlockSpec((1, views * STRIP, tile), lambda t, me: (0, 0, t))] * count
    table = (views, table_rows(source.shape[2] // 256), 256)
    flops = 2 * views * own * count * table[1] * 256
    return pl.pallas_call(
        lambda *refs: gather_kernel(views, tile, count, *refs),
        out_shape=outs,
        grid_spec=pltpu.PrefetchScalarGridSpec(
            num_scalar_prefetch=1,
            grid=(tiles,),
            in_specs=[part(k) for k in ways] + [whole(source.shape)],
            out_specs=out_specs,
            scratch_shapes=[pltpu.VMEM(table, BF16)],
        ),
        compiler_params=pltpu.CompilerParams(vmem_limit_bytes=32 * 1024 * 1024),
        cost_estimate=pl.CostEstimate(
            flops=flops, bytes_accessed=source.size * 2, transcendentals=0
        ),
    )(me, *([packed] * count), source)


def roll(value, shift):
    return pltpu.roll(value, shift % 128, 1)


def unpack(a_ref, r64, r32, r16):
    for b in range(2):
        r64[pl.ds(b, 18, stride=2), :] = roll(a_ref[0:18, :], -64 * b)
    for b in range(4):
        r32[pl.ds(b, 33, stride=4), :] = roll(a_ref[18:51, :], -32 * b)
    for b in range(8):
        r16[pl.ds(b, 39, stride=8), :] = roll(a_ref[50:89, :], -16 * b)


def assemble(place, shard, shard_refs, a_ref):
    a_ref[...] = jnp.zeros_like(a_ref)
    shards, rows, _ = shard_refs.shape
    for k in range(shards):
        owner = sum(((k >> bit) & 1) * (shards >> (bit + 1)) for bit in range(shards.bit_length()))
        start = (place ^ owner) * shard
        shift = start & 127
        value = pltpu.roll(shard_refs[k].astype(F32), shift, 1)
        keep = iota((rows, 128), 1) >= shift
        first = start >> 7
        a_ref[pl.ds(first, rows), :] += jnp.where(keep, value, 0.0)
        a_ref[pl.ds(first + 1, rows), :] += jnp.where(keep, 0.0, value)


def repeat(weight, out_ref, times):
    out_ref[...] = jnp.zeros_like(out_ref)
    rows, width = weight.shape
    wide = widen(weight)
    for part in range(times):
        tile, shift = divmod(width * part, 128)
        out_ref[rows * part : rows * (part + 1), 128 * tile : 128 * (tile + 1)] = roll(
            wide, shift
        ).astype(BF16)


def blocks_sum(ref, rows, width, times):
    total = sum(
        roll(ref[rows * part : rows * (part + 1), :], -width * part) for part in range(times)
    )
    return jnp.where(iota((rows, 128), 1) < width, total, 0.0)


def column(rows):
    return rows.T[:, 0:1]


def main_kernel(views, shard, me_ref, *refs):
    shard_refs, refs = refs[0], refs[1:]
    (
    x0,
    x1,
    x2,
    x3,
    delta_ref,
    target_ref,
    weight_ref,
    out_ref,
    sums_ref,
    a_ref,
    r64,
    r32,
    r16,
    xs,
    hb,
    he,
    ff,
    fe,
    jb,
    ib,
    ie,
    ee,
    dl,
    di,
    df,
    dh,
    blk,
    w2t_s,
    w2_s,
    u1t_s,
    u1_s,
    u2t_s,
    u2_s,
    tri_s,
    g64,
    g32,
    g16,
    gw1,
    gw2,
    gu1,
    gu2,
    gb2,
    gc1,
    gc2,
    gd1,
    gs2,
    gdd,
    loss_s,
    ) = refs
    step = pl.program_id(0)
    n = CHUNK
    lane = iota((1, n), 1)
    first_ray = lane < RAY
    me = me_ref[0]

    @pl.when(step == 0)
    def _():
        assemble(me_ref[1], shard, shard_refs, a_ref)
        unpack(a_ref, r64, r32, r16)
        for ref in (g64, g32, g16, gw1, gw2, gu1, gu2, gb2, gc1, gc2, gd1, gs2, gdd, loss_s):
            ref[...] = jnp.zeros_like(ref)
        before = (iota((n, n), 0) < iota((n, n), 1)) & (
            (iota((n, n), 0) < RAY) == (iota((n, n), 1) < RAY)
        )
        tri_s[...] = before.astype(F32).astype(BF16)
        w1t = jnp.where(iota((64, 128), 1) < 36, 1.0, 0.0) * jnp.concatenate(
            [r64[0:36, :], jnp.zeros((92, 128), F32)], axis=0
        ).T[:64]
        for view in range(views):
            blk[64 * view : 64 * (view + 1), :] = roll(w1t, STRIP * view).astype(BF16)
        w2 = r32[0:64, :][:, :32]
        u1a = r32[65:97, :][:, :32]
        u2 = r16[4:36, :][:, :16]
        repeat(w2.T, w2t_s, views)
        repeat(w2, w2_s, views)
        repeat(u1a.T, u1t_s, views)
        repeat(u1a, u1_s, views)
        repeat(u2.T, u2t_s, views)
        repeat(u2, u2_s, views)

    for k, ref in enumerate((x0, x1, x2, x3)):
        xs[me ^ k] = ref[0]

    b2 = column(r32[64:72, :])[:32]
    u1b = r32[97:129, :][:, :32]
    u1bt = u1b.T.astype(BF16)
    u1b = u1b.astype(BF16)
    c1 = column(r32[129:137, :])[:32]
    c2 = column(r16[36:44, :])[:16]
    keep16 = iota((48, 128), 1) < 16
    qkv = sum(
        roll(jnp.where(keep16, r16[pl.ds(37 + a, 48, stride=4), :], 0.0), 16 * a) for a in range(4)
    )
    wq, wk, wv = qkv[0:16], qkv[16:32], qkv[32:48]
    wqb = wq[:, :64].astype(BF16)
    wqt = wq[:, :64].T.astype(BF16)
    wk_of = [roll(wk, 64 * r).astype(BF16) for r in range(2)]
    wv_of = [roll(wv, 64 * r).astype(BF16) for r in range(2)]
    wo = r16[229:293, :][:, :16]
    wob = wo.astype(BF16)
    wot = wo.T.astype(BF16)
    s1 = r16[293:309, :][:, :16]
    s1b = s1.astype(BF16)
    s1t = s1.T.astype(BF16)
    d1 = column(r16[309:317, :])[:16]
    s2 = column(r16[310:318, :])[:16]
    d2 = r16[311:312, 0:1]

    def strip_of(group, local, lanes):
        at = STRIP * local + 32
        strip = xs[group, at : at + 8, lanes].astype(F32)
        return strip[0:3], strip[4:5]

    def stack(values):
        return jnp.concatenate(values, axis=0) if len(values) > 1 else values[0]

    def cut(value, rows, local):
        return value[rows * local : rows * (local + 1)]

    counts = [min(views, SEEN_VIEWS - at) for at in range(0, SEEN_VIEWS, views)]

    m = TILE
    lane_tiles = [slice(at, at + m) for at in range(0, n, m)]
    join = lambda values: jnp.concatenate(values, axis=1) if len(values) > 1 else values[0]

    def forward_tile(lanes):
        sum1 = jnp.zeros((32, m), F32)
        sum2 = jnp.zeros((32, m), F32)
        seen = jnp.zeros((1, m), F32)
        for group, count in enumerate(counts):
            wide, thin = 64 * count, 32 * count
            value, slope = elu_pair(dot(blk[0:wide, 0 : views * STRIP], xs[group, :, lanes]))
            hidden = value.astype(BF16)
            hb[group, 0:wide, lanes] = hidden
            he[group, 0:wide, lanes] = slope
            value, slope = elu_pair(dot(w2t_s[0:thin, 0:wide], hidden) + stack([b2] * count))
            ff[group, 0:thin, lanes] = value
            fe[group, 0:thin, lanes] = slope
            for local in range(count):
                vis = strip_of(group, local, lanes)[1]
                one = cut(value, 32, local)
                part = vis * one
                sum1 = sum1 + part
                sum2 = sum2 + part * one
                seen = seen + vis
        average = sum1 / seen
        variance = sum2 / seen - average * average
        variance_low = variance.astype(BF16)
        shared = dot(u1bt, variance_low) + c1
        num = jnp.zeros((16, m), F32)
        den = jnp.zeros((16, m), F32)
        col = jnp.zeros((3, m), F32)
        for group, count in enumerate(counts):
            thin, low = 32 * count, 16 * count
            feature = ff[group, 0:thin, lanes]
            joined = (feature - stack([average] * count)).astype(BF16)
            jb[group, 0:thin, lanes] = joined
            value, slope = elu_pair(dot(u1t_s[0:thin, 0:thin], joined) + stack([shared] * count))
            inner = value.astype(BF16)
            ib[group, 0:thin, lanes] = inner
            ie[group, 0:thin, lanes] = slope
            raw = jnp.exp(dot(u2t_s[0:low, 0:thin], inner) + stack([c2] * count))
            for local in range(count):
                rgb, vis = strip_of(group, local, lanes)
                e = vis * cut(raw, 16, local)
                ee[group, 16 * local : 16 * (local + 1), lanes] = e
                num = num + e * feature[32 * local : 32 * local + 16]
                den = den + e
                col = col + e[0:1] * rgb
        return average, 1.0 / seen, variance_low, num, den, col

    done = [forward_tile(lanes) for lanes in lane_tiles]
    average, inv_seen, variance_low, num, den, col = [join(list(x)) for x in zip(*done)]

    inv = 1.0 / den
    tokens = num / den
    colour = col / den[0:1]
    token_low = tokens.astype(BF16)
    token_t = tokens.T.astype(BF16)
    halves = [token_t[RAY * r : RAY * (r + 1)] for r in range(2)]
    query = dot(wqt, token_low).astype(BF16).astype(F32) * 0.25
    kk_f = dot(halves[0], wk_of[0]) + dot(halves[1], wk_of[1])
    vv_f = dot(halves[0], wv_of[0]) + dot(halves[1], wv_of[1])
    kk = kk_f.astype(BF16)
    vv = vv_f.astype(BF16)
    kkt = kk.astype(F32).T.astype(BF16)
    vvt = vv.astype(F32).T.astype(BF16)

    def spread(value, head):
        mine = value[16 * head : 16 * (head + 1)].astype(F32)
        one = jnp.where(first_ray, mine, 0.0)
        rows = []
        for part in (one, mine - one):
            rows += [jnp.zeros((16 * head, n), BF16)] if head else []
            rows.append(part.astype(BF16))
            rows += [jnp.zeros((48 - 16 * head, n), BF16)] if head < 3 else []
        return jnp.concatenate(rows, axis=0)

    def fold(value):
        return jnp.where(first_ray, value[:16], value[16:])

    def head_rows(value, head):
        at = 16 * head
        return jnp.concatenate([value[at : at + 16], value[64 + at : 80 + at]], axis=0)

    probs = []
    lows = []
    attended = []
    query_of = []
    for head in range(4):
        q_head = spread(query, head)
        query_of.append(q_head)
        tiles = []
        for at in range(0, n, 128):
            score = dot(kk, q_head[:, at : at + 128])
            score = jnp.exp(score - jnp.max(score, axis=0, keepdims=True))
            tiles.append(score * (1.0 / jnp.sum(score, axis=0, keepdims=True)))
        probs.append(tiles)
        low = jnp.concatenate([tile.astype(BF16) for tile in tiles], axis=1)
        lows.append(low)
        attended.append(fold(dot(head_rows(vvt, head), low)))
    raw_attended = attended
    attended = jnp.concatenate(attended, axis=0).astype(BF16)
    mixed = tokens + dot(wot, attended)
    mixed_low = mixed.astype(BF16)
    value, s_slope = elu_pair(dot(s1t, mixed_low) + d1)
    act = value.astype(BF16).astype(F32)
    z = jnp.sum(act * s2, axis=0, keepdims=True) + d2
    delta = delta_ref[0]
    ez = jnp.exp(-jnp.abs(z))
    density = jnp.maximum(z, 0.0) + jnp.log1p(ez)
    sigmoid = jnp.where(z >= 0.0, 1.0, ez) / (1.0 + ez)
    optical = density * delta
    tri = tri_s[...]

    def exact_rows(value):
        pad = jnp.zeros((13, n), F32)
        return jnp.concatenate([p.astype(F32) for p in parts(value, 3)] + [pad], axis=0).astype(BF16)

    before = jnp.sum(dot(exact_rows(optical), tri), axis=0, keepdims=True)
    through = jnp.exp(-before)
    gone = jnp.exp(-optical)
    render = through * (1.0 - gone)
    drawn = render * colour
    targets = target_ref[0]
    rweight = weight_ref[0]
    d_pixel = jnp.zeros((3, n), F32)
    loss = jnp.zeros((1, 1), F32)
    for r in range(2):
        mask = first_ray if r == 0 else jnp.logical_not(first_ray)
        pixel = jnp.sum(jnp.where(mask, drawn, 0.0), axis=1, keepdims=True)
        miss = pixel - targets[0:3, r : r + 1]
        scale = rweight[0:1, r : r + 1]
        loss = loss + scale * jnp.sum(miss * miss, axis=0, keepdims=True)
        d_pixel = d_pixel + jnp.where(mask, 2.0 * scale * miss, 0.0)
    place = iota((8, 128), 1) + 128 * iota((8, 128), 0)
    loss_s[...] += jnp.where(place == 0, loss, 0.0) + jnp.where(
        place == 1, rweight[0:1, 0:1] + rweight[0:1, 1:2], 0.0
    )

    d_render = jnp.sum(d_pixel * colour, axis=0, keepdims=True)
    d_colour = d_pixel * render
    d_before = -render * d_render
    d_optical = through * gone * d_render + jnp.sum(
        dot(exact_rows(d_before), tri, NT), axis=0, keepdims=True
    )
    dz = d_optical * delta * sigmoid
    gs2[...] += act * dz
    gdd[...] += jnp.where(iota((8, n), 0) == 0, dz, 0.0)
    d_pre = s2 * dz * s_slope
    gd1[...] += d_pre
    g16[293:309, :] += widen(dot_right(mixed_low, d_pre, NT))
    d_mixed = dot_right(s1b, d_pre, NN)
    g16[229:293, :] += widen(dot_right(attended, d_mixed, NT))
    d_att = dot_right(wob, d_mixed, NN)
    d_query = []
    d_kk = jnp.zeros((RAY, 128), F32)
    d_vv = jnp.zeros((RAY, 128), F32)
    for head in range(4):
        mine = d_att[16 * head : 16 * (head + 1)]
        shift = jnp.sum(mine * raw_attended[head], axis=0, keepdims=True)
        d_head = spread(d_att, head)
        d_vv = d_vv + dot(lows[head], d_head, NT)
        tiles = []
        for place, prob in enumerate(probs[head]):
            at = slice(128 * place, 128 * (place + 1))
            tiles.append((prob * (dot(vv, d_head[:, at]) - shift[:, at])).astype(BF16))
        d_score = jnp.concatenate(tiles, axis=1)
        d_query.append(fold(dot(head_rows(kkt, head), d_score)) * 0.25)
        d_kk = d_kk + dot(d_score, query_of[head], NT)
    d_query = jnp.concatenate(d_query, axis=0)
    gq = dot_right(token_low, d_query, NT)
    gk = [dot_right(halves[r], d_kk, TN) for r in range(2)]
    gv = [dot_right(halves[r], d_vv, TN) for r in range(2)]
    wide = jnp.concatenate([widen(gq), gk[0] + roll(gk[1], 64), gv[0] + roll(gv[1], 64)], axis=0)
    for a in range(4):
        at = pl.ds(37 + a, 48, stride=4)
        g16[at, :] += jnp.where(keep16, roll(wide, -16 * a), 0.0)
    d_halves = [
        dot_left(d_kk, wk_of[r], NT) + dot_left(d_vv, wv_of[r], NT) for r in range(2)
    ]
    d_tokens = d_mixed + dot_right(wqb, d_query, NN) + jnp.concatenate(d_halves, axis=0).T
    d_num = d_tokens * inv
    d_den = -d_num * tokens
    d_col = d_colour * inv[0:1]
    d_den0 = -jnp.sum(d_col * colour, axis=0, keepdims=True)
    row16 = iota((16, n), 0)
    d_den = d_den + jnp.where(row16 == 0, d_den0, 0.0)

    def backward_tile(lanes):
        own_num, own_den, own_col = d_num[:, lanes], d_den[:, lanes], d_col[:, lanes]
        d_average = jnp.zeros((32, m), F32)
        d_shared = jnp.zeros((32, m), F32)
        sum_c2 = jnp.zeros((16, m), F32)
        for group, count in enumerate(counts):
            thin, low = 32 * count, 16 * count
            d_logit = []
            for local in range(count):
                at = slice(16 * local, 16 * (local + 1))
                rgb, _ = strip_of(group, local, lanes)
                e = ee[group, at, lanes]
                d_e = own_num * ff[group, 32 * local : 32 * local + 16, lanes] + own_den
                shade = jnp.sum(own_col * rgb, axis=0, keepdims=True)
                d_e = d_e + jnp.where(row16[:, :m] == 0, shade, 0.0)
                d_logit.append(d_e * e)
                sum_c2 = sum_c2 + d_logit[-1]
                ee[group, at, lanes] = own_num * e
            piece = stack(d_logit).astype(BF16)
            dl[group, 0:low, lanes] = piece
            d_inner = dot(u2_s[0:thin, 0:low], piece) * ie[group, 0:thin, lanes]
            piece = d_inner.astype(BF16)
            di[group, 0:thin, lanes] = piece
            d_joined = dot(u1_s[0:thin, 0:thin], piece)
            ie[group, 0:thin, lanes] = d_joined
            for local in range(count):
                d_shared = d_shared + cut(d_inner, 32, local)
                d_average = d_average - cut(d_joined, 32, local)
        shared_low = d_shared.astype(BF16)
        d_variance = dot(u1b, shared_low)
        gc1[:, lanes] += d_shared
        gc2[:, lanes] += sum_c2
        d_square = d_variance * inv_seen[:, lanes]
        d_sum = (d_average - 2.0 * average[:, lanes] * d_variance) * inv_seen[:, lanes]
        sum_b2 = jnp.zeros((32, m), F32)
        for group, count in enumerate(counts):
            wide, thin = 64 * count, 32 * count
            d_feature = []
            for local in range(count):
                at = slice(32 * local, 32 * (local + 1))
                vis = strip_of(group, local, lanes)[1]
                feature = ff[group, at, lanes]
                d_one = ie[group, at, lanes] + vis * (d_sum + 2.0 * feature * d_square)
                kept = ee[group, 16 * local : 16 * (local + 1), lanes]
                d_one = jnp.concatenate([d_one[:16] + kept, d_one[16:]], axis=0)
                d_one = d_one * fe[group, at, lanes]
                sum_b2 = sum_b2 + d_one
                d_feature.append(d_one)
            piece = stack(d_feature).astype(BF16)
            df[group, 0:thin, lanes] = piece
            d_hidden = dot(w2_s[0:wide, 0:thin], piece) * he[group, 0:wide, lanes]
            dh[group, 0:wide, lanes] = d_hidden.astype(BF16)
        gb2[:, lanes] += sum_b2
        return shared_low

    shared_low = join([backward_tile(lanes) for lanes in lane_tiles])
    g32[97:129, :] += widen(dot(variance_low, shared_low, NT))
    for group, count in enumerate(counts):
        wide, thin, low = 64 * count, 32 * count, 16 * count
        gu2[0:thin, 0:low] += dot(ib[group, 0:thin], dl[group, 0:low], NT)
        gu1[0:thin, 0:thin] += dot(jb[group, 0:thin], di[group, 0:thin], NT)
        gw2[0:wide, 0:thin] += dot(hb[group, 0:wide], df[group, 0:thin], NT)
        gw1[:, 0:wide] += dot(xs[group], dh[group, 0:wide], NT)

    @pl.when(step == pl.num_programs(0) - 1)
    def _():
        ones = jnp.ones((8, n), BF16)
        row_of = lambda ref: widen(dot_right(ones, ref[...], NT, 3)[0:1])
        g32[0:64, :] = blocks_sum(gw2, 64, 32, views)
        g32[65:97, :] = blocks_sum(gu1, 32, 32, views)
        g16[4:36, :] = blocks_sum(gu2, 32, 16, views)
        g32[64:65, :] = row_of(gb2)
        g32[129:130, :] = row_of(gc1)
        g16[36:37, :] = row_of(gc2)
        g16[309:310, :] = row_of(gd1)
        g16[310:311, :] = row_of(gs2)
        g16[311:312, :] = jnp.where(iota((1, 128), 1) == 0, row_of(gdd), 0.0)
        total = gw1[0:36, 0:128]
        total = total + roll(gw1[STRIP : STRIP + 36, 0:128], 64)
        total = total + gw1[2 * STRIP : 2 * STRIP + 36, 128:256]
        g64[0:36, :] = jnp.where(iota((36, 128), 1) < 64, total, 0.0)
        out_ref[...] = jnp.zeros_like(out_ref)
        out_ref[0:18, :] = sum(roll(g64[pl.ds(b, 18, stride=2), :], 64 * b) for b in range(2))
        out_ref[18:51, :] += sum(roll(g32[pl.ds(b, 33, stride=4), :], 32 * b) for b in range(4))
        out_ref[50:89, :] += sum(roll(g16[pl.ds(b, 39, stride=8), :], 16 * b) for b in range(8))
        sums_ref[...] = jnp.where(
            iota(sums_ref.shape, 1) == 0, loss_s[0:1, 0:1], loss_s[0:1, 1:2]
        )


def widen(value):
    rows, width = value.shape
    return jnp.concatenate([value, jnp.zeros((rows, 128 - width), F32)], axis=1)


def run_main(me, blocks, pieces, shard, deltas, targets, ray_weight):
    rows, points = blocks[0].shape[1:]
    views = rows // STRIP
    n = CHUNK
    steps = points // n
    shards = pieces.shape[0]
    sums = (shards, -(-(shard + 2) // 128) * 128)
    whole = deltas.shape[0] // 2
    pairs = deltas.reshape(whole, 1, n)
    target_pairs = jnp.pad(
        targets.reshape(whole, 2, 3).transpose(0, 2, 1), ((0, 0), (0, 5), (0, 126))
    )
    weight_pairs = jnp.pad(ray_weight.reshape(whole, 1, 2), ((0, 0), (0, 7), (0, 126)))
    vm = pltpu.VMEM
    own = lambda t, me: (me[0] * steps + t, 0, 0)
    block = pl.BlockSpec((1, rows, n), lambda t, me: (0, 0, t))
    piece = pl.BlockSpec(pieces.shape, lambda t, me: (0, 0, 0))
    return pl.pallas_call(
        lambda *refs: main_kernel(views, shard, *refs),
        out_shape=[
            jax.ShapeDtypeStruct((96, 128), F32),
            jax.ShapeDtypeStruct(sums, F32),
        ],
        grid_spec=pltpu.PrefetchScalarGridSpec(
            num_scalar_prefetch=1,
            grid=(steps,),
            in_specs=[piece]
            + [block] * 4
            + [
                pl.BlockSpec((1, 1, n), own),
                pl.BlockSpec((1, 8, 128), own),
                pl.BlockSpec((1, 8, 128), own),
            ],
            out_specs=[
                pl.BlockSpec((96, 128), lambda t, me: (0, 0)),
                pl.BlockSpec(sums, lambda t, me: (0, 0)),
            ],
            scratch_shapes=[
                vm((120, 128), F32),
                vm((56, 128), F32),
                vm((168, 128), F32),
                vm((336, 128), F32),
                vm((4, rows, n), BF16),
                vm((4, 64 * views, n), BF16),
                vm((4, 64 * views, n), F32),
                vm((4, 32 * views, n), F32),
                vm((4, 32 * views, n), F32),
                vm((4, 32 * views, n), BF16),
                vm((4, 32 * views, n), BF16),
                vm((4, 32 * views, n), F32),
                vm((4, 16 * views, n), F32),
                vm((4, 16 * views, n), BF16),
                vm((4, 32 * views, n), BF16),
                vm((4, 32 * views, n), BF16),
                vm((4, 64 * views, n), BF16),
                vm((64 * views, 128), BF16),
                vm((32 * views, 256), BF16),
                vm((64 * views, 128), BF16),
                vm((32 * views, 128), BF16),
                vm((32 * views, 128), BF16),
                vm((16 * views, 128), BF16),
                vm((32 * views, 128), BF16),
                vm((n, n), BF16),
                vm((56, 128), F32),
                vm((168, 128), F32),
                vm((336, 128), F32),
                vm((rows, 256), F32),
                vm((64 * views, 128), F32),
                vm((32 * views, 128), F32),
                vm((32 * views, 128), F32),
                vm((32, n), F32),
                vm((32, n), F32),
                vm((16, n), F32),
                vm((16, n), F32),
                vm((16, n), F32),
                vm((8, n), F32),
                vm((8, 128), F32),
            ],
        ),
        compiler_params=pltpu.CompilerParams(vmem_limit_bytes=48 * 1024 * 1024),
    )(me, pieces, *blocks, pairs, target_pairs, weight_pairs)


def adamw(master, first_moment, second_moment, gradient, step_count):
    step_float = step_count[0].astype(F32)
    first_new = MOMENT_DECAY * first_moment + (1.0 - MOMENT_DECAY) * gradient
    second_new = SQUARE_DECAY * second_moment + (1.0 - SQUARE_DECAY) * gradient * gradient
    first_fix = 1.0 - jnp.power(MOMENT_DECAY, step_float)
    second_fix = 1.0 - jnp.power(SQUARE_DECAY, step_float)
    update = first_new / first_fix / (jnp.sqrt(second_new / second_fix) + EPSILON)
    master_new = master - LEARNING_RATE * (update + WEIGHT_DECAY * master)
    return (master_new, first_new, second_new)


def body(
    master,
    first_moment,
    second_moment,
    step_count,
    feature_maps,
    pixel_index,
    visible,
    deltas,
    targets,
    scene_id,
    scene_weight,
):
    group = lax.axis_size("views")
    shards = lax.axis_size("rays")
    assert feature_maps.shape[2] <= SEEN_BIT
    shard = master.shape[0]
    spots = [lax.axis_index("views"), lax.axis_index("rays")]
    me = jnp.stack(spots).astype(jnp.int32)
    swap = lambda size, k: [(i, i ^ k) for i in range(size)]
    rows = -(-shard // 2048) * 16
    piece = jnp.pad(master.astype(BF16), (0, rows * 128 - shard)).reshape(rows, 128)
    packed = pixel_index.T + (visible.T << SEEN_SHIFT)
    held = piece[None]
    links = shards.bit_length() - 1
    for link in range(links):
        held = jnp.concatenate([held, lax.ppermute(held, "rays", swap(shards, shards >> (link + 1)))])
    far = gather_rows(packed, feature_maps, me, group, (3, 2))
    three = lax.ppermute(far[0], "views", swap(group, 3))
    two = lax.ppermute(far[1], "views", swap(group, 2))
    near = gather_rows(packed, feature_maps, me, group, (1,))
    one = lax.ppermute(near[0], "views", swap(group, 1))
    mine = gather_rows(packed, feature_maps, me, group, (0,))
    hits = (scene_id[:, None] == jnp.arange(scene_weight.shape[0])[None, :]).astype(F32)
    ray_weight = jnp.sum(hits * scene_weight.astype(F32)[None, :], axis=1)
    result, sums = run_main(me, [mine[0], one, two, three], held, shard, deltas, targets, ray_weight)
    summed = result[:89].reshape(-1)
    size = shards * shard
    if summed.shape[0] < size:
        summed = jnp.pad(summed, (0, size - summed.shape[0]))
    loss_at, far_at = shard, shard + 1
    send = jnp.concatenate([summed[:size].reshape(shards, shard), sums], axis=1)
    got = lax.all_to_all(send, "rays", 0, 0, tiled=True)
    partial = jnp.sum(got, axis=0)
    whole = partial
    for k in range(1, group):
        whole = whole + lax.ppermute(partial, "views", [(i, i ^ k) for i in range(group)])
    scaled = whole[: shard + 1] / whole[far_at : far_at + shard + 1]
    loss = scaled[loss_at]
    gradient = scaled[:shard]
    return (loss, *adamw(master, first_moment, second_moment, gradient, step_count))


def solution(mesh):
    placed = (
        P("rays"),
        P("rays"),
        P("rays"),
        P(),
        P("views", None, None),
        P("rays", "views"),
        P("rays", "views"),
        P("rays", None),
        P("rays", None),
        P("rays"),
        P(),
    )
    return jax.shard_map(
        body,
        mesh=mesh,
        in_specs=placed,
        out_specs=(P(), P("rays"), P("rays"), P("rays")),
        check_vma=False,
    )
```
